128 devices in a mesh: dom: 32 (over y, x, core), sub: 4 (over z).
Axes of the slice: x: 4, y: 4, z: 4, core: 2. Of those that a mesh axis runs over, the one named last changes fastest.
Arguments:
- solution: float32 [8, 8, 8, 65536], P(None, None, None, ('dom', 'sub')), may hold values from -6 to 6
- forcing: float32 [8, 8, 8, 65536], P(None, None, None, ('dom', 'sub')), may hold values from -600 to 600
- metric: float32 [7, 8, 8, 8, 65536], P(None, None, None, None, ('dom', 'sub')), may hold values from -2.5 to 100, as said below
- entity_ids: int32 [26, 65536], P(None, ('dom', 'sub')), may hold values from 0 to 196607, as said below
- new_owner: int32 [65536], P(('dom', 'sub')), may hold values from 0 to 127, as said below
Outputs:
- smoothed: float32 [8, 8, 8, 65536], P(None, None, None, ('dom', 'sub'))
- moved_metric: float32 [7, 8, 8, 8, 65536], P(None, None, None, None, ('dom', 'sub'))
The draws below stay inside these ranges and needn't reach their ends.
Inputs may be any that keep to these rules, and one draw needn't show every extreme that they name: `new_owner`: an element stays on its device or goes to one of the device's four neighbours: the previous or next device along dom with the same sub index, or the previous or next along sub with the same dom index, indices wrapping around. Two neighbouring devices hand each other equally many elements, at most 64; in every draw some pair of neighbours along dom and some pair along sub hand each other exactly 64. `entity_ids`: face and edge ids come in blocks of 1536 consecutive ids, corner ids in blocks of 512; block b is summed by device b. Every face id is carried by exactly 2 element faces, every edge id by exactly 4 element edges, every corner id by exactly 8 element corners, their shared nodes lining up in the listed order. An id carried by a device's elements lies in the device's own block or in that of the next device along dom, along sub, or along both (indices wrapping around); every device's elements carry exactly 128 faces, 480 edges and 448 corners of the next block along dom, exactly 128 faces, 480 edges and 448 corners of the next block along sub, and exactly 32 edges, 64 corners and no face of the next block along both. metric[0], metric[1], metric[2] and metric[6] are positive; at every node |metric[3]| <= 0.5 sqrt(metric[0] metric[1]), |metric[4]| <= 0.5 sqrt(metric[0] metric[2]), |metric[5]| <= 0.5 sqrt(metric[1] metric[2]).
All inputs are finite; a program needn't handle non-finite values.
Results may differ from the reference program's by a relative error of at most 0.00005.
Values sent between devices are 32-bit elements; how exact they have to be, the bound alone decides.
A program may use at most 128 MiB of HBM per device.

```python
import math
import jax
import jax.numpy as jnp
import numpy as np
from jax import lax

NP = 8
EX = 4
EY = 4
EZ = 32
E_DEV = 512
MOVE = 64
ELEMS = 65536
N_DOM = 32
N_SUB = 4


def device_grid():
    dev_total = N_DOM * N_SUB
    devices = jnp.arange(dev_total, dtype=jnp.int32)
    return (devices, devices // N_SUB, devices % N_SUB)


def draw_new_owner(key, part):
    dev_total = N_DOM * N_SUB
    devices, dom_place, sub_place = device_grid()
    base_key = jax.random.fold_in(key, 7)
    dom_key, sub_key, pick_dom, pick_sub, order_key = jax.random.split(base_key, 5)
    lowest = (MOVE + 1) // 2
    dom_pairs = jax.random.randint(dom_key, (dev_total,), lowest, MOVE + 1).astype(jnp.int32)
    dom_pairs = dom_pairs.at[jax.random.randint(pick_dom, (), 0, dev_total)].set(MOVE)
    sub_pairs = jax.random.randint(sub_key, (dev_total,), lowest, MOVE + 1).astype(jnp.int32)
    sub_pairs = sub_pairs.at[jax.random.randint(pick_sub, (), 0, dev_total)].set(MOVE)
    prev_dom = (dom_place + N_DOM - 1) % N_DOM * N_SUB + sub_place
    next_dom = (dom_place + 1) % N_DOM * N_SUB + sub_place
    prev_sub = dom_place * N_SUB + (sub_place + N_SUB - 1) % N_SUB
    next_sub = dom_place * N_SUB + (sub_place + 1) % N_SUB
    counts = jnp.stack([dom_pairs[prev_dom], dom_pairs, sub_pairs[prev_sub], sub_pairs], axis=1)
    targets = jnp.stack([prev_dom, next_dom, prev_sub, next_sub], axis=1)
    bounds = jnp.cumsum(counts, axis=1).astype(jnp.int32)
    ranks = jnp.arange(E_DEV, dtype=jnp.int32)
    direction = jnp.sum((ranks[None, :, None] >= bounds[:, None, :]).astype(jnp.int32), axis=2)
    picked = jnp.take_along_axis(targets, jnp.clip(direction, 0, 3), axis=1)
    chosen_owner = jnp.where(direction < 4, picked, devices[:, None]).astype(jnp.int32)
    orders = jax.vmap(lambda sub_key_one: jax.random.permutation(sub_key_one, E_DEV).astype(jnp.int32))(jax.random.split(order_key, dev_total))
    owners = jnp.zeros((dev_total, E_DEV), jnp.int32).at[devices[:, None], orders].set(chosen_owner)
    return owners.reshape(-1)


def draw_entity_ids(key, part):
    dev_total = N_DOM * N_SUB
    devices, dom_place, sub_place = device_grid()
    base_key = jax.random.fold_in(key, 21)
    layout_key, face_key, edge_key, corner_key = jax.random.split(base_key, 4)

    def permutations(perm_key, length):
        return jax.vmap(lambda one_key: jax.random.permutation(one_key, length).astype(jnp.int32))(jax.random.split(perm_key, dev_total))
    layout = permutations(layout_key, E_DEV)
    slot_values = jnp.broadcast_to(jnp.arange(E_DEV, dtype=jnp.int32)[None, :], (dev_total, E_DEV))
    slot_of = jnp.zeros((dev_total, E_DEV), jnp.int32).at[devices[:, None], layout].set(slot_values)
    coord_x = dom_place[:, None] * EX + layout // (EY * EZ)
    coord_y = sub_place[:, None] * EY + layout // EZ % EY
    coord_z = layout % EZ
    face_perm = permutations(face_key, 3 * E_DEV)
    edge_perm = permutations(edge_key, 3 * E_DEV)
    corner_perm = permutations(corner_key, E_DEV)

    def owned(shift_x, shift_y, shift_z, axis_index, per_elem, perm_table):
        owner_x = (coord_x + shift_x) % (EX * N_DOM)
        owner_y = (coord_y + shift_y) % (EY * N_SUB)
        owner_z = (coord_z + shift_z) % EZ
        owner_dev = owner_x // EX * N_SUB + owner_y // EY
        owner_local = (owner_x % EX * EY + owner_y % EY) * EZ + owner_z
        owner_slot = slot_of[owner_dev, owner_local]
        owner_row = owner_slot * per_elem + axis_index
        return owner_dev * (per_elem * E_DEV) + perm_table[owner_dev, owner_row]
    rows_out = []
    for face_index in range(6):
        axis_index = face_index // 2
        offset = face_index % 2
        shifts = [0, 0, 0]
        shifts[axis_index] = offset
        rows_out.append(owned(shifts[0], shifts[1], shifts[2], axis_index, 3, face_perm))
    for edge_index in range(12):
        axis_index = edge_index // 4
        first_bit = edge_index % 4 // 2
        second_bit = edge_index % 2
        if axis_index == 0:
            shifts = (0, first_bit, second_bit)
        elif axis_index == 1:
            shifts = (first_bit, 0, second_bit)
        else:
            shifts = (first_bit, second_bit, 0)
        rows_out.append(owned(shifts[0], shifts[1], shifts[2], axis_index, 3, edge_perm))
    for corner_index in range(8):
        rows_out.append(owned(corner_index // 4, corner_index // 2 % 2, corner_index % 2, 0, 1, corner_perm))
    return jnp.stack(rows_out).reshape(26, dev_total * E_DEV).astype(jnp.int32)


def draw_metric(key, part):
    array_shape = (NP, NP, NP, ELEMS)
    subkeys = [jax.random.fold_in(key, 100 + layer_index) for layer_index in range(7)]
    factors = [jnp.exp(jax.random.uniform(subkeys[layer_index], array_shape, jnp.float32, math.log(0.2), math.log(5.0))) for layer_index in range(3)]
    mass_term = jnp.exp(jax.random.uniform(subkeys[6], array_shape, jnp.float32, math.log(5.0), math.log(100.0)))
    spreads = [jax.random.uniform(subkeys[3 + layer_index], array_shape, jnp.float32, -0.45, 0.45) for layer_index in range(3)]
    cross_rs = spreads[0] * jnp.sqrt(factors[0] * factors[1])
    cross_rt = spreads[1] * jnp.sqrt(factors[0] * factors[2])
    cross_st = spreads[2] * jnp.sqrt(factors[1] * factors[2])
    return jnp.stack([factors[0], factors[1], factors[2], cross_rs, cross_rt, cross_st, mass_term]).astype(jnp.float32)


def levels(key, dims, shards, smallest, high):
    def one(dim, blocks):
        heights = jax.random.uniform(jax.random.fold_in(jax.random.fold_in(key, 6), dim), (blocks,), jnp.float32, smallest / len(shards), high / len(shards))
        return jnp.repeat(jnp.exp(heights), dims[dim] // blocks).reshape((-1,) + (1,) * (len(dims) - dim - 1))

    gain = one(*shards[0])
    for cut in shards[1:]:
        gain = gain * one(*cut)
    return gain


def scatter_about(key, shape, scale, bound, cuts=(), held_as=jnp.bfloat16):
    drawn = jax.random.normal(key, shape, jnp.float32) * scale
    if len(cuts) > 0:
        drawn = levels(key, shape, cuts, -0.22, 0.18) * drawn
    return jnp.clip(drawn, min=-bound, max=bound).astype(held_as)


def setup_inputs(seed: int = 0) -> dict:
    splits = jax.random.split(jax.random.key(seed), 6)
    return {
        "solution": scatter_about(splits[0], (NP, NP, NP, ELEMS), 1.0, 6.0, ((3, 128),), jnp.float32),
        "forcing": scatter_about(splits[1], (NP, NP, NP, ELEMS), 100.0, 600.0, ((3, 128),), jnp.float32),
        "metric": draw_metric(jax.random.fold_in(splits[5], 71), 0),
        "entity_ids": draw_entity_ids(jax.random.fold_in(splits[5], 71), 0),
        "new_owner": draw_new_owner(jax.random.fold_in(splits[5], 71), 0),
    }


RELAX = 0.6


def derivative_table(order):
    count = order + 1
    points = -np.cos(np.pi * np.arange(count) / order)
    legendre = np.zeros((count, count))
    for sweep in range(80):
        legendre[:, 0] = 1.0
        legendre[:, 1] = points
        for degree in range(2, count):
            legendre[:, degree] = ((2 * degree - 1) * points * legendre[:, degree - 1] - (degree - 1) * legendre[:, degree - 2]) / degree
        points = points - (points * legendre[:, order] - legendre[:, order - 1]) / (count * legendre[:, order])
    legendre[:, 0] = 1.0
    legendre[:, 1] = points
    for degree in range(2, count):
        legendre[:, degree] = ((2 * degree - 1) * points * legendre[:, degree - 1] - (degree - 1) * legendre[:, degree - 2]) / degree
    values = legendre[:, order]
    identity = np.eye(count)
    spread = points[:, None] - points[None, :] + identity
    table = values[:, None] / values[None, :] / spread
    table = table * (1.0 - identity)
    table[0, 0] = -order * count / 4.0
    table[order, order] = order * count / 4.0
    return jnp.asarray(table, dtype=jnp.float32)


def element_apply(solution, metric, derivative):
    highest = lax.Precision.HIGHEST
    grad_r = jnp.einsum('ai,ijke->ajke', derivative, solution, precision=highest)
    grad_s = jnp.einsum('bj,ijke->ibke', derivative, solution, precision=highest)
    grad_t = jnp.einsum('ck,ijke->ijce', derivative, solution, precision=highest)
    flux_r = metric[0] * grad_r + metric[3] * grad_s + metric[4] * grad_t
    flux_s = metric[3] * grad_r + metric[1] * grad_s + metric[5] * grad_t
    flux_t = metric[4] * grad_r + metric[5] * grad_s + metric[2] * grad_t
    image = jnp.einsum('ai,ajke->ijke', derivative, flux_r, precision=highest)
    image = image + jnp.einsum('bj,ibke->ijke', derivative, flux_s, precision=highest)
    image = image + jnp.einsum('ck,ijce->ijke', derivative, flux_t, precision=highest)
    image = image + metric[6] * solution
    squared = derivative * derivative
    diagonal = jnp.einsum('ai,ajke->ijke', squared, metric[0], precision=highest)
    diagonal = diagonal + jnp.einsum('bj,ibke->ijke', squared, metric[1], precision=highest)
    diagonal = diagonal + jnp.einsum('ck,ijce->ijke', squared, metric[2], precision=highest)
    along = jnp.diagonal(derivative)
    along_i = along[:, None, None, None]
    along_j = along[None, :, None, None]
    along_k = along[None, None, :, None]
    diagonal = diagonal + 2.0 * along_i * along_j * metric[3] + 2.0 * along_i * along_k * metric[4] + 2.0 * along_j * along_k * metric[5]
    diagonal = diagonal + metric[6]
    return image, diagonal


def shared_slots(final_index):
    inside = slice(1, final_index)
    end_points = (0, final_index)
    face_slots = [(0, inside, inside), (final_index, inside, inside), (inside, 0, inside), (inside, final_index, inside), (inside, inside, 0), (inside, inside, final_index)]
    edge_slots = [(inside, first_end, second_end) for first_end in end_points for second_end in end_points]
    edge_slots = edge_slots + [(first_end, inside, second_end) for first_end in end_points for second_end in end_points]
    edge_slots = edge_slots + [(first_end, second_end, inside) for first_end in end_points for second_end in end_points]
    corner_slots = [(first_end, second_end, third_end) for first_end in end_points for second_end in end_points for third_end in end_points]
    return face_slots, edge_slots, corner_slots


def shared_parts(element_cube):
    face_slots, edge_slots, corner_slots = shared_slots(element_cube.shape[0] - 1)
    face_part = jnp.stack([element_cube[slot_index] for slot_index in face_slots])
    edge_part = jnp.stack([element_cube[slot_index] for slot_index in edge_slots])
    corners = jnp.stack([element_cube[slot_index] for slot_index in corner_slots])
    return face_part, edge_part, corners


def place_shared(element_cube, face_part, edge_part, corners):
    face_slots, edge_slots, corner_slots = shared_slots(element_cube.shape[0] - 1)
    for number, slot_index in enumerate(face_slots):
        element_cube = element_cube.at[slot_index].set(face_part[number])
    for number, slot_index in enumerate(edge_slots):
        element_cube = element_cube.at[slot_index].set(edge_part[number])
    for number, slot_index in enumerate(corner_slots):
        element_cube = element_cube.at[slot_index].set(corners[number])
    return element_cube


def assemble_kind(part, ids, segments):
    kind_count = part.shape[0]
    elem_total = part.shape[-1]
    by_element = jnp.moveaxis(part, -1, 1)
    inner_shape = by_element.shape[2:]
    flattened = by_element.reshape(kind_count * elem_total, -1)
    segment_ids = ids.reshape(-1).astype(jnp.int32)
    totals = jax.ops.segment_sum(flattened, segment_ids, num_segments=segments)
    returned = jnp.take(totals, segment_ids, axis=0).reshape((kind_count, elem_total) + inner_shape)
    return jnp.moveaxis(returned, 1, -1)


def new_positions(new_owner, dom_total, sub_total, per_dev):
    dev_total = dom_total * sub_total
    elem_total = dev_total * per_dev
    element = jnp.arange(elem_total, dtype=jnp.int32)
    home_device = (element // per_dev).astype(jnp.int32)
    dom_place = home_device // sub_total
    sub_place = home_device % sub_total
    neighbours = [((dom_place + dom_total - 1) % dom_total) * sub_total + sub_place, ((dom_place + 1) % dom_total) * sub_total + sub_place, dom_place * sub_total + (sub_place + sub_total - 1) % sub_total, dom_place * sub_total + (sub_place + 1) % sub_total]
    departed = new_owner != home_device
    out_dir = jnp.zeros((elem_total,), jnp.int32)
    rank_in = jnp.zeros((elem_total,), jnp.int32)
    for direction, neighbour in enumerate(neighbours):
        chosen = departed & (new_owner == neighbour)
        ranked = (jnp.cumsum(chosen.reshape(dev_total, per_dev).astype(jnp.int32), axis=1) - 1).astype(jnp.int32).reshape(-1)
        out_dir = jnp.where(chosen, jnp.int32(direction), out_dir).astype(jnp.int32)
        rank_in = jnp.where(chosen, ranked, rank_in).astype(jnp.int32)
    in_dir = (out_dir + 1 - 2 * (out_dir % 2)).astype(jnp.int32)
    arrivals = jnp.zeros((dev_total, 4), jnp.int32).at[new_owner, in_dir].add(departed.astype(jnp.int32))
    offsets = (jnp.cumsum(arrivals, axis=1) - arrivals).astype(jnp.int32)
    hole_index = (offsets[new_owner, in_dir] + rank_in).astype(jnp.int32)
    leaving = departed.reshape(dev_total, per_dev)
    hole_rank = (jnp.cumsum(leaving.astype(jnp.int32), axis=1) - 1).astype(jnp.int32)
    peers = jnp.arange(dev_total, dtype=jnp.int32)
    slot_values = jnp.broadcast_to(jnp.arange(per_dev, dtype=jnp.int32)[None, :], (dev_total, per_dev))
    hole_slot = jnp.zeros((dev_total, per_dev), jnp.int32).at[peers[:, None], jnp.where(leaving, hole_rank, per_dev)].set(slot_values, mode="drop")
    target = new_owner * per_dev + hole_slot[new_owner, jnp.clip(hole_index, 0, per_dev - 1)]
    return jnp.where(departed, target, element).astype(jnp.int32)


def reference(solution, forcing, metric, entity_ids, new_owner):
    elem_total = solution.shape[-1]
    derivative = derivative_table(NP - 1)
    image, diagonal = element_apply(solution, metric, derivative)
    both = jnp.stack([image, diagonal], axis=3)
    face_part, edge_part, corners = shared_parts(both)
    face_part = assemble_kind(face_part, entity_ids[0:6], 3 * elem_total)
    edge_part = assemble_kind(edge_part, entity_ids[6:18], 3 * elem_total)
    corners = assemble_kind(corners, entity_ids[18:26], elem_total)
    assembled = place_shared(both, face_part, edge_part, corners)
    relaxed = solution + RELAX * (forcing - assembled[:, :, :, 0]) / assembled[:, :, :, 1]
    position = new_positions(new_owner, N_DOM, N_SUB, E_DEV)
    smoothed = jnp.zeros_like(relaxed).at[..., position].set(relaxed)
    moved_metric = jnp.zeros_like(metric).at[..., position].set(metric)
    return smoothed, moved_metric
```

```python
import functools

import jax
import jax.numpy as jnp
import numpy as np
from jax import lax
from jax.experimental import pallas as pl
from jax.experimental.pallas import tpu as pltpu
from jax.sharding import PartitionSpec as P

N = 8
E = 512
NODES = N * N * N
EX = 4
EY = 4
EZ = 32
MOVE = 64
RELAX = 0.6
F_BLOCK, E_BLOCK, C_BLOCK = 3 * E, 3 * E, E
F_KEYS, E_KEYS, C_KEYS = 1792, 2560, 1536
E_HI, C_HI = E_KEYS // 256, C_KEYS // 256
MSG = 224
BOTH = 24
INTERPRET = False

f32, bf16, i32 = jnp.float32, jnp.bfloat16, jnp.int32


def derivative_table(order):
    count = order + 1
    points = -np.cos(np.pi * np.arange(count) / order)
    legendre = np.zeros((count, count))
    for sweep in range(80):
        legendre[:, 0] = 1.0
        legendre[:, 1] = points
        for degree in range(2, count):
            legendre[:, degree] = (
                (2 * degree - 1) * points * legendre[:, degree - 1]
                - (degree - 1) * legendre[:, degree - 2]
            ) / degree
        points = points - (points * legendre[:, order] - legendre[:, order - 1]) / (
            count * legendre[:, order]
        )
    legendre[:, 0] = 1.0
    legendre[:, 1] = points
    for degree in range(2, count):
        legendre[:, degree] = (
            (2 * degree - 1) * points * legendre[:, degree - 1]
            - (degree - 1) * legendre[:, degree - 2]
        ) / degree
    values = legendre[:, order]
    identity = np.eye(count)
    spread = points[:, None] - points[None, :] + identity
    table = values[:, None] / values[None, :] / spread
    table = table * (1.0 - identity)
    table[0, 0] = -order * count / 4.0
    table[order, order] = order * count / 4.0
    return table.astype(np.float32)


TABLE = derivative_table(N - 1)
SQUARED = TABLE * TABLE
ALONG = [float(v) for v in np.diagonal(TABLE)]


def row_of(i, j, k):
    return (i * N + j) * N + k


EDGE_ROWS = (
    [(row_of(0, a, b), N * N) for a in (0, 7) for b in (0, 7)]
    + [(row_of(a, 0, b), N) for a in (0, 7) for b in (0, 7)]
    + [(row_of(a, b, 0), 1) for a in (0, 7) for b in (0, 7)]
)
CORNER_ROWS = [row_of(a, b, c) for a in (0, 7) for b in (0, 7) for c in (0, 7)]


def split3(x):
    hi = x.astype(bf16)
    rest = x - hi.astype(f32)
    mid = rest.astype(bf16)
    low = (rest - mid.astype(f32)).astype(bf16)
    return hi, mid, low


def stack3(x):
    return jnp.concatenate(split3(x), axis=0)


def sum3(x):
    m = x.shape[0] // 3
    return x[0:m] + x[m : 2 * m] + x[2 * m : 3 * m]


def dot_nn(a, b):
    return lax.dot_general(a, b, (((1,), (0,)), ((), ())), preferred_element_type=f32)


def dot_nt(a, b):
    return lax.dot_general(a, b, (((1,), (1,)), ((), ())), preferred_element_type=f32)


def small_row(key, count):
    ok = (key >= 0) & (key < count)
    return jnp.where(ok, key, -1).astype(f32).astype(bf16)


def iota_rows(count, lanes):
    return lax.broadcasted_iota(i32, (count, lanes), 0).astype(f32).astype(bf16)


def onehot(row, count):
    lanes = row.shape[1]
    io = iota_rows(count, 128)
    one, zero = jnp.ones((count, 128), bf16), jnp.zeros((count, 128), bf16)
    cols = [
        jnp.where(io == jnp.broadcast_to(row[:, g : g + 128], (count, 128)), one, zero)
        for g in range(0, lanes, 128)
    ]
    return cols[0] if len(cols) == 1 else jnp.concatenate(cols, axis=1)


def prefix_matrix():
    a = lax.broadcasted_iota(i32, (E, E), 0)
    b = lax.broadcasted_iota(i32, (E, E), 1)
    return jnp.where(a <= b, 1.0, 0.0).astype(bf16)


def ranks(mask, tri):
    m = mask.shape[0]
    flags = jnp.where(mask, 1.0, 0.0)
    within = dot_nn(flags.astype(bf16), tri) - 1.0
    if m > 1:
        before = jnp.zeros((1, 1), f32)
        offs = [before]
        for r in range(m - 1):
            before = before + jnp.sum(flags[r : r + 1], axis=1, keepdims=True)
            offs.append(before)
        within = within + jnp.concatenate(offs, axis=0)
    return within.astype(i32)


def move_rows(owner, devs, tri):
    own = devs[0]
    departed = owner != own
    leave = jnp.full((1, E), -1, i32)
    arrive = jnp.full((1, E), -1, i32)
    flags = [departed] + [departed & (owner == devs[d]) for d in range(1, 5)]
    stacked = jnp.concatenate([jnp.where(f, 1.0, 0.0) for f in flags] + [jnp.zeros((3, E), f32)], axis=0)
    pre = dot_nn(stacked.astype(bf16), tri)
    hole = pre[0:1] - 1.0
    start = jnp.zeros((1, 1), f32)
    for d in range(4):
        chosen = flags[d + 1]
        rank = pre[d + 1 : d + 2] - 1.0
        leave = jnp.where(chosen, d * MOVE + rank.astype(i32), leave)
        count = pre[d + 1 : d + 2, E - 1 : E]
        pos = hole - start
        inside = departed & (pos >= 0.0) & (pos < count)
        arrive = jnp.where(inside, d * MOVE + pos.astype(i32), arrive)
        start = start + count
    return departed, leave, arrive


def swapped(col):
    return jnp.where(col >= 0, col ^ MOVE, -1)


def lane_low(rows):
    return lax.broadcasted_iota(i32, (rows, 128), 1) < MOVE


def pack_block(x, pa, pb):
    half = NODES // 2
    ya = sum3(dot_nt(stack3(x[0:half]), pa))
    yb = sum3(dot_nt(stack3(x[half:]), pb))
    low = lane_low(half)
    out = []
    for g in (0, 128):
        a, b = ya[:, g : g + 128], yb[:, g : g + 128]
        out.append(jnp.where(low, a, b))
        out.append(jnp.where(low, b, a))
    return out


def land_block(x, got, pa, pb, departed):
    half = NODES // 2
    low = lane_low(half)
    zl, zh = [], []
    for g in (0, 2):
        zl.append(jnp.where(low, got[g + 1], got[g]))
        zh.append(jnp.where(low, got[g], got[g + 1]))
    zl = jnp.concatenate(zl, axis=1)
    zh = jnp.concatenate(zh, axis=1)
    yl = sum3(dot_nn(stack3(zl), pb))
    yh = sum3(dot_nn(stack3(zh), pa))
    keep = jnp.logical_not(departed)
    return jnp.where(keep, x[0:half], yl), jnp.where(keep, x[half:], yh)


def pack_kernel(devs, owner_ref, met_ref, o0, o1, o2, o3, pa, pb):
    @pl.when(pl.program_id(0) == 0)
    def _():
        _, leave, _ = move_rows(owner_ref[...], [devs[d] for d in range(5)], prefix_matrix())
        pa[...] = onehot(small_row(leave, 256), 256)
        pb[...] = onehot(small_row(swapped(leave), 256), 256)

    out = pack_block(met_ref[0].reshape(NODES, E), pa[...], pb[...])
    for ref, val in zip((o0, o1, o2, o3), out):
        ref[...] = val


def pack_metric(devs, owner, metric):
    half = NODES // 2
    return pl.pallas_call(
        pack_kernel,
        grid=(7,),
        in_specs=[
            pl.BlockSpec(memory_space=pltpu.SMEM),
            pl.BlockSpec((1, E), lambda m: (0, 0)),
            pl.BlockSpec((1, N, N, N, E), lambda m: (m, 0, 0, 0, 0)),
        ],
        out_specs=[pl.BlockSpec((half, 128), lambda m: (m, 0))] * 4,
        out_shape=[jax.ShapeDtypeStruct((7 * half, 128), f32)] * 4,
        scratch_shapes=[pltpu.VMEM((256, E), bf16)] * 2,
        interpret=INTERPRET,
        name="pack",
    )(devs, owner, metric)


def contract_i(src, table, put):
    for j in range(N):
        xs = [src(i, j) for i in range(N)]
        for a in range(N):
            put(a, j, sum(float(table[a, i]) * xs[i] for i in range(N) if table[a, i] != 0.0))


def contract_j(src, table, put):
    for i in range(N):
        xs = [src(i, j) for j in range(N)]
        for b in range(N):
            put(i, b, sum(float(table[b, j]) * xs[j] for j in range(N) if table[b, j] != 0.0))


def key_rows(ids, block, devs, dom_base, both_base, sub_base, tri):
    rel, inside = [], []
    for d in (0, 2, 4, 5):
        r = ids - devs[d] * block
        rel.append(r)
        inside.append((r >= 0) & (r < block))
    key = jnp.where(inside[0], rel[0], -1)
    key = jnp.where(inside[1], dom_base + ranks(inside[1], tri), key)
    key = jnp.where(inside[2], sub_base + ranks(inside[2], tri), key)
    if both_base is not None:
        key = jnp.where(inside[3], both_base + ranks(inside[3], tri), key)
    row = jnp.where(inside[0], rel[0], jnp.where(inside[1], rel[1], jnp.where(inside[2], rel[2], rel[3])))
    return key, row.astype(f32)


def tile(ref, r):
    return ref[pl.ds(r * N, N), :]


def apply_kernel(
    devs, ids, sol, met, kmat, im_out, dg_out, key_out, tf, te, tc, md, ms,
    vf, ve, vc, rix, ga, gb, gc, of, le, ol, acc_e,
):
    c = pl.program_id(0)

    @pl.when(c == 0)
    def _():
        tri = prefix_matrix()
        dv = [devs[d] for d in range(6)]
        k, r = key_rows(ids[0:6], F_BLOCK, dv, 1536, None, 1664, tri)
        key_out[0:6, :] = k
        rix[0:6, :] = r
        k, r = key_rows(ids[6:18], E_BLOCK, dv, 1536, 2016, 2048, tri)
        key_out[6:18, :] = k
        rix[6:18, :] = r
        k, r = key_rows(ids[18:26], C_BLOCK, dv, 512, 960, 1024, tri)
        key_out[18:26, :] = k
        rix[18:26, :] = r

    im, dg = im_out.at[0], dg_out.at[0]
    fwd, bwd = kmat.at[0], kmat.at[1]
    half = NODES // 2

    def kdot(m, x):
        return lax.dot_general(
            m, x, (((1,), (0,)), ((), ())),
            precision=lax.Precision.HIGHEST, preferred_element_type=f32,
        )

    def put_a(i, j, v):
        ga[pl.ds((i * N + j) * N, N), :] = v

    def put_b(i, j, v):
        gb[pl.ds((i * N + j) * N, N), :] = v

    contract_i(lambda i, j: sol[i, j], TABLE, put_a)
    contract_j(lambda i, j: sol[i, j], TABLE, put_b)
    for h in range(2):
        x = sol[h * 4 : h * 4 + 4].reshape(half, 128)
        gc[h * half : (h + 1) * half, :] = kdot(fwd[...], x)

    for i in range(N):
        for j in range(N):
            r = i * N + j
            a, b, t = tile(ga, r), tile(gb, r), tile(gc, r)
            m3, m4, m5 = met[3, i, j], met[4, i, j], met[5, i, j]
            ga[pl.ds(r * N, N), :] = met[0, i, j] * a + m3 * b + m4 * t
            gb[pl.ds(r * N, N), :] = m3 * a + met[1, i, j] * b + m5 * t
            gc[pl.ds(r * N, N), :] = m4 * a + m5 * b + met[2, i, j] * t

    for h in range(2):
        im[h * half : (h + 1) * half, :] = kdot(bwd[...], gc[h * half : (h + 1) * half, :])

    def add_im(i, j, v):
        im[pl.ds((i * N + j) * N, N), :] += v

    contract_i(lambda i, j: tile(ga, i * N + j), TABLE.T, add_im)

    def add_im_last(i, j, v):
        im[pl.ds((i * N + j) * N, N), :] += v + met[6, i, j] * sol[i, j]

    contract_j(lambda i, j: tile(gb, i * N + j), TABLE.T, add_im_last)

    sq = kmat.at[2]
    for h in range(2):
        x = met[2, h * 4 : h * 4 + 4].reshape(half, 128)
        dg[h * half : (h + 1) * half, :] = kdot(sq[...], x)

    def add_dg(i, j, v):
        dg[pl.ds((i * N + j) * N, N), :] += v

    contract_i(lambda i, j: met[0, i, j], SQUARED.T, add_dg)
    kk = lax.broadcasted_iota(i32, (N, 128), 0)
    dk = jnp.where(kk == 0, ALONG[0], jnp.where(kk == N - 1, ALONG[N - 1], 0.0))

    def add_dg_last(i, j, v):
        v = v + met[6, i, j]
        if ALONG[i] * ALONG[j] != 0.0:
            v = v + (2.0 * ALONG[i] * ALONG[j]) * met[3, i, j]
        if ALONG[i] != 0.0:
            v = v + (2.0 * ALONG[i]) * dk * met[4, i, j]
        if ALONG[j] != 0.0:
            v = v + (2.0 * ALONG[j]) * dk * met[5, i, j]
        dg[pl.ds((i * N + j) * N, N), :] += v

    contract_j(lambda i, j: met[1, i, j], SQUARED.T, add_dg_last)

    lanes = pl.ds(pl.multiple_of(c * 128, 128), 128)

    def face(ref, f):
        if f < 2:
            base = 0 if f == 0 else 448
            return ref[base : base + 64, :]
        if f < 4:
            j = 0 if f == 2 else 7
            return jnp.concatenate([ref[pl.ds((i * N + j) * N, N), :] for i in range(N)], axis=0)
        return ref[pl.ds(0 if f == 4 else 7, 64, stride=N), :]

    top = lax.broadcasted_iota(i32, (N, 128), 0) == 0
    for f in range(6):
        at = pl.ds(pl.multiple_of(f * E + c * 128, 128), 128)
        a, b = face(im, f), face(dg, f)
        mark = jnp.broadcast_to(rix[f : f + 1, lanes], (N, 128))
        a = jnp.concatenate([jnp.where(top, mark, a[0:N]), a[N:]], axis=0)
        for s, (p, q) in enumerate(zip(split3(a), split3(b))):
            vf[s * 128 : s * 128 + 64, at] = p
            vf[s * 128 + 64 : s * 128 + 128, at] = q
    for e in range(12):
        at = pl.ds(pl.multiple_of(e * E + c * 128, 128), 128)
        start, stride = EDGE_ROWS[e]
        rows = pl.ds(start, N) if stride == 1 else pl.ds(start, N, stride=stride)
        a, b = im[rows, :], dg[rows, :]
        mark = jnp.broadcast_to(rix[6 + e : 7 + e, lanes], (N, 128))
        x = jnp.concatenate([jnp.where(top, mark, a), b], axis=0)
        for s, p in enumerate(split3(x)):
            ve[s * 16 : s * 16 + 16, at] = p
    for q in range(8):
        at = pl.ds(pl.multiple_of(q * E + c * 128, 128), 128)
        r = CORNER_ROWS[q]
        vc[0:1, at] = im[r : r + 1, :]
        vc[1:2, at] = dg[r : r + 1, :]
        vc[2:3, at] = rix[18 + q : 19 + q, lanes]
        vc[3:8, at] = jnp.zeros((5, 128), f32)

    @pl.when(c == 3)
    def _():
        def face_block(n, carry):
            for f in range(6):
                of[:, f * E : (f + 1) * E] = onehot(small_row(key_out[f : f + 1, :] - n * 256, 256), 256)
            acc = dot_nt(vf[...], of[...])
            tf[:, pl.ds(pl.multiple_of(n * 256, 256), 256)] = sum3(acc)
            return carry

        lax.fori_loop(0, F_KEYS // 256, face_block, 0)

        for e in range(12):
            at = slice(e * E, (e + 1) * E)
            key = key_out[6 + e : 7 + e, :]
            hi = small_row(key >> 8, E_HI)
            ol[:, at] = onehot(small_row(key & 255, 256), 256)
            for g in range(4):
                ag = slice(e * E + g * 128, e * E + (g + 1) * 128)
                hb = jnp.broadcast_to(hi[:, g * 128 : (g + 1) * 128], (16, 128))
                zero = jnp.zeros((16, 128), bf16)
                parts = [ve[s * 16 : s * 16 + 16, ag] for s in range(3)]
                for h in range(E_HI):
                    m = hb == jnp.full((16, 128), float(h), bf16)
                    for s in range(3):
                        le[(s * E_HI + h) * 16 : (s * E_HI + h + 1) * 16, ag] = jnp.where(m, parts[s], zero)
        acc_e[...] = dot_nt(le[...], ol[...])
        for h in range(E_HI):
            te[h] = sum(acc_e[(s * E_HI + h) * 16 : (s * E_HI + h + 1) * 16, :] for s in range(3))

        full = E * 8
        for q in range(8):
            at = slice(q * E, (q + 1) * E)
            ol[:, at] = onehot(small_row(key_out[18 + q : 19 + q, :] & 255, 256), 256)
        hi = jnp.concatenate([key_out[18 + q : 19 + q, :] >> 8 for q in range(8)], axis=1)
        x = vc[...]
        big = jnp.concatenate(
            [jnp.where(jnp.broadcast_to(hi, (8, full)) == h, x, 0.0) for h in range(C_HI)], axis=0
        )
        acc = sum3(dot_nt(stack3(big), ol[:, 0:full]))
        for h in range(C_HI):
            tc[h] = acc[h * 8 : (h + 1) * 8]

        md[0:128, :] = tf[:, 1536:1664]
        ms[0:128, :] = tf[:, 1664:1792]
        for g in range(4):
            er, cr = msg_rows(g)
            half_lanes = slice((g % 2) * 128, (g % 2) * 128 + 128)
            md[er : er + 16, :] = te[6 + g // 2, :, half_lanes]
            ms[er : er + 16, :] = te[8 + g // 2, :, half_lanes]
            md[cr : cr + 8, :] = tc[2 + g // 2, :, half_lanes]
            ms[cr : cr + 8, :] = tc[4 + g // 2, :, half_lanes]


def msg_rows(g):
    if g < 3:
        return 128 + 16 * g, 176 + 8 * g
    return 200, 216


def apply_scatter(devs, ids, solution, metric):
    eye = np.eye(NODES // 2 // N, dtype=np.float32)
    kmat = np.stack([np.kron(eye, TABLE), np.kron(eye, TABLE.T), np.kron(eye, SQUARED.T)])
    chunk = lambda c: (c, 0, 0)
    whole2 = lambda c: (0, 0)
    whole3 = lambda c: (0, 0, 0)
    return pl.pallas_call(
        apply_kernel,
        grid=(4,),
        in_specs=[
            pl.BlockSpec(memory_space=pltpu.SMEM),
            pl.BlockSpec((26, E), whole2),
            pl.BlockSpec((N, N, N, 128), lambda c: (0, 0, 0, c)),
            pl.BlockSpec((7, N, N, N, 128), lambda c: (0, 0, 0, 0, c)),
            pl.BlockSpec((3, 256, 256), whole3),
        ],
        out_specs=[
            pl.BlockSpec((1, NODES, 128), chunk),
            pl.BlockSpec((1, NODES, 128), chunk),
            pl.BlockSpec((26, E), whole2),
            pl.BlockSpec((128, F_KEYS), whole2),
            pl.BlockSpec((E_HI, 16, 256), whole3),
            pl.BlockSpec((C_HI, 8, 256), whole3),
            pl.BlockSpec((MSG, 128), whole2),
            pl.BlockSpec((MSG, 128), whole2),
        ],
        out_shape=[
            jax.ShapeDtypeStruct((4, NODES, 128), f32),
            jax.ShapeDtypeStruct((4, NODES, 128), f32),
            jax.ShapeDtypeStruct((26, E), i32),
            jax.ShapeDtypeStruct((128, F_KEYS), f32),
            jax.ShapeDtypeStruct((E_HI, 16, 256), f32),
            jax.ShapeDtypeStruct((C_HI, 8, 256), f32),
            jax.ShapeDtypeStruct((MSG, 128), f32),
            jax.ShapeDtypeStruct((MSG, 128), f32),
        ],
        scratch_shapes=[
            pltpu.VMEM((384, 6 * E), bf16),
            pltpu.VMEM((48, 12 * E), bf16),
            pltpu.VMEM((8, 8 * E), f32),
            pltpu.VMEM((26, E), f32),
            pltpu.VMEM((NODES, 128), f32),
            pltpu.VMEM((NODES, 128), f32),
            pltpu.VMEM((NODES, 128), f32),
            pltpu.VMEM((256, 6 * E), bf16),
            pltpu.VMEM((3 * E_HI * 16, 12 * E), bf16),
            pltpu.VMEM((256, 12 * E), bf16),
            pltpu.VMEM((3 * E_HI * 16, 256), f32),
        ],
        compiler_params=pltpu.CompilerParams(vmem_limit_bytes=56 << 20),
        interpret=INTERPRET,
        name="apply",
    )(devs, ids, solution, metric, kmat)


def owner_kernel(tf, te, tc, gd, gs, gboth, tf2, te2, tc2, rd, rs, rb):
    vals = jnp.concatenate([gd[0:128, :], gs[0:128, :]], axis=1)
    key = vals[0:1, :].astype(i32)
    vs = stack3(vals)
    ret = jnp.zeros((384, 256), f32)
    for n in range(F_BLOCK // 256):
        o = onehot(small_row(key - n * 256, 256), 256)
        total = tf[:, n * 256 : (n + 1) * 256] + sum3(dot_nt(vs, o))
        tf2[:, n * 256 : (n + 1) * 256] = total
        ret = ret + dot_nn(stack3(total), o)
    ret = sum3(ret)
    rd[0:128, :] = ret[:, 0:128]
    rs[0:128, :] = ret[:, 128:256]

    lane = lax.broadcasted_iota(i32, (1, 128), 1)

    def lines(rows, id_row, total_ref, total_out, his, cut, at):
        vals, keys = [], []
        for src in (gd, gs):
            for g in range(4):
                r = msg_rows(g)[at]
                v = src[r : r + rows, :]
                k = v[id_row : id_row + 1].astype(i32)
                if src is gd and g == 3:
                    k = jnp.where(lane >= cut, -1, k)
                vals.append(v)
                keys.append(k)
        r = msg_rows(3)[at] - (MSG - BOTH)
        v = gboth[r : r + rows, :]
        keys.append(jnp.where(lane < cut, -1, v[id_row : id_row + 1].astype(i32)))
        vals.append(v)
        x = jnp.concatenate(vals, axis=1)
        key = jnp.concatenate(keys, axis=1)
        hi = key >> 8
        o = onehot(small_row(key & 255, 256), 256)
        big = jnp.concatenate([jnp.where(jnp.broadcast_to(hi, x.shape) == h, x, 0.0) for h in range(his)], axis=0)
        acc = sum3(dot_nt(stack3(big), o))
        totals = jnp.concatenate([total_ref[h] for h in range(his)], axis=0) + acc
        for h in range(his):
            total_out[h] = totals[h * rows : (h + 1) * rows]
        y = sum3(dot_nn(stack3(totals), o))
        back = jnp.zeros_like(x)
        for h in range(his):
            back = jnp.where(jnp.broadcast_to(hi, x.shape) == h, y[h * rows : (h + 1) * rows], back)
        for n, dst in enumerate((rd, rs)):
            for g in range(4):
                p = msg_rows(g)[at]
                dst[p : p + rows, :] = back[:, (n * 4 + g) * 128 : (n * 4 + g + 1) * 128]
        rb[r : r + rows, :] = back[:, 1024:1152]

    lines(16, 0, te, te2, E_BLOCK // 256, 96, 0)
    lines(8, 2, tc, tc2, C_BLOCK // 256, 64, 1)


def owner_sums(tf, te, tc, got_dom, got_sub, got_both):
    return pl.pallas_call(
        owner_kernel,
        out_shape=[
            jax.ShapeDtypeStruct((128, F_BLOCK), f32),
            jax.ShapeDtypeStruct((E_BLOCK // 256, 16, 256), f32),
            jax.ShapeDtypeStruct((C_BLOCK // 256, 8, 256), f32),
            jax.ShapeDtypeStruct((MSG, 128), f32),
            jax.ShapeDtypeStruct((MSG, 128), f32),
            jax.ShapeDtypeStruct((BOTH, 128), f32),
        ],
        interpret=INTERPRET,
        name="owner",
    )(tf, te, tc, got_dom, got_sub, got_both)


def relax_kernel(
    devs, owner, keys, tf, te, tc, rd, rs, rb, im_in, dg_in, sol, forc,
    out, o0, o1, o2, o3, im, dg, tfs, of, gf, ge, gc, rel,
):
    im[...] = im_in[...]
    dg[...] = dg_in[...]
    for s, p in enumerate(split3(tf[...])):
        tfs[s * 128 : (s + 1) * 128, 0:1536] = p
    for s, p in enumerate(split3(rd[0:128, :])):
        tfs[s * 128 : (s + 1) * 128, 1536:1664] = p
    for s, p in enumerate(split3(rs[0:128, :])):
        tfs[s * 128 : (s + 1) * 128, 1664:1792] = p

    def face_gather(f, carry):
        key = keys[pl.ds(f, 1), :]
        for n in range(F_KEYS // 256):
            of[n * 256 : (n + 1) * 256, :] = onehot(small_row(key - n * 256, 256), 256)
        gf[f] = sum3(dot_nn(tfs[...], of[...]))
        return carry

    lax.fori_loop(0, 6, face_gather, 0)

    lane = lax.broadcasted_iota(i32, (1, 128), 1)

    def table(own, his, rows, at, cut):
        blocks = [own[h] for h in range(his)]
        for src in (rd, rs):
            for g in (0, 2):
                pair = []
                for q in (g, g + 1):
                    r = msg_rows(q)[at]
                    v = src[r : r + rows, :]
                    if src is rd and q == 3:
                        b = r - (MSG - BOTH)
                        v = jnp.where(jnp.broadcast_to(lane, (rows, 128)) >= cut, rb[b : b + rows, :], v)
                    pair.append(v)
                blocks.append(jnp.concatenate(pair, axis=1))
        return stack3(jnp.concatenate(blocks, axis=0))

    def line_gather(tab, first, count, his, rows, dst):
        def one(q, carry):
            key = keys[pl.ds(first + q, 1), :]
            hi = key >> 8
            y = sum3(dot_nn(tab, onehot(small_row(key & 255, 256), 256)))
            back = jnp.zeros((rows, E), f32)
            for h in range(his):
                back = jnp.where(jnp.broadcast_to(hi, (rows, E)) == h, y[h * rows : (h + 1) * rows], back)
            dst[q] = back
            return carry

        lax.fori_loop(0, count, one, 0)

    line_gather(table(te, 6, 16, 0, 96), 6, 12, E_HI, 16, ge)
    line_gather(table(tc, 2, 8, 1, 64), 18, 8, C_HI, 8, gc)

    for c in range(4):
        at = slice(c * 128, (c + 1) * 128)
        for ref, base in ((im.at[c], 0), (dg.at[c], 1)):
            for f in range(6):
                v = gf[f, base * 64 : base * 64 + 64, at]
                if f < 2:
                    start = 0 if f == 0 else 448
                    ref[start : start + 64, :] = v
                elif f < 4:
                    j = 0 if f == 2 else 7
                    for i in range(N):
                        ref[pl.ds((i * N + j) * N, N), :] = v[i * N : (i + 1) * N]
                else:
                    ref[pl.ds(0 if f == 4 else 7, 64, stride=N), :] = v
            for e in range(12):
                start, stride = EDGE_ROWS[e]
                rows = pl.ds(start, N) if stride == 1 else pl.ds(start, N, stride=stride)
                ref[rows, :] = ge[e, base * 8 : base * 8 + 8, at]
            for q in range(8):
                r = CORNER_ROWS[q]
                ref[r : r + 1, :] = gc[q, base : base + 1, at]
        s = sol[:, :, :, at].reshape(NODES, 128)
        v = s + RELAX * (forc[:, :, :, at].reshape(NODES, 128) - im[c]) / dg[c]
        rel[:, at] = v
    out[...] = rel[...].reshape(N, N, N, E)
    _, leave, _ = move_rows(owner[...], [devs[d] for d in range(5)], prefix_matrix())
    pa = onehot(small_row(leave, 256), 256)
    pb = onehot(small_row(swapped(leave), 256), 256)
    for ref, val in zip((o0, o1, o2, o3), pack_block(rel[...], pa, pb)):
        ref[...] = val


def gather_relax(devs, owner, keys, tf, te, tc, rd, rs, rb, im, dg, solution, forcing):
    half = NODES // 2
    vm = pl.BlockSpec(memory_space=pltpu.VMEM)
    return pl.pallas_call(
        relax_kernel,
        in_specs=[pl.BlockSpec(memory_space=pltpu.SMEM)] + [vm] * 12,
        out_shape=[jax.ShapeDtypeStruct((N, N, N, E), f32)] + [jax.ShapeDtypeStruct((half, 128), f32)] * 4,
        scratch_shapes=[
            pltpu.VMEM((4, NODES, 128), f32),
            pltpu.VMEM((4, NODES, 128), f32),
            pltpu.VMEM((384, F_KEYS), bf16),
            pltpu.VMEM((F_KEYS, E), bf16),
            pltpu.VMEM((6, 128, E), f32),
            pltpu.VMEM((12, 16, E), f32),
            pltpu.VMEM((8, 8, E), f32),
            pltpu.VMEM((NODES, E), f32),
        ],
        compiler_params=pltpu.CompilerParams(vmem_limit_bytes=48 << 20),
        interpret=INTERPRET,
        name="relax",
    )(devs, owner, keys, tf, te, tc, rd, rs, rb, im, dg, solution, forcing)


def land_kernel(devs, owner_ref, x_ref, a0, a1, a2, a3, out, pa, pb, dep):
    @pl.when(pl.program_id(0) == 0)
    def _():
        departed, _, arrive = move_rows(owner_ref[...], [devs[d] for d in range(5)], prefix_matrix())
        pa[...] = onehot(small_row(arrive, 256), 256)
        pb[...] = onehot(small_row(swapped(arrive), 256), 256)
        dep[...] = jnp.broadcast_to(jnp.where(departed, 1.0, 0.0), (8, E))

    departed = dep[0:1, :] > 0.5
    got = [a[...] for a in (a0, a1, a2, a3)]
    shape = x_ref.shape
    lo, hi = land_block(x_ref[...].reshape(NODES, E), got, pa[...], pb[...], departed)
    half = shape[:-4] + (N // 2, N, N, E)
    if len(shape) == 5:
        out[0, 0:4] = lo.reshape(half[1:])
        out[0, 4:8] = hi.reshape(half[1:])
    else:
        out[0:4] = lo.reshape(half)
        out[4:8] = hi.reshape(half)


def land(devs, owner, x, got, name):
    half = NODES // 2
    parts = x.shape[0] if x.ndim == 5 else 1
    if x.ndim == 5:
        spec = pl.BlockSpec((1, N, N, N, E), lambda m: (m, 0, 0, 0, 0))
    else:
        spec = pl.BlockSpec((N, N, N, E), lambda m: (0, 0, 0, 0))
    return pl.pallas_call(
        land_kernel,
        grid=(parts,),
        in_specs=[
            pl.BlockSpec(memory_space=pltpu.SMEM),
            pl.BlockSpec((1, E), lambda m: (0, 0)),
            spec,
        ]
        + [pl.BlockSpec((half, 128), lambda m: (m, 0))] * 4,
        out_specs=spec,
        out_shape=jax.ShapeDtypeStruct(x.shape, f32),
        scratch_shapes=[pltpu.VMEM((256, E), bf16)] * 2 + [pltpu.VMEM((8, E), f32)],
        interpret=INTERPRET,
        name=name,
    )(devs, owner, x, *got)


def shift(value, axis, steps):
    count = lax.axis_size(axis)
    return lax.ppermute(value, axis, [(s, (s + steps) % count) for s in range(count)])


def shift_both(value, steps):
    a, b = lax.axis_size("dom"), lax.axis_size("sub")
    pairs = [(d * b + s, (d + steps) % a * b + (s + steps) % b) for d in range(a) for s in range(b)]
    return lax.ppermute(value, ("dom", "sub"), pairs)


def exchange(sent):
    return [
        shift(sent[1], "dom", 1),
        shift(sent[0], "dom", -1),
        shift(sent[3], "sub", 1),
        shift(sent[2], "sub", -1),
    ]


def on_device(solution, forcing, metric, entity_ids, new_owner):
    a, b = lax.axis_size("dom"), lax.axis_size("sub")
    d, s = lax.axis_index("dom"), lax.axis_index("sub")
    da, db = (d + 1) % a, (d + a - 1) % a
    sa, sb = (s + 1) % b, (s + b - 1) % b
    devs = jnp.stack([d * b + s, db * b + s, da * b + s, d * b + sb, d * b + sa, da * b + sa]).astype(i32)
    owner = new_owner.reshape(1, E)

    sent = pack_metric(devs, owner, metric)
    im, dg, keys, tf, te, tc, md, ms = apply_scatter(devs, entity_ids, solution, metric)
    gd = shift(md, "dom", 1)
    gs = shift(ms, "sub", 1)
    gb = shift_both(md[MSG - BOTH :], 1)
    tf, te, tc, rd, rs, rb = owner_sums(tf, te, tc, gd, gs, gb)
    rd = shift(rd, "dom", -1)
    rs = shift(rs, "sub", -1)
    rb = shift_both(rb, -1)
    relaxed, *moved = gather_relax(
        devs, owner, keys, tf, te, tc, rd, rs, rb, im, dg, solution, forcing
    )
    moved_metric = land(devs, owner, metric, exchange(sent), "land_metric")
    smoothed = land(devs, owner, relaxed, exchange(moved), "land_field")
    return smoothed, moved_metric


def solution(mesh):
    cols = ("dom", "sub")
    placed = (
        P(None, None, None, cols),
        P(None, None, None, cols),
        P(None, None, None, None, cols),
        P(None, cols),
        P(cols),
    )
    return jax.shard_map(
        on_device,
        mesh=mesh,
        in_specs=placed,
        out_specs=(P(None, None, None, cols), P(None, None, None, None, cols)),
        check_vma=False,
    )
```

```python
import functools

import jax
import jax.numpy as jnp
import numpy as np
from jax import lax
from jax.experimental import pallas as pl
from jax.experimental.pallas import tpu as pltpu
from jax.sharding import PartitionSpec as P

N = 8
E = 512
NODES = N * N * N
EX = 4
EY = 4
EZ = 32
MOVE = 64
RELAX = 0.6
F_BLOCK, E_BLOCK, C_BLOCK = 3 * E, 3 * E, E
F_KEYS, E_KEYS, C_KEYS = 1792, 2560, 1536
E_HI, C_HI = E_KEYS // 256, C_KEYS // 256
MSG = 224
BOTH = 24
INTERPRET = False

f32, bf16, i32 = jnp.float32, jnp.bfloat16, jnp.int32


def derivative_table(order):
    count = order + 1
    points = -np.cos(np.pi * np.arange(count) / order)
    legendre = np.zeros((count, count))
    for sweep in range(80):
        legendre[:, 0] = 1.0
        legendre[:, 1] = points
        for degree in range(2, count):
            legendre[:, degree] = (
                (2 * degree - 1) * points * legendre[:, degree - 1]
                - (degree - 1) * legendre[:, degree - 2]
            ) / degree
        points = points - (points * legendre[:, order] - legendre[:, order - 1]) / (
            count * legendre[:, order]
        )
    legendre[:, 0] = 1.0
    legendre[:, 1] = points
    for degree in range(2, count):
        legendre[:, degree] = (
            (2 * degree - 1) * points * legendre[:, degree - 1]
            - (degree - 1) * legendre[:, degree - 2]
        ) / degree
    values = legendre[:, order]
    identity = np.eye(count)
    spread = points[:, None] - points[None, :] + identity
    table = values[:, None] / values[None, :] / spread
    table = table * (1.0 - identity)
    table[0, 0] = -order * count / 4.0
    table[order, order] = order * count / 4.0
    return table.astype(np.float32)


TABLE = derivative_table(N - 1)
SQUARED = TABLE * TABLE
ALONG = [float(v) for v in np.diagonal(TABLE)]


def row_of(i, j, k):
    return (i * N + j) * N + k


EDGE_ROWS = (
    [(row_of(0, a, b), N * N) for a in (0, 7) for b in (0, 7)]
    + [(row_of(a, 0, b), N) for a in (0, 7) for b in (0, 7)]
    + [(row_of(a, b, 0), 1) for a in (0, 7) for b in (0, 7)]
)
CORNER_ROWS = [row_of(a, b, c) for a in (0, 7) for b in (0, 7) for c in (0, 7)]


def split3(x):
    hi = x.astype(bf16)
    rest = x - hi.astype(f32)
    mid = rest.astype(bf16)
    low = (rest - mid.astype(f32)).astype(bf16)
    return hi, mid, low


def stack3(x):
    return jnp.concatenate(split3(x), axis=0)


def sum3(x):
    m = x.shape[0] // 3
    return x[0:m] + x[m : 2 * m] + x[2 * m : 3 * m]


def dot_nn(a, b):
    return lax.dot_general(a, b, (((1,), (0,)), ((), ())), preferred_element_type=f32)


def dot_nt(a, b):
    return lax.dot_general(a, b, (((1,), (1,)), ((), ())), preferred_element_type=f32)


def small_row(key, count):
    ok = (key >= 0) & (key < count)
    return jnp.where(ok, key, -1).astype(f32).astype(bf16)


def iota_rows(count, lanes):
    return lax.broadcasted_iota(i32, (count, lanes), 0).astype(f32).astype(bf16)


def onehot(row, count):
    lanes = row.shape[1]
    io = iota_rows(count, 128)
    one, zero = jnp.ones((count, 128), bf16), jnp.zeros((count, 128), bf16)
    cols = [
        jnp.where(io == jnp.broadcast_to(row[:, g : g + 128], (count, 128)), one, zero)
        for g in range(0, lanes, 128)
    ]
    return cols[0] if len(cols) == 1 else jnp.concatenate(cols, axis=1)


def prefix_matrix():
    a = lax.broadcasted_iota(i32, (E, E), 0)
    b = lax.broadcasted_iota(i32, (E, E), 1)
    return jnp.where(a <= b, 1.0, 0.0).astype(bf16)


def ranks(mask, tri):
    m = mask.shape[0]
    flags = jnp.where(mask, 1.0, 0.0)
    within = dot_nn(flags.astype(bf16), tri) - 1.0
    if m > 1:
        before = jnp.zeros((1, 1), f32)
        offs = [before]
        for r in range(m - 1):
            before = before + jnp.sum(flags[r : r + 1], axis=1, keepdims=True)
            offs.append(before)
        within = within + jnp.concatenate(offs, axis=0)
    return within.astype(i32)


def move_rows(owner, devs, tri):
    own = devs[0]
    departed = owner != own
    leave = jnp.full((1, E), -1, i32)
    arrive = jnp.full((1, E), -1, i32)
    flags = [departed] + [departed & (owner == devs[d]) for d in range(1, 5)]
    stacked = jnp.concatenate([jnp.where(f, 1.0, 0.0) for f in flags] + [jnp.zeros((3, E), f32)], axis=0)
    pre = dot_nn(stacked.astype(bf16), tri)
    hole = pre[0:1] - 1.0
    start = jnp.zeros((1, 1), f32)
    for d in range(4):
        chosen = flags[d + 1]
        rank = pre[d + 1 : d + 2] - 1.0
        leave = jnp.where(chosen, d * MOVE + rank.astype(i32), leave)
        count = pre[d + 1 : d + 2, E - 1 : E]
        pos = hole - start
        inside = departed & (pos >= 0.0) & (pos < count)
        arrive = jnp.where(inside, d * MOVE + pos.astype(i32), arrive)
        start = start + count
    return departed, leave, arrive


def swapped(col):
    return jnp.where(col >= 0, col ^ MOVE, -1)


def lane_low(rows):
    return lax.broadcasted_iota(i32, (rows, 128), 1) < MOVE


def pack_block(x, pa, pb):
    half = NODES // 2
    ya = sum3(dot_nt(stack3(x[0:half]), pa))
    yb = sum3(dot_nt(stack3(x[half:]), pb))
    low = lane_low(half)
    out = []
    for g in (0, 128):
        a, b = ya[:, g : g + 128], yb[:, g : g + 128]
        out.append(jnp.where(low, a, b))
        out.append(jnp.where(low, b, a))
    return out


def land_block(x, got, pa, pb, departed):
    half = NODES // 2
    low = lane_low(half)
    zl, zh = [], []
    for g in (0, 2):
        zl.append(jnp.where(low, got[g + 1], got[g]))
        zh.append(jnp.where(low, got[g], got[g + 1]))
    zl = jnp.concatenate(zl, axis=1)
    zh = jnp.concatenate(zh, axis=1)
    yl = sum3(dot_nn(stack3(zl), pb))
    yh = sum3(dot_nn(stack3(zh), pa))
    keep = jnp.logical_not(departed)
    return jnp.where(keep, x[0:half], yl), jnp.where(keep, x[half:], yh)


def pack_kernel(devs, owner_ref, met_ref, o0, o1, o2, o3, pa, pb):
    @pl.when(pl.program_id(0) == 0)
    def _():
        _, leave, _ = move_rows(owner_ref[...], [devs[d] for d in range(5)], prefix_matrix())
        pa[...] = onehot(small_row(leave, 256), 256)
        pb[...] = onehot(small_row(swapped(leave), 256), 256)

    out = pack_block(met_ref[0].reshape(NODES, E), pa[...], pb[...])
    for ref, val in zip((o0, o1, o2, o3), out):
        ref[...] = val


def pack_metric(devs, owner, metric):
    half = NODES // 2
    return pl.pallas_call(
        pack_kernel,
        grid=(7,),
        in_specs=[
            pl.BlockSpec(memory_space=pltpu.SMEM),
            pl.BlockSpec((1, E), lambda m: (0, 0)),
            pl.BlockSpec((1, N, N, N, E), lambda m: (m, 0, 0, 0, 0)),
        ],
        out_specs=[pl.BlockSpec((half, 128), lambda m: (m, 0))] * 4,
        out_shape=[jax.ShapeDtypeStruct((7 * half, 128), f32)] * 4,
        scratch_shapes=[pltpu.VMEM((256, E), bf16)] * 2,
        interpret=INTERPRET,
        name="pack",
    )(devs, owner, metric)


def contract_i(src, table, put):
    for j in range(N):
        xs = [src(i, j) for i in range(N)]
        for a in range(N):
            put(a, j, sum(float(table[a, i]) * xs[i] for i in range(N) if table[a, i] != 0.0))


def contract_j(src, table, put):
    for i in range(N):
        xs = [src(i, j) for j in range(N)]
        for b in range(N):
            put(i, b, sum(float(table[b, j]) * xs[j] for j in range(N) if table[b, j] != 0.0))


def key_rows(ids, block, devs, dom_base, both_base, sub_base, tri):
    rel, inside = [], []
    for d in (0, 2, 4, 5):
        r = ids - devs[d] * block
        rel.append(r)
        inside.append((r >= 0) & (r < block))
    key = jnp.where(inside[0], rel[0], -1)
    key = jnp.where(inside[1], dom_base + ranks(inside[1], tri), key)
    key = jnp.where(inside[2], sub_base + ranks(inside[2], tri), key)
    if both_base is not None:
        key = jnp.where(inside[3], both_base + ranks(inside[3], tri), key)
    row = jnp.where(inside[0], rel[0], jnp.where(inside[1], rel[1], jnp.where(inside[2], rel[2], rel[3])))
    return key, row.astype(f32)


def tile(ref, r):
    return ref[pl.ds(r * N, N), :]


def apply_kernel(
    devs, ids, sol, met, kmat, im_out, dg_out, key_out, tf, te, tc, md, ms,
    vf, ve, vc, rix, ga, gb, gc, of, le, ol, acc_e,
):
    c = pl.program_id(0)

    @pl.when(c == 0)
    def _():
        tri = prefix_matrix()
        dv = [devs[d] for d in range(6)]
        k, r = key_rows(ids[0:6], F_BLOCK, dv, 1536, None, 1664, tri)
        key_out[0:6, :] = k
        rix[0:6, :] = r
        k, r = key_rows(ids[6:18], E_BLOCK, dv, 1536, 2016, 2048, tri)
        key_out[6:18, :] = k
        rix[6:18, :] = r
        k, r = key_rows(ids[18:26], C_BLOCK, dv, 512, 960, 1024, tri)
        key_out[18:26, :] = k
        rix[18:26, :] = r

    im, dg = im_out.at[0], dg_out.at[0]
    fwd, bwd = kmat.at[0], kmat.at[1]
    half = NODES // 2

    def kdot(m, x):
        return lax.dot_general(
            m, x, (((1,), (0,)), ((), ())),
            precision=lax.Precision.HIGHEST, preferred_element_type=f32,
        )

    def put_a(i, j, v):
        ga[pl.ds((i * N + j) * N, N), :] = v

    def put_b(i, j, v):
        gb[pl.ds((i * N + j) * N, N), :] = v

    contract_i(lambda i, j: sol[i, j], TABLE, put_a)
    contract_j(lambda i, j: sol[i, j], TABLE, put_b)
    for h in range(2):
        x = sol[h * 4 : h * 4 + 4].reshape(half, 128)
        gc[h * half : (h + 1) * half, :] = kdot(fwd[...], x)

    for i in range(N):
        for j in range(N):
            r = i * N + j
            a, b, t = tile(ga, r), tile(gb, r), tile(gc, r)
            m3, m4, m5 = met[3, i, j], met[4, i, j], met[5, i, j]
            ga[pl.ds(r * N, N), :] = met[0, i, j] * a + m3 * b + m4 * t
            gb[pl.ds(r * N, N), :] = m3 * a + met[1, i, j] * b + m5 * t
            gc[pl.ds(r * N, N), :] = m4 * a + m5 * b + met[2, i, j] * t

    for h in range(2):
        im[h * half : (h + 1) * half, :] = kdot(bwd[...], gc[h * half : (h + 1) * half, :])

    def add_im(i, j, v):
        im[pl.ds((i * N + j) * N, N), :] += v

    contract_i(lambda i, j: tile(ga, i * N + j), TABLE.T, add_im)

    def add_im_last(i, j, v):
        im[pl.ds((i * N + j) * N, N), :] += v + met[6, i, j] * sol[i, j]

    contract_j(lambda i, j: tile(gb, i * N + j), TABLE.T, add_im_last)

    sq = kmat.at[2]
    for h in range(2):
        x = met[2, h * 4 : h * 4 + 4].reshape(half, 128)
        dg[h * half : (h + 1) * half, :] = kdot(sq[...], x)

    def add_dg(i, j, v):
        dg[pl.ds((i * N + j) * N, N), :] += v

    contract_i(lambda i, j: met[0, i, j], SQUARED.T, add_dg)
    kk = lax.broadcasted_iota(i32, (N, 128), 0)
    dk = jnp.where(kk == 0, ALONG[0], jnp.where(kk == N - 1, ALONG[N - 1], 0.0))

    def add_dg_last(i, j, v):
        v = v + met[6, i, j]
        if ALONG[i] * ALONG[j] != 0.0:
            v = v + (2.0 * ALONG[i] * ALONG[j]) * met[3, i, j]
        if ALONG[i] != 0.0:
            v = v + (2.0 * ALONG[i]) * dk * met[4, i, j]
        if ALONG[j] != 0.0:
            v = v + (2.0 * ALONG[j]) * dk * met[5, i, j]
        dg[pl.ds((i * N + j) * N, N), :] += v

    contract_j(lambda i, j: met[1, i, j], SQUARED.T, add_dg_last)

    lanes = pl.ds(pl.multiple_of(c * 128, 128), 128)

    def face(ref, f):
        if f < 2:
            base = 0 if f == 0 else 448
            return ref[base : base + 64, :]
        if f < 4:
            j = 0 if f == 2 else 7
            return jnp.concatenate([ref[pl.ds((i * N + j) * N, N), :] for i in range(N)], axis=0)
        return ref[pl.ds(0 if f == 4 else 7, 64, stride=N), :]

    top = lax.broadcasted_iota(i32, (N, 128), 0) == 0
    for f in range(6):
        at = pl.ds(pl.multiple_of(f * E + c * 128, 128), 128)
        a, b = face(im, f), face(dg, f)
        mark = jnp.broadcast_to(rix[f : f + 1, lanes], (N, 128))
        a = jnp.concatenate([jnp.where(top, mark, a[0:N]), a[N:]], axis=0)
        for s, (p, q) in enumerate(zip(split3(a), split3(b))):
            vf[s * 128 : s * 128 + 64, at] = p
            vf[s * 128 + 64 : s * 128 + 128, at] = q
    for e in range(12):
        at = pl.ds(pl.multiple_of(e * E + c * 128, 128), 128)
        start, stride = EDGE_ROWS[e]
        rows = pl.ds(start, N) if stride == 1 else pl.ds(start, N, stride=stride)
        a, b = im[rows, :], dg[rows, :]
        mark = jnp.broadcast_to(rix[6 + e : 7 + e, lanes], (N, 128))
        x = jnp.concatenate([jnp.where(top, mark, a), b], axis=0)
        for s, p in enumerate(split3(x)):
            ve[s * 16 : s * 16 + 16, at] = p
    for q in range(8):
        at = pl.ds(pl.multiple_of(q * E + c * 128, 128), 128)
        r = CORNER_ROWS[q]
        vc[0:1, at] = im[r : r + 1, :]
        vc[1:2, at] = dg[r : r + 1, :]
        vc[2:3, at] = rix[18 + q : 19 + q, lanes]
        vc[3:8, at] = jnp.zeros((5, 128), f32)

    @pl.when(c == 3)
    def _():
        def face_block(n, carry):
            for f in range(6):
                of[:, f * E : (f + 1) * E] = onehot(small_row(key_out[f : f + 1, :] - n * 256, 256), 256)
            acc = dot_nt(vf[...], of[...])
            tf[:, pl.ds(pl.multiple_of(n * 256, 256), 256)] = sum3(acc)
            return carry

        lax.fori_loop(0, F_KEYS // 256, face_block, 0)

        for e in range(12):
            at = slice(e * E, (e + 1) * E)
            key = key_out[6 + e : 7 + e, :]
            hi = small_row(key >> 8, E_HI)
            ol[:, at] = onehot(small_row(key & 255, 256), 256)
            for g in range(4):
                ag = slice(e * E + g * 128, e * E + (g + 1) * 128)
                hb = jnp.broadcast_to(hi[:, g * 128 : (g + 1) * 128], (16, 128))
                zero = jnp.zeros((16, 128), bf16)
                parts = [ve[s * 16 : s * 16 + 16, ag] for s in range(3)]
                for h in range(E_HI):
                    m = hb == jnp.full((16, 128), float(h), bf16)
                    for s in range(3):
                        le[(s * E_HI + h) * 16 : (s * E_HI + h + 1) * 16, ag] = jnp.where(m, parts[s], zero)
        acc_e[...] = dot_nt(le[...], ol[...])
        for h in range(E_HI):
            te[h] = sum(acc_e[(s * E_HI + h) * 16 : (s * E_HI + h + 1) * 16, :] for s in range(3))

        full = E * 8
        for q in range(8):
            at = slice(q * E, (q + 1) * E)
            ol[:, at] = onehot(small_row(key_out[18 + q : 19 + q, :] & 255, 256), 256)
        hi = jnp.concatenate([key_out[18 + q : 19 + q, :] >> 8 for q in range(8)], axis=1)
        x = vc[...]
        big = jnp.concatenate(
            [jnp.where(jnp.broadcast_to(hi, (8, full)) == h, x, 0.0) for h in range(C_HI)], axis=0
        )
        acc = sum3(dot_nt(stack3(big), ol[:, 0:full]))
        for h in range(C_HI):
            tc[h] = acc[h * 8 : (h + 1) * 8]

        md[0:128, :] = tf[:, 1536:1664]
        ms[0:128, :] = tf[:, 1664:1792]
        for g in range(4):
            er, cr = msg_rows(g)
            half_lanes = slice((g % 2) * 128, (g % 2) * 128 + 128)
            md[er : er + 16, :] = te[6 + g // 2, :, half_lanes]
            ms[er : er + 16, :] = te[8 + g // 2, :, half_lanes]
            md[cr : cr + 8, :] = tc[2 + g // 2, :, half_lanes]
            ms[cr : cr + 8, :] = tc[4 + g // 2, :, half_lanes]


def msg_rows(g):
    if g < 3:
        return 128 + 16 * g, 176 + 8 * g
    return 200, 216


def apply_scatter(devs, ids, solution, metric):
    eye = np.eye(NODES // 2 // N, dtype=np.float32)
    kmat = np.stack([np.kron(eye, TABLE), np.kron(eye, TABLE.T), np.kron(eye, SQUARED.T)])
    chunk = lambda c: (c, 0, 0)
    whole2 = lambda c: (0, 0)
    whole3 = lambda c: (0, 0, 0)
    return pl.pallas_call(
        apply_kernel,
        grid=(4,),
        in_specs=[
            pl.BlockSpec(memory_space=pltpu.SMEM),
            pl.BlockSpec((26, E), whole2),
            pl.BlockSpec((N, N, N, 128), lambda c: (0, 0, 0, c)),
            pl.BlockSpec((7, N, N, N, 128), lambda c: (0, 0, 0, 0, c)),
            pl.BlockSpec((3, 256, 256), whole3),
        ],
        out_specs=[
            pl.BlockSpec((1, NODES, 128), chunk),
            pl.BlockSpec((1, NODES, 128), chunk),
            pl.BlockSpec((26, E), whole2),
            pl.BlockSpec((128, F_KEYS), whole2),
            pl.BlockSpec((E_HI, 16, 256), whole3),
            pl.BlockSpec((C_HI, 8, 256), whole3),
            pl.BlockSpec((MSG, 128), whole2),
            pl.BlockSpec((MSG, 128), whole2),
        ],
        out_shape=[
            jax.ShapeDtypeStruct((4, NODES, 128), f32),
            jax.ShapeDtypeStruct((4, NODES, 128), f32),
            jax.ShapeDtypeStruct((26, E), i32),
            jax.ShapeDtypeStruct((128, F_KEYS), f32),
            jax.ShapeDtypeStruct((E_HI, 16, 256), f32),
            jax.ShapeDtypeStruct((C_HI, 8, 256), f32),
            jax.ShapeDtypeStruct((MSG, 128), f32),
            jax.ShapeDtypeStruct((MSG, 128), f32),
        ],
        scratch_shapes=[
            pltpu.VMEM((384, 6 * E), bf16),
            pltpu.VMEM((48, 12 * E), bf16),
            pltpu.VMEM((8, 8 * E), f32),
            pltpu.VMEM((26, E), f32),
            pltpu.VMEM((NODES, 128), f32),
            pltpu.VMEM((NODES, 128), f32),
            pltpu.VMEM((NODES, 128), f32),
            pltpu.VMEM((256, 6 * E), bf16),
            pltpu.VMEM((3 * E_HI * 16, 12 * E), bf16),
            pltpu.VMEM((256, 12 * E), bf16),
            pltpu.VMEM((3 * E_HI * 16, 256), f32),
        ],
        compiler_params=pltpu.CompilerParams(vmem_limit_bytes=56 << 20),
        interpret=INTERPRET,
        name="apply",
    )(devs, ids, solution, metric, kmat)


def owner_sums(tf, te, tc, gd, gs, gboth, tf2, te2, tc2, rd, rs, rb):
    vals = jnp.concatenate([gd[0:128, :], gs[0:128, :]], axis=1)
    key = vals[0:1, :].astype(i32)
    vs = stack3(vals)
    ret = jnp.zeros((384, 256), f32)
    for n in range(F_BLOCK // 256):
        o = onehot(small_row(key - n * 256, 256), 256)
        total = tf[:, n * 256 : (n + 1) * 256] + sum3(dot_nt(vs, o))
        tf2[:, n * 256 : (n + 1) * 256] = total
        ret = ret + dot_nn(stack3(total), o)
    ret = sum3(ret)
    rd[0:128, :] = ret[:, 0:128]
    rs[0:128, :] = ret[:, 128:256]

    lane = lax.broadcasted_iota(i32, (1, 128), 1)

    def lines(rows, id_row, total_ref, total_out, his, cut, at):
        vals, keys = [], []
        for src in (gd, gs):
            for g in range(4):
                r = msg_rows(g)[at]
                v = src[r : r + rows, :]
                k = v[id_row : id_row + 1].astype(i32)
                if src is gd and g == 3:
                    k = jnp.where(lane >= cut, -1, k)
                vals.append(v)
                keys.append(k)
        r = msg_rows(3)[at] - (MSG - BOTH)
        v = gboth[r : r + rows, :]
        keys.append(jnp.where(lane < cut, -1, v[id_row : id_row + 1].astype(i32)))
        vals.append(v)
        x = jnp.concatenate(vals, axis=1)
        key = jnp.concatenate(keys, axis=1)
        hi = key >> 8
        o = onehot(small_row(key & 255, 256), 256)
        big = jnp.concatenate([jnp.where(jnp.broadcast_to(hi, x.shape) == h, x, 0.0) for h in range(his)], axis=0)
        acc = sum3(dot_nt(stack3(big), o))
        totals = jnp.concatenate([total_ref[h] for h in range(his)], axis=0) + acc
        for h in range(his):
            total_out[h] = totals[h * rows : (h + 1) * rows]
        y = sum3(dot_nn(stack3(totals), o))
        back = jnp.zeros_like(x)
        for h in range(his):
            back = jnp.where(jnp.broadcast_to(hi, x.shape) == h, y[h * rows : (h + 1) * rows], back)
        for n, dst in enumerate((rd, rs)):
            for g in range(4):
                p = msg_rows(g)[at]
                dst[p : p + rows, :] = back[:, (n * 4 + g) * 128 : (n * 4 + g + 1) * 128]
        rb[r : r + rows, :] = back[:, 1024:1152]

    lines(16, 0, te, te2, E_BLOCK // 256, 96, 0)
    lines(8, 2, tc, tc2, C_BLOCK // 256, 64, 1)


def gather_shared(keys, tf, te, tc, rd, rs, rb, tfs, of, gf, ge, gc):
    for s, p in enumerate(split3(tf[...])):
        tfs[s * 128 : (s + 1) * 128, 0:1536] = p
    for s, p in enumerate(split3(rd[0:128, :])):
        tfs[s * 128 : (s + 1) * 128, 1536:1664] = p
    for s, p in enumerate(split3(rs[0:128, :])):
        tfs[s * 128 : (s + 1) * 128, 1664:1792] = p

    def face_gather(f, carry):
        key = keys[pl.ds(f, 1), :]
        for n in range(F_KEYS // 256):
            of[n * 256 : (n + 1) * 256, :] = onehot(small_row(key - n * 256, 256), 256)
        gf[f] = sum3(dot_nn(tfs[...], of[...]))
        return carry

    lax.fori_loop(0, 6, face_gather, 0)

    lane = lax.broadcasted_iota(i32, (1, 128), 1)

    def table(own, his, rows, at, cut):
        blocks = [own[h] for h in range(his)]
        for src in (rd, rs):
            for g in (0, 2):
                pair = []
                for q in (g, g + 1):
                    r = msg_rows(q)[at]
                    v = src[r : r + rows, :]
                    if src is rd and q == 3:
                        b = r - (MSG - BOTH)
                        v = jnp.where(jnp.broadcast_to(lane, (rows, 128)) >= cut, rb[b : b + rows, :], v)
                    pair.append(v)
                blocks.append(jnp.concatenate(pair, axis=1))
        return stack3(jnp.concatenate(blocks, axis=0))

    def line_gather(tab, first, count, his, rows, dst):
        def one(q, carry):
            key = keys[pl.ds(first + q, 1), :]
            hi = key >> 8
            y = sum3(dot_nn(tab, onehot(small_row(key & 255, 256), 256)))
            back = jnp.zeros((rows, E), f32)
            for h in range(his):
                back = jnp.where(jnp.broadcast_to(hi, (rows, E)) == h, y[h * rows : (h + 1) * rows], back)
            dst[q] = back
            return carry

        lax.fori_loop(0, count, one, 0)

    line_gather(table(te, 6, 16, 0, 96), 6, 12, E_HI, 16, ge)
    line_gather(table(tc, 2, 8, 1, 64), 18, 8, C_HI, 8, gc)

def place_relax(im, dg, gf, ge, gc, sol, forc, rel):
    for c in range(4):
        at = slice(c * 128, (c + 1) * 128)
        for ref, base in ((im.at[c], 0), (dg.at[c], 1)):
            for f in range(6):
                v = gf[f, base * 64 : base * 64 + 64, at]
                if f < 2:
                    start = 0 if f == 0 else 448
                    ref[start : start + 64, :] = v
                elif f < 4:
                    j = 0 if f == 2 else 7
                    for i in range(N):
                        ref[pl.ds((i * N + j) * N, N), :] = v[i * N : (i + 1) * N]
                else:
                    ref[pl.ds(0 if f == 4 else 7, 64, stride=N), :] = v
            for e in range(12):
                start, stride = EDGE_ROWS[e]
                rows = pl.ds(start, N) if stride == 1 else pl.ds(start, N, stride=stride)
                ref[rows, :] = ge[e, base * 8 : base * 8 + 8, at]
            for q in range(8):
                r = CORNER_ROWS[q]
                ref[r : r + 1, :] = gc[q, base : base + 1, at]
        s = sol[:, :, :, at].reshape(NODES, 128)
        v = s + RELAX * (forc[:, :, :, at].reshape(NODES, 128) - im[c]) / dg[c]
        rel[:, at] = v

MESH = pl.DeviceIdType.MESH


def exchange_kernel(
    owner, keys, tf, te, tc, md, ms, im_in, dg_in, sol_in, forc_in,
    out, a0, a1, a2, a3,
    gd, gs, gb, tf2, te2, tc2, sd, ss, sb, rd, rs, rb,
    im, dg, sol, forc, tfs, of, gf, ge, gc, rel, p0, p1, p2, p3,
    local_sem, send_sem, recv_sem,
):
    na, nb = lax.axis_size("dom"), lax.axis_size("sub")
    d, s = lax.axis_index("dom"), lax.axis_index("sub")
    dn, dp = lax.rem(d + 1, na), lax.rem(d + na - 1, na)
    sn, sp = lax.rem(s + 1, nb), lax.rem(s + nb - 1, nb)
    prev_dom, next_dom, prev_sub, next_sub = (dp, s), (dn, s), (d, sp), (d, sn)
    prev_both, next_both = (dp, sp), (dn, sn)
    loads = [
        pltpu.make_async_copy(src, dst, local_sem.at[n])
        for n, (src, dst) in enumerate(((im_in, im), (dg_in, dg), (sol_in, sol), (forc_in, forc)))
    ]
    for copy in loads:
        copy.start()

    barrier = pltpu.get_barrier_semaphore()
    for peer in (prev_dom, next_dom, prev_sub, next_sub, prev_both, next_both):
        pl.semaphore_signal(barrier, inc=1, device_id=peer, device_id_type=MESH)
    pl.semaphore_wait(barrier, 6)

    def send(n, src, dst, peer):
        copy = pltpu.make_async_remote_copy(
            src_ref=src, dst_ref=dst, send_sem=send_sem.at[n], recv_sem=recv_sem.at[n],
            device_id=peer, device_id_type=MESH,
        )
        copy.start()
        return copy

    first = [
        send(0, ms, gs, next_sub),
        send(1, md, gd, next_dom),
        send(2, md.at[pl.ds(MSG - BOTH, BOTH)], gb, next_both),
    ]
    for copy in first:
        copy.wait()
    owner_sums(tf, te, tc, gd, gs, gb, tf2, te2, tc2, sd, ss, sb)
    second = [
        send(3, ss, rs, prev_sub),
        send(4, sd, rd, prev_dom),
        send(5, sb, rb, prev_both),
    ]
    for copy in second:
        copy.wait()
    gather_shared(keys, tf2, te2, tc2, rd, rs, rb, tfs, of, gf, ge, gc)
    for copy in loads:
        copy.wait()
    place_relax(im, dg, gf, ge, gc, sol, forc, rel)
    devs = [x * nb + y for x, y in ((d, s), prev_dom, next_dom, prev_sub, next_sub)]
    _, leave, _ = move_rows(owner[...], devs, prefix_matrix())
    pa = onehot(small_row(leave, 256), 256)
    pb = onehot(small_row(swapped(leave), 256), 256)
    for ref, val in zip((p0, p1, p2, p3), pack_block(rel[...], pa, pb)):
        ref[...] = val
    third = [
        send(6, p2, a3, prev_sub),
        send(7, p3, a2, next_sub),
        send(8, p0, a1, prev_dom),
        send(9, p1, a0, next_dom),
    ]
    out[...] = rel[...].reshape(N, N, N, E)
    for copy in third:
        copy.wait()


def exchange_relax(owner, keys, tf, te, tc, md, ms, im, dg, solution, forcing):
    half = NODES // 2
    vm = pl.BlockSpec(memory_space=pltpu.VMEM)
    hbm = pl.BlockSpec(memory_space=pl.ANY)
    msg, both = pltpu.VMEM((MSG, 128), f32), pltpu.VMEM((BOTH, 128), f32)
    return pl.pallas_call(
        exchange_kernel,
        in_specs=[vm] * 7 + [hbm] * 4,
        out_shape=[jax.ShapeDtypeStruct((N, N, N, E), f32)] + [jax.ShapeDtypeStruct((half, 128), f32)] * 4,
        scratch_shapes=[
            msg, msg, both,
            pltpu.VMEM((128, F_BLOCK), f32),
            pltpu.VMEM((E_BLOCK // 256, 16, 256), f32),
            pltpu.VMEM((C_BLOCK // 256, 8, 256), f32),
            msg, msg, both, msg, msg, both,
            pltpu.VMEM((4, NODES, 128), f32),
            pltpu.VMEM((4, NODES, 128), f32),
            pltpu.VMEM((N, N, N, E), f32),
            pltpu.VMEM((N, N, N, E), f32),
            pltpu.VMEM((384, F_KEYS), bf16),
            pltpu.VMEM((F_KEYS, E), bf16),
            pltpu.VMEM((6, 128, E), f32),
            pltpu.VMEM((12, 16, E), f32),
            pltpu.VMEM((8, 8, E), f32),
            pltpu.VMEM((NODES, E), f32),
            pltpu.VMEM((half, 128), f32),
            pltpu.VMEM((half, 128), f32),
            pltpu.VMEM((half, 128), f32),
            pltpu.VMEM((half, 128), f32),
            pltpu.SemaphoreType.DMA((4,)),
            pltpu.SemaphoreType.DMA((10,)),
            pltpu.SemaphoreType.DMA((10,)),
        ],
        compiler_params=pltpu.CompilerParams(
            vmem_limit_bytes=48 << 20, collective_id=0, has_side_effects=True
        ),
        interpret=pltpu.InterpretParams() if INTERPRET else False,
        name="exchange",
    )(owner, keys, tf, te, tc, md, ms, im, dg, solution, forcing)


def land_kernel(devs, owner_ref, x_ref, a0, a1, a2, a3, out, pa, pb, dep):
    @pl.when(pl.program_id(0) == 0)
    def _():
        departed, _, arrive = move_rows(owner_ref[...], [devs[d] for d in range(5)], prefix_matrix())
        pa[...] = onehot(small_row(arrive, 256), 256)
        pb[...] = onehot(small_row(swapped(arrive), 256), 256)
        dep[...] = jnp.broadcast_to(jnp.where(departed, 1.0, 0.0), (8, E))

    departed = dep[0:1, :] > 0.5
    got = [a[...] for a in (a0, a1, a2, a3)]
    shape = x_ref.shape
    lo, hi = land_block(x_ref[...].reshape(NODES, E), got, pa[...], pb[...], departed)
    half = shape[:-4] + (N // 2, N, N, E)
    if len(shape) == 5:
        out[0, 0:4] = lo.reshape(half[1:])
        out[0, 4:8] = hi.reshape(half[1:])
    else:
        out[0:4] = lo.reshape(half)
        out[4:8] = hi.reshape(half)


def land(devs, owner, x, got, name):
    half = NODES // 2
    parts = x.shape[0] if x.ndim == 5 else 1
    if x.ndim == 5:
        spec = pl.BlockSpec((1, N, N, N, E), lambda m: (m, 0, 0, 0, 0))
    else:
        spec = pl.BlockSpec((N, N, N, E), lambda m: (0, 0, 0, 0))
    return pl.pallas_call(
        land_kernel,
        grid=(parts,),
        in_specs=[
            pl.BlockSpec(memory_space=pltpu.SMEM),
            pl.BlockSpec((1, E), lambda m: (0, 0)),
            spec,
        ]
        + [pl.BlockSpec((half, 128), lambda m: (m, 0))] * 4,
        out_specs=spec,
        out_shape=jax.ShapeDtypeStruct(x.shape, f32),
        scratch_shapes=[pltpu.VMEM((256, E), bf16)] * 2 + [pltpu.VMEM((8, E), f32)],
        interpret=INTERPRET,
        name=name,
    )(devs, owner, x, *got)


def shift(value, axis, steps):
    count = lax.axis_size(axis)
    return lax.ppermute(value, axis, [(s, (s + steps) % count) for s in range(count)])


def exchange(sent):
    return [
        shift(sent[1], "dom", 1),
        shift(sent[0], "dom", -1),
        shift(sent[3], "sub", 1),
        shift(sent[2], "sub", -1),
    ]


def on_device(solution, forcing, metric, entity_ids, new_owner):
    a, b = lax.axis_size("dom"), lax.axis_size("sub")
    d, s = lax.axis_index("dom"), lax.axis_index("sub")
    da, db = (d + 1) % a, (d + a - 1) % a
    sa, sb = (s + 1) % b, (s + b - 1) % b
    devs = jnp.stack([d * b + s, db * b + s, da * b + s, d * b + sb, d * b + sa, da * b + sa]).astype(i32)
    owner = new_owner.reshape(1, E)

    sent = pack_metric(devs, owner, metric)
    arrived = exchange(sent)
    later, *sent = lax.optimization_barrier((devs, *sent))
    im, dg, keys, tf, te, tc, md, ms = apply_scatter(later, entity_ids, solution, metric)
    relaxed, *moved = exchange_relax(owner, keys, tf, te, tc, md, ms, im, dg, solution, forcing)
    moved_metric = land(devs, owner, metric, arrived, "land_metric")
    smoothed = land(devs, owner, relaxed, moved, "land_field")
    return smoothed, moved_metric


def solution(mesh):
    cols = ("dom", "sub")
    placed = (
        P(None, None, None, cols),
        P(None, None, None, cols),
        P(None, None, None, None, cols),
        P(None, cols),
        P(cols),
    )
    return jax.shard_map(
        on_device,
        mesh=mesh,
        in_specs=placed,
        out_specs=(P(None, None, None, cols), P(None, None, None, None, cols)),
        check_vma=False,
    )
```

```python
import functools

import jax
import jax.numpy as jnp
import numpy as np
from jax import lax
from jax.experimental import pallas as pl
from jax.experimental.pallas import tpu as pltpu
from jax.sharding import PartitionSpec as P

N = 8
E = 512
NODES = N * N * N
EX = 4
EY = 4
EZ = 32
MOVE = 64
RELAX = 0.6
F_BLOCK, E_BLOCK, C_BLOCK = 3 * E, 3 * E, E
F_KEYS, E_KEYS, C_KEYS = 1792, 2560, 1536
E_HI, C_HI = E_KEYS // 256, C_KEYS // 256
MSG = 224
BOTH = 24
INTERPRET = False

f32, bf16, i32 = jnp.float32, jnp.bfloat16, jnp.int32


def derivative_table(order):
    count = order + 1
    points = -np.cos(np.pi * np.arange(count) / order)
    legendre = np.zeros((count, count))
    for sweep in range(80):
        legendre[:, 0] = 1.0
        legendre[:, 1] = points
        for degree in range(2, count):
            legendre[:, degree] = (
                (2 * degree - 1) * points * legendre[:, degree - 1]
                - (degree - 1) * legendre[:, degree - 2]
            ) / degree
        points = points - (points * legendre[:, order] - legendre[:, order - 1]) / (
            count * legendre[:, order]
        )
    legendre[:, 0] = 1.0
    legendre[:, 1] = points
    for degree in range(2, count):
        legendre[:, degree] = (
            (2 * degree - 1) * points * legendre[:, degree - 1]
            - (degree - 1) * legendre[:, degree - 2]
        ) / degree
    values = legendre[:, order]
    identity = np.eye(count)
    spread = points[:, None] - points[None, :] + identity
    table = values[:, None] / values[None, :] / spread
    table = table * (1.0 - identity)
    table[0, 0] = -order * count / 4.0
    table[order, order] = order * count / 4.0
    return table.astype(np.float32)


TABLE = derivative_table(N - 1)
SQUARED = TABLE * TABLE
ALONG = [float(v) for v in np.diagonal(TABLE)]


def row_of(i, j, k):
    return (i * N + j) * N + k


EDGE_ROWS = (
    [(row_of(0, a, b), N * N) for a in (0, 7) for b in (0, 7)]
    + [(row_of(a, 0, b), N) for a in (0, 7) for b in (0, 7)]
    + [(row_of(a, b, 0), 1) for a in (0, 7) for b in (0, 7)]
)
CORNER_ROWS = [row_of(a, b, c) for a in (0, 7) for b in (0, 7) for c in (0, 7)]


def split3(x):
    hi = x.astype(bf16)
    rest = x - hi.astype(f32)
    mid = rest.astype(bf16)
    low = (rest - mid.astype(f32)).astype(bf16)
    return hi, mid, low


def stack3(x):
    return jnp.concatenate(split3(x), axis=0)


def sum3(x):
    m = x.shape[0] // 3
    return x[0:m] + x[m : 2 * m] + x[2 * m : 3 * m]


def dot_nn(a, b):
    return lax.dot_general(a, b, (((1,), (0,)), ((), ())), preferred_element_type=f32)


def dot_nt(a, b):
    return lax.dot_general(a, b, (((1,), (1,)), ((), ())), preferred_element_type=f32)


def small_row(key, count):
    ok = (key >= 0) & (key < count)
    return jnp.where(ok, key, -1).astype(f32).astype(bf16)


def iota_rows(count, lanes):
    return lax.broadcasted_iota(i32, (count, lanes), 0).astype(f32).astype(bf16)


def onehot(row, count):
    lanes = row.shape[1]
    io = iota_rows(count, 128)
    one, zero = jnp.ones((count, 128), bf16), jnp.zeros((count, 128), bf16)
    cols = [
        jnp.where(io == jnp.broadcast_to(row[:, g : g + 128], (count, 128)), one, zero)
        for g in range(0, lanes, 128)
    ]
    return cols[0] if len(cols) == 1 else jnp.concatenate(cols, axis=1)


def prefix_matrix():
    a = lax.broadcasted_iota(i32, (E, E), 0)
    b = lax.broadcasted_iota(i32, (E, E), 1)
    return jnp.where(a <= b, 1.0, 0.0).astype(bf16)


def ranks(mask, tri):
    m = mask.shape[0]
    flags = jnp.where(mask, 1.0, 0.0)
    within = dot_nn(flags.astype(bf16), tri) - 1.0
    if m > 1:
        before = jnp.zeros((1, 1), f32)
        offs = [before]
        for r in range(m - 1):
            before = before + jnp.sum(flags[r : r + 1], axis=1, keepdims=True)
            offs.append(before)
        within = within + jnp.concatenate(offs, axis=0)
    return within.astype(i32)


def move_rows(owner, devs, tri):
    own = devs[0]
    departed = owner != own
    leave = jnp.full((1, E), -1, i32)
    arrive = jnp.full((1, E), -1, i32)
    flags = [departed] + [departed & (owner == devs[d]) for d in range(1, 5)]
    stacked = jnp.concatenate([jnp.where(f, 1.0, 0.0) for f in flags] + [jnp.zeros((3, E), f32)], axis=0)
    pre = dot_nn(stacked.astype(bf16), tri)
    hole = pre[0:1] - 1.0
    start = jnp.zeros((1, 1), f32)
    for d in range(4):
        chosen = flags[d + 1]
        rank = pre[d + 1 : d + 2] - 1.0
        leave = jnp.where(chosen, d * MOVE + rank.astype(i32), leave)
        count = pre[d + 1 : d + 2, E - 1 : E]
        pos = hole - start
        inside = departed & (pos >= 0.0) & (pos < count)
        arrive = jnp.where(inside, d * MOVE + pos.astype(i32), arrive)
        start = start + count
    return departed, leave, arrive


def swapped(col):
    return jnp.where(col >= 0, col ^ MOVE, -1)


def lane_low(rows):
    return lax.broadcasted_iota(i32, (rows, 128), 1) < MOVE


def pack_block(x, pa, pb):
    half = NODES // 2
    ya = sum3(dot_nt(stack3(x[0:half]), pa))
    yb = sum3(dot_nt(stack3(x[half:]), pb))
    low = lane_low(half)
    out = []
    for g in (0, 128):
        a, b = ya[:, g : g + 128], yb[:, g : g + 128]
        out.append(jnp.where(low, a, b))
        out.append(jnp.where(low, b, a))
    return out


def land_block(x, got, pa, pb, departed):
    half = NODES // 2
    low = lane_low(half)
    zl, zh = [], []
    for g in (0, 2):
        zl.append(jnp.where(low, got[g + 1], got[g]))
        zh.append(jnp.where(low, got[g], got[g + 1]))
    zl = jnp.concatenate(zl, axis=1)
    zh = jnp.concatenate(zh, axis=1)
    yl = sum3(dot_nn(stack3(zl), pb))
    yh = sum3(dot_nn(stack3(zh), pa))
    keep = jnp.logical_not(departed)
    return jnp.where(keep, x[0:half], yl), jnp.where(keep, x[half:], yh)


def contract_i(src, table, put):
    for j in range(N):
        xs = [src(i, j) for i in range(N)]
        for a in range(N):
            put(a, j, sum(float(table[a, i]) * xs[i] for i in range(N) if table[a, i] != 0.0))


def contract_j(src, table, put):
    for i in range(N):
        xs = [src(i, j) for j in range(N)]
        for b in range(N):
            put(i, b, sum(float(table[b, j]) * xs[j] for j in range(N) if table[b, j] != 0.0))


def key_rows(ids, block, devs, dom_base, both_base, sub_base, tri):
    rel, inside = [], []
    for d in (0, 2, 4, 5):
        r = ids - devs[d] * block
        rel.append(r)
        inside.append((r >= 0) & (r < block))
    key = jnp.where(inside[0], rel[0], -1)
    key = jnp.where(inside[1], dom_base + ranks(inside[1], tri), key)
    key = jnp.where(inside[2], sub_base + ranks(inside[2], tri), key)
    if both_base is not None:
        key = jnp.where(inside[3], both_base + ranks(inside[3], tri), key)
    row = jnp.where(inside[0], rel[0], jnp.where(inside[1], rel[1], jnp.where(inside[2], rel[2], rel[3])))
    return key, row.astype(f32)


def tile(ref, r):
    return ref[pl.ds(r * N, N), :]


def make_keys(ids, devs, key_out, rix, tri):
    k, r = key_rows(ids[0:6], F_BLOCK, devs, 1536, None, 1664, tri)
    key_out[0:6, :] = k
    rix[0:6, :] = r
    k, r = key_rows(ids[6:18], E_BLOCK, devs, 1536, 2016, 2048, tri)
    key_out[6:18, :] = k
    rix[6:18, :] = r
    k, r = key_rows(ids[18:26], C_BLOCK, devs, 512, 960, 1024, tri)
    key_out[18:26, :] = k
    rix[18:26, :] = r


def apply_chunk(c, sol_all, met_all, kmat, im_all, dg_all, rix, vf, ve, vc, ga, gb, gc):
    lanes = pl.ds(pl.multiple_of(c * 128, 128), 128)
    sol = sol_all.at[:, :, :, lanes]
    met = met_all.at[:, :, :, :, lanes]
    im, dg = im_all.at[c], dg_all.at[c]
    fwd, bwd = kmat.at[0], kmat.at[1]
    half = NODES // 2

    def kdot(m, x):
        return lax.dot_general(
            m, x, (((1,), (0,)), ((), ())),
            precision=lax.Precision.HIGHEST, preferred_element_type=f32,
        )

    def put_a(i, j, v):
        ga[pl.ds((i * N + j) * N, N), :] = v

    def put_b(i, j, v):
        gb[pl.ds((i * N + j) * N, N), :] = v

    contract_i(lambda i, j: sol[i, j], TABLE, put_a)
    contract_j(lambda i, j: sol[i, j], TABLE, put_b)
    for h in range(2):
        x = sol[h * 4 : h * 4 + 4].reshape(half, 128)
        gc[h * half : (h + 1) * half, :] = kdot(fwd[...], x)

    for i in range(N):
        for j in range(N):
            r = i * N + j
            a, b, t = tile(ga, r), tile(gb, r), tile(gc, r)
            m3, m4, m5 = met[3, i, j], met[4, i, j], met[5, i, j]
            ga[pl.ds(r * N, N), :] = met[0, i, j] * a + m3 * b + m4 * t
            gb[pl.ds(r * N, N), :] = m3 * a + met[1, i, j] * b + m5 * t
            gc[pl.ds(r * N, N), :] = m4 * a + m5 * b + met[2, i, j] * t

    for h in range(2):
        im[h * half : (h + 1) * half, :] = kdot(bwd[...], gc[h * half : (h + 1) * half, :])

    def add_im(i, j, v):
        im[pl.ds((i * N + j) * N, N), :] += v

    contract_i(lambda i, j: tile(ga, i * N + j), TABLE.T, add_im)

    def add_im_last(i, j, v):
        im[pl.ds((i * N + j) * N, N), :] += v + met[6, i, j] * sol[i, j]

    contract_j(lambda i, j: tile(gb, i * N + j), TABLE.T, add_im_last)

    sq = kmat.at[2]
    for h in range(2):
        x = met[2, h * 4 : h * 4 + 4].reshape(half, 128)
        dg[h * half : (h + 1) * half, :] = kdot(sq[...], x)

    def add_dg(i, j, v):
        dg[pl.ds((i * N + j) * N, N), :] += v

    contract_i(lambda i, j: met[0, i, j], SQUARED.T, add_dg)
    kk = lax.broadcasted_iota(i32, (N, 128), 0)
    dk = jnp.where(kk == 0, ALONG[0], jnp.where(kk == N - 1, ALONG[N - 1], 0.0))

    def add_dg_last(i, j, v):
        v = v + met[6, i, j]
        if ALONG[i] * ALONG[j] != 0.0:
            v = v + (2.0 * ALONG[i] * ALONG[j]) * met[3, i, j]
        if ALONG[i] != 0.0:
            v = v + (2.0 * ALONG[i]) * dk * met[4, i, j]
        if ALONG[j] != 0.0:
            v = v + (2.0 * ALONG[j]) * dk * met[5, i, j]
        dg[pl.ds((i * N + j) * N, N), :] += v

    contract_j(lambda i, j: met[1, i, j], SQUARED.T, add_dg_last)

    def face(ref, f):
        if f < 2:
            base = 0 if f == 0 else 448
            return ref[base : base + 64, :]
        if f < 4:
            j = 0 if f == 2 else 7
            return jnp.concatenate([ref[pl.ds((i * N + j) * N, N), :] for i in range(N)], axis=0)
        return ref[pl.ds(0 if f == 4 else 7, 64, stride=N), :]

    top = lax.broadcasted_iota(i32, (N, 128), 0) == 0
    for f in range(6):
        at = pl.ds(pl.multiple_of(f * E + c * 128, 128), 128)
        a, b = face(im, f), face(dg, f)
        mark = jnp.broadcast_to(rix[f : f + 1, lanes], (N, 128))
        a = jnp.concatenate([jnp.where(top, mark, a[0:N]), a[N:]], axis=0)
        for s, (p, q) in enumerate(zip(split3(a), split3(b))):
            vf[s * 128 : s * 128 + 64, at] = p
            vf[s * 128 + 64 : s * 128 + 128, at] = q
    for e in range(12):
        at = pl.ds(pl.multiple_of(e * E + c * 128, 128), 128)
        start, stride = EDGE_ROWS[e]
        rows = pl.ds(start, N) if stride == 1 else pl.ds(start, N, stride=stride)
        a, b = im[rows, :], dg[rows, :]
        mark = jnp.broadcast_to(rix[6 + e : 7 + e, lanes], (N, 128))
        x = jnp.concatenate([jnp.where(top, mark, a), b], axis=0)
        for s, p in enumerate(split3(x)):
            ve[s * 16 : s * 16 + 16, at] = p
    for q in range(8):
        at = pl.ds(pl.multiple_of(q * E + c * 128, 128), 128)
        r = CORNER_ROWS[q]
        vc[0:1, at] = im[r : r + 1, :]
        vc[1:2, at] = dg[r : r + 1, :]
        vc[2:3, at] = rix[18 + q : 19 + q, lanes]
        vc[3:8, at] = jnp.zeros((5, 128), f32)


def scatter_shared(key_out, tf, te, tc, md, ms, vf, ve, vc, of, le, ol, acc_e):
    def face_block(n, carry):
        for f in range(6):
            of[:, f * E : (f + 1) * E] = onehot(small_row(key_out[f : f + 1, :] - n * 256, 256), 256)
        acc = dot_nt(vf[...], of[...])
        tf[:, pl.ds(pl.multiple_of(n * 256, 256), 256)] = sum3(acc)
        return carry

    lax.fori_loop(0, F_KEYS // 256, face_block, 0)

    for e in range(12):
        at = slice(e * E, (e + 1) * E)
        key = key_out[6 + e : 7 + e, :]
        hi = small_row(key >> 8, E_HI)
        ol[:, at] = onehot(small_row(key & 255, 256), 256)
        for g in range(4):
            ag = slice(e * E + g * 128, e * E + (g + 1) * 128)
            hb = jnp.broadcast_to(hi[:, g * 128 : (g + 1) * 128], (16, 128))
            zero = jnp.zeros((16, 128), bf16)
            parts = [ve[s * 16 : s * 16 + 16, ag] for s in range(3)]
            for h in range(E_HI):
                m = hb == jnp.full((16, 128), float(h), bf16)
                for s in range(3):
                    le[(s * E_HI + h) * 16 : (s * E_HI + h + 1) * 16, ag] = jnp.where(m, parts[s], zero)
    acc_e[...] = dot_nt(le[...], ol[...])
    for h in range(E_HI):
        te[h] = sum(acc_e[(s * E_HI + h) * 16 : (s * E_HI + h + 1) * 16, :] for s in range(3))

    full = E * 8
    for q in range(8):
        at = slice(q * E, (q + 1) * E)
        ol[:, at] = onehot(small_row(key_out[18 + q : 19 + q, :] & 255, 256), 256)
    hi = jnp.concatenate([key_out[18 + q : 19 + q, :] >> 8 for q in range(8)], axis=1)
    x = vc[...]
    big = jnp.concatenate(
        [jnp.where(jnp.broadcast_to(hi, (8, full)) == h, x, 0.0) for h in range(C_HI)], axis=0
    )
    acc = sum3(dot_nt(stack3(big), ol[:, 0:full]))
    for h in range(C_HI):
        tc[h] = acc[h * 8 : (h + 1) * 8]

    md[0:128, :] = tf[:, 1536:1664]
    ms[0:128, :] = tf[:, 1664:1792]
    for g in range(4):
        er, cr = msg_rows(g)
        half_lanes = slice((g % 2) * 128, (g % 2) * 128 + 128)
        md[er : er + 16, :] = te[6 + g // 2, :, half_lanes]
        ms[er : er + 16, :] = te[8 + g // 2, :, half_lanes]
        md[cr : cr + 8, :] = tc[2 + g // 2, :, half_lanes]
        ms[cr : cr + 8, :] = tc[4 + g // 2, :, half_lanes]


def msg_rows(g):
    if g < 3:
        return 128 + 16 * g, 176 + 8 * g
    return 200, 216


def owner_sums(tf, te, tc, gd, gs, gboth, tf2, te2, tc2, rd, rs, rb):
    vals = jnp.concatenate([gd[0:128, :], gs[0:128, :]], axis=1)
    key = vals[0:1, :].astype(i32)
    vs = stack3(vals)
    ret = jnp.zeros((384, 256), f32)
    for n in range(F_BLOCK // 256):
        o = onehot(small_row(key - n * 256, 256), 256)
        total = tf[:, n * 256 : (n + 1) * 256] + sum3(dot_nt(vs, o))
        tf2[:, n * 256 : (n + 1) * 256] = total
        ret = ret + dot_nn(stack3(total), o)
    ret = sum3(ret)
    rd[0:128, :] = ret[:, 0:128]
    rs[0:128, :] = ret[:, 128:256]

    lane = lax.broadcasted_iota(i32, (1, 128), 1)

    def lines(rows, id_row, total_ref, total_out, his, cut, at):
        vals, keys = [], []
        for src in (gd, gs):
            for g in range(4):
                r = msg_rows(g)[at]
                v = src[r : r + rows, :]
                k = v[id_row : id_row + 1].astype(i32)
                if src is gd and g == 3:
                    k = jnp.where(lane >= cut, -1, k)
                vals.append(v)
                keys.append(k)
        r = msg_rows(3)[at] - (MSG - BOTH)
        v = gboth[r : r + rows, :]
        keys.append(jnp.where(lane < cut, -1, v[id_row : id_row + 1].astype(i32)))
        vals.append(v)
        x = jnp.concatenate(vals, axis=1)
        key = jnp.concatenate(keys, axis=1)
        hi = key >> 8
        o = onehot(small_row(key & 255, 256), 256)
        big = jnp.concatenate([jnp.where(jnp.broadcast_to(hi, x.shape) == h, x, 0.0) for h in range(his)], axis=0)
        acc = sum3(dot_nt(stack3(big), o))
        totals = jnp.concatenate([total_ref[h] for h in range(his)], axis=0) + acc
        for h in range(his):
            total_out[h] = totals[h * rows : (h + 1) * rows]
        y = sum3(dot_nn(stack3(totals), o))
        back = jnp.zeros_like(x)
        for h in range(his):
            back = jnp.where(jnp.broadcast_to(hi, x.shape) == h, y[h * rows : (h + 1) * rows], back)
        for n, dst in enumerate((rd, rs)):
            for g in range(4):
                p = msg_rows(g)[at]
                dst[p : p + rows, :] = back[:, (n * 4 + g) * 128 : (n * 4 + g + 1) * 128]
        rb[r : r + rows, :] = back[:, 1024:1152]

    lines(16, 0, te, te2, E_BLOCK // 256, 96, 0)
    lines(8, 2, tc, tc2, C_BLOCK // 256, 64, 1)


def gather_shared(keys, tf, te, tc, rd, rs, rb, tfs, of, gf, ge, gc):
    for s, p in enumerate(split3(tf[...])):
        tfs[s * 128 : (s + 1) * 128, 0:1536] = p
    for s, p in enumerate(split3(rd[0:128, :])):
        tfs[s * 128 : (s + 1) * 128, 1536:1664] = p
    for s, p in enumerate(split3(rs[0:128, :])):
        tfs[s * 128 : (s + 1) * 128, 1664:1792] = p

    def face_gather(f, carry):
        key = keys[pl.ds(f, 1), :]
        for n in range(F_KEYS // 256):
            of[n * 256 : (n + 1) * 256, :] = onehot(small_row(key - n * 256, 256), 256)
        gf[f] = sum3(dot_nn(tfs[...], of[...]))
        return carry

    lax.fori_loop(0, 6, face_gather, 0)

    lane = lax.broadcasted_iota(i32, (1, 128), 1)

    def table(own, his, rows, at, cut):
        blocks = [own[h] for h in range(his)]
        for src in (rd, rs):
            for g in (0, 2):
                pair = []
                for q in (g, g + 1):
                    r = msg_rows(q)[at]
                    v = src[r : r + rows, :]
                    if src is rd and q == 3:
                        b = r - (MSG - BOTH)
                        v = jnp.where(jnp.broadcast_to(lane, (rows, 128)) >= cut, rb[b : b + rows, :], v)
                    pair.append(v)
                blocks.append(jnp.concatenate(pair, axis=1))
        return stack3(jnp.concatenate(blocks, axis=0))

    def line_gather(tab, first, count, his, rows, dst):
        def one(q, carry):
            key = keys[pl.ds(first + q, 1), :]
            hi = key >> 8
            y = sum3(dot_nn(tab, onehot(small_row(key & 255, 256), 256)))
            back = jnp.zeros((rows, E), f32)
            for h in range(his):
                back = jnp.where(jnp.broadcast_to(hi, (rows, E)) == h, y[h * rows : (h + 1) * rows], back)
            dst[q] = back
            return carry

        lax.fori_loop(0, count, one, 0)

    line_gather(table(te, 6, 16, 0, 96), 6, 12, E_HI, 16, ge)
    line_gather(table(tc, 2, 8, 1, 64), 18, 8, C_HI, 8, gc)

def place_relax(im, dg, gf, ge, gc, sol, forc, rel):
    for c in range(4):
        at = slice(c * 128, (c + 1) * 128)
        for ref, base in ((im.at[c], 0), (dg.at[c], 1)):
            for f in range(6):
                v = gf[f, base * 64 : base * 64 + 64, at]
                if f < 2:
                    start = 0 if f == 0 else 448
                    ref[start : start + 64, :] = v
                elif f < 4:
                    j = 0 if f == 2 else 7
                    for i in range(N):
                        ref[pl.ds((i * N + j) * N, N), :] = v[i * N : (i + 1) * N]
                else:
                    ref[pl.ds(0 if f == 4 else 7, 64, stride=N), :] = v
            for e in range(12):
                start, stride = EDGE_ROWS[e]
                rows = pl.ds(start, N) if stride == 1 else pl.ds(start, N, stride=stride)
                ref[rows, :] = ge[e, base * 8 : base * 8 + 8, at]
            for q in range(8):
                r = CORNER_ROWS[q]
                ref[r : r + 1, :] = gc[q, base : base + 1, at]
        s = sol[:, :, :, at].reshape(NODES, 128)
        v = s + RELAX * (forc[:, :, :, at].reshape(NODES, 128) - im[c]) / dg[c]
        rel[:, at] = v

MESH = pl.DeviceIdType.MESH


def main_kernel(
    owner, ids, kmat_in, sol_in, forc_in, met_in,
    out, a0, a1, a2, a3,
    met, sol, forc, kmat, im, dg, keys, rix, tf, te, tc, md, ms,
    gd, gs, gb, tf2, te2, tc2, sd, ss, sb, rd, rs, rb,
    vf, ve, vc, ga, gb2, gc2, of, le, ol, acc_e,
    tfs, og, gf, ge, gc, rel, p0, p1, p2, p3, pa, pb,
    load_sem, msg_send, msg_recv, move_send, move_recv,
):
    na, nb = lax.axis_size("dom"), lax.axis_size("sub")
    d, s = lax.axis_index("dom"), lax.axis_index("sub")
    dn, dp = lax.rem(d + 1, na), lax.rem(d + na - 1, na)
    sn, sp = lax.rem(s + 1, nb), lax.rem(s + nb - 1, nb)
    prev_dom, next_dom, prev_sub, next_sub = (dp, s), (dn, s), (d, sp), (d, sn)
    prev_both, next_both = (dp, sp), (dn, sn)
    loads = [pltpu.make_async_copy(met_in.at[m], met.at[m], load_sem.at[m]) for m in range(7)]
    loads.append(pltpu.make_async_copy(sol_in, sol, load_sem.at[7]))
    loads.append(pltpu.make_async_copy(forc_in, forc, load_sem.at[8]))
    loads.append(pltpu.make_async_copy(kmat_in, kmat, load_sem.at[9]))
    for copy in loads:
        copy.start()

    barrier = pltpu.get_barrier_semaphore()
    for peer in (prev_dom, next_dom, prev_sub, next_sub, prev_both, next_both):
        pl.semaphore_signal(barrier, inc=1, device_id=peer, device_id_type=MESH)

    devs = [x * nb + y for x, y in ((d, s), prev_dom, next_dom, prev_sub, next_sub, next_both)]
    tri = prefix_matrix()
    make_keys(ids, devs, keys, rix, tri)
    _, leave, _ = move_rows(owner[...], devs, tri)
    pa[...] = onehot(small_row(leave, 256), 256)
    pb[...] = onehot(small_row(swapped(leave), 256), 256)
    pl.semaphore_wait(barrier, 6)

    def remote(src, dst, send_sem, recv_sem, peer):
        copy = pltpu.make_async_remote_copy(
            src_ref=src, dst_ref=dst, send_sem=send_sem, recv_sem=recv_sem,
            device_id=peer, device_id_type=MESH,
        )
        copy.start()
        return copy

    half = NODES // 2
    moves = []

    def move(m, x):
        for ref, val in zip((p0, p1, p2, p3), pack_block(x, pa[...], pb[...])):
            ref[m] = val
        for n, (src, dst, peer) in enumerate(
            ((p2, a3, prev_sub), (p3, a2, next_sub), (p0, a1, prev_dom), (p1, a0, next_dom))
        ):
            moves.append(remote(src.at[m], dst.at[m], move_send.at[m, n], move_recv.at[m, n], peer))

    for m in range(7):
        loads[m].wait()
        move(m, met[m].reshape(NODES, E))

    loads[7].wait()
    loads[9].wait()

    def chunk(c, carry):
        apply_chunk(c, sol, met, kmat, im, dg, rix, vf, ve, vc, ga, gb2, gc2)
        return carry

    lax.fori_loop(0, 4, chunk, 0)
    scatter_shared(keys, tf, te, tc, md, ms, vf, ve, vc, of, le, ol, acc_e)

    def send(n, src, dst, peer):
        return remote(src, dst, msg_send.at[n], msg_recv.at[n], peer)

    first = [
        send(0, ms, gs, next_sub),
        send(1, md, gd, next_dom),
        send(2, md.at[pl.ds(MSG - BOTH, BOTH)], gb, next_both),
    ]
    for copy in first:
        copy.wait()
    owner_sums(tf, te, tc, gd, gs, gb, tf2, te2, tc2, sd, ss, sb)
    second = [
        send(3, ss, rs, prev_sub),
        send(4, sd, rd, prev_dom),
        send(5, sb, rb, prev_both),
    ]
    for copy in second:
        copy.wait()
    gather_shared(keys, tf2, te2, tc2, rd, rs, rb, tfs, og, gf, ge, gc)
    loads[8].wait()
    place_relax(im, dg, gf, ge, gc, sol, forc, rel)
    move(7, rel[...])
    out[...] = rel[...].reshape(N, N, N, E)
    for copy in moves:
        copy.wait()


def main_call(owner, ids, solution, forcing, metric):
    half = NODES // 2
    eye = np.eye(half // N, dtype=np.float32)
    kmat = np.stack([np.kron(eye, TABLE), np.kron(eye, TABLE.T), np.kron(eye, SQUARED.T)])
    vm = pl.BlockSpec(memory_space=pltpu.VMEM)
    hbm = pl.BlockSpec(memory_space=pl.ANY)
    box = pltpu.VMEM((N, N, N, E), f32)
    planes = pltpu.VMEM((4, NODES, 128), f32)
    msg, both = pltpu.VMEM((MSG, 128), f32), pltpu.VMEM((BOTH, 128), f32)
    work = pltpu.VMEM((NODES, 128), f32)
    moved = pltpu.VMEM((8, half, 128), f32)
    return pl.pallas_call(
        main_kernel,
        in_specs=[vm] * 2 + [hbm] * 4,
        out_specs=[vm] * 5,
        out_shape=[jax.ShapeDtypeStruct((N, N, N, E), f32)] + [jax.ShapeDtypeStruct((8, half, 128), f32)] * 4,
        scratch_shapes=[
            pltpu.VMEM((7, N, N, N, E), f32), box, box,
            pltpu.VMEM((3, 256, 256), f32), planes, planes,
            pltpu.VMEM((26, E), i32),
            pltpu.VMEM((26, E), f32),
            pltpu.VMEM((128, F_KEYS), f32),
            pltpu.VMEM((E_HI, 16, 256), f32),
            pltpu.VMEM((C_HI, 8, 256), f32),
            msg, msg,
            msg, msg, both,
            pltpu.VMEM((128, F_BLOCK), f32),
            pltpu.VMEM((E_BLOCK // 256, 16, 256), f32),
            pltpu.VMEM((C_BLOCK // 256, 8, 256), f32),
            msg, msg, both, msg, msg, both,
            pltpu.VMEM((384, 6 * E), bf16),
            pltpu.VMEM((48, 12 * E), bf16),
            pltpu.VMEM((8, 8 * E), f32),
            work, work, work,
            pltpu.VMEM((256, 6 * E), bf16),
            pltpu.VMEM((3 * E_HI * 16, 12 * E), bf16),
            pltpu.VMEM((256, 12 * E), bf16),
            pltpu.VMEM((3 * E_HI * 16, 256), f32),
            pltpu.VMEM((384, F_KEYS), bf16),
            pltpu.VMEM((F_KEYS, E), bf16),
            pltpu.VMEM((6, 128, E), f32),
            pltpu.VMEM((12, 16, E), f32),
            pltpu.VMEM((8, 8, E), f32),
            pltpu.VMEM((NODES, E), f32),
            moved, moved, moved, moved,
            pltpu.VMEM((256, E), bf16),
            pltpu.VMEM((256, E), bf16),
            pltpu.SemaphoreType.DMA((10,)),
            pltpu.SemaphoreType.DMA((6,)),
            pltpu.SemaphoreType.DMA((6,)),
            pltpu.SemaphoreType.DMA((8, 4)),
            pltpu.SemaphoreType.DMA((8, 4)),
        ],
        compiler_params=pltpu.CompilerParams(
            vmem_limit_bytes=48 << 20, collective_id=0, has_side_effects=True
        ),
        interpret=pltpu.InterpretParams() if INTERPRET else False,
        name="main",
    )(owner, ids, kmat, solution, forcing, metric)


def land_kernel(devs, owner_ref, met_in, rel_in, a0, a1, a2, a3, met_out, rel_out, y, out_sem):
    order = list(range(8))
    departed, _, arrive = move_rows(owner_ref[...], [devs[d] for d in range(5)], prefix_matrix())
    pa = onehot(small_row(arrive, 256), 256)
    pb = onehot(small_row(swapped(arrive), 256), 256)
    stores = []
    for m in order:
        x = (rel_in if m == 7 else met_in.at[m])[...].reshape(NODES, E)
        lo, hi = land_block(x, [a[m] for a in (a0, a1, a2, a3)], pa, pb, departed)
        y[m, 0:4] = lo.reshape(4, N, N, E)
        y[m, 4:8] = hi.reshape(4, N, N, E)
        stores.append(pltpu.make_async_copy(y.at[m], met_out.at[m] if m < 7 else rel_out, out_sem.at[m]))
        stores[-1].start()
    for copy in stores:
        copy.wait()


def land(devs, owner, metric, relaxed, got):
    vm = pl.BlockSpec(memory_space=pltpu.VMEM)
    hbm = pl.BlockSpec(memory_space=pltpu.HBM)
    return pl.pallas_call(
        land_kernel,
        in_specs=[pl.BlockSpec(memory_space=pltpu.SMEM)] + [vm] * 7,
        out_specs=[hbm] * 2,
        out_shape=[jax.ShapeDtypeStruct(metric.shape, f32), jax.ShapeDtypeStruct(relaxed.shape, f32)],
        scratch_shapes=[
            pltpu.VMEM((8, N, N, N, E), f32),
            pltpu.SemaphoreType.DMA((8,)),
        ],
        compiler_params=pltpu.CompilerParams(vmem_limit_bytes=14 << 20),
        interpret=INTERPRET,
        name="land",
    )(devs, owner, metric, relaxed, *got)


def on_device(solution, forcing, metric, entity_ids, new_owner):
    a, b = lax.axis_size("dom"), lax.axis_size("sub")
    d, s = lax.axis_index("dom"), lax.axis_index("sub")
    da, db = (d + 1) % a, (d + a - 1) % a
    sa, sb = (s + 1) % b, (s + b - 1) % b
    devs = jnp.stack([d * b + s, db * b + s, da * b + s, d * b + sb, d * b + sa, da * b + sa]).astype(i32)
    owner = new_owner.reshape(1, E)

    relaxed, *got = main_call(owner, entity_ids, solution, forcing, metric)
    moved_metric, smoothed = land(devs, owner, metric, relaxed, got)
    return smoothed, moved_metric


def solution(mesh):
    cols = ("dom", "sub")
    placed = (
        P(None, None, None, cols),
        P(None, None, None, cols),
        P(None, None, None, None, cols),
        P(None, cols),
        P(cols),
    )
    return jax.shard_map(
        on_device,
        mesh=mesh,
        in_specs=placed,
        out_specs=(P(None, None, None, cols), P(None, None, None, None, cols)),
        check_vma=False,
    )
```

```python
import functools

import jax
import jax.numpy as jnp
import numpy as np
from jax import lax
from jax.experimental import pallas as pl
from jax.experimental.pallas import tpu as pltpu
from jax.sharding import PartitionSpec as P

N = 8
E = 512
NODES = N * N * N
EX = 4
EY = 4
EZ = 32
MOVE = 64
RELAX = 0.6
F_BLOCK, E_BLOCK, C_BLOCK = 3 * E, 3 * E, E
F_KEYS, E_KEYS, C_KEYS = 1792, 2560, 1536
E_HI, C_HI = E_KEYS // 256, C_KEYS // 256
PLANE = 48
F_ROWS = 2 * PLANE
LINES = 96
BOTH = 24
INTERPRET = False

f32, bf16, i32 = jnp.float32, jnp.bfloat16, jnp.int32


def derivative_table(order):
    count = order + 1
    points = -np.cos(np.pi * np.arange(count) / order)
    legendre = np.zeros((count, count))
    for sweep in range(80):
        legendre[:, 0] = 1.0
        legendre[:, 1] = points
        for degree in range(2, count):
            legendre[:, degree] = (
                (2 * degree - 1) * points * legendre[:, degree - 1]
                - (degree - 1) * legendre[:, degree - 2]
            ) / degree
        points = points - (points * legendre[:, order] - legendre[:, order - 1]) / (
            count * legendre[:, order]
        )
    legendre[:, 0] = 1.0
    legendre[:, 1] = points
    for degree in range(2, count):
        legendre[:, degree] = (
            (2 * degree - 1) * points * legendre[:, degree - 1]
            - (degree - 1) * legendre[:, degree - 2]
        ) / degree
    values = legendre[:, order]
    identity = np.eye(count)
    spread = points[:, None] - points[None, :] + identity
    table = values[:, None] / values[None, :] / spread
    table = table * (1.0 - identity)
    table[0, 0] = -order * count / 4.0
    table[order, order] = order * count / 4.0
    return table.astype(np.float32)


TABLE = derivative_table(N - 1)
SQUARED = TABLE * TABLE
ALONG = [float(v) for v in np.diagonal(TABLE)]


def row_of(i, j, k):
    return (i * N + j) * N + k


EDGE_ROWS = (
    [(row_of(0, a, b), N * N) for a in (0, 7) for b in (0, 7)]
    + [(row_of(a, 0, b), N) for a in (0, 7) for b in (0, 7)]
    + [(row_of(a, b, 0), 1) for a in (0, 7) for b in (0, 7)]
)
CORNER_ROWS = [row_of(a, b, c) for a in (0, 7) for b in (0, 7) for c in (0, 7)]


def split2(x):
    hi = x.astype(bf16)
    return hi, (x - hi.astype(f32)).astype(bf16)


def stack2(x):
    return jnp.concatenate(split2(x), axis=0)


def sum2(x):
    m = x.shape[0] // 2
    return x[0:m] + x[m:]


def dot_nn(a, b):
    return lax.dot_general(a, b, (((1,), (0,)), ((), ())), preferred_element_type=f32)


def dot_nt(a, b):
    return lax.dot_general(a, b, (((1,), (1,)), ((), ())), preferred_element_type=f32)


def small_row(key, count):
    ok = (key >= 0) & (key < count)
    return jnp.where(ok, key, -1).astype(f32).astype(bf16)


def iota_rows(count, lanes):
    return lax.broadcasted_iota(i32, (count, lanes), 0).astype(f32).astype(bf16)


def onehot(row, count):
    lanes = row.shape[1]
    io = iota_rows(count, 128)
    one, zero = jnp.ones((count, 128), bf16), jnp.zeros((count, 128), bf16)
    cols = [
        jnp.where(io == jnp.broadcast_to(row[:, g : g + 128], (count, 128)), one, zero)
        for g in range(0, lanes, 128)
    ]
    return cols[0] if len(cols) == 1 else jnp.concatenate(cols, axis=1)


def prefix_matrix():
    a = lax.broadcasted_iota(i32, (E, E), 0)
    b = lax.broadcasted_iota(i32, (E, E), 1)
    return jnp.where(a <= b, 1.0, 0.0).astype(bf16)


def ranks(mask, tri):
    m = mask.shape[0]
    flags = jnp.where(mask, 1.0, 0.0)
    within = dot_nn(flags.astype(bf16), tri) - 1.0
    if m > 1:
        before = jnp.zeros((1, 1), f32)
        offs = [before]
        for r in range(m - 1):
            before = before + jnp.sum(flags[r : r + 1], axis=1, keepdims=True)
            offs.append(before)
        within = within + jnp.concatenate(offs, axis=0)
    return within.astype(i32)


def move_rows(owner, devs, tri):
    own = devs[0]
    departed = owner != own
    leave = jnp.full((1, E), -1, i32)
    arrive = jnp.full((1, E), -1, i32)
    flags = [departed] + [departed & (owner == devs[d]) for d in range(1, 5)]
    stacked = jnp.concatenate([jnp.where(f, 1.0, 0.0) for f in flags] + [jnp.zeros((3, E), f32)], axis=0)
    pre = dot_nn(stacked.astype(bf16), tri)
    hole = pre[0:1] - 1.0
    start = jnp.zeros((1, 1), f32)
    for d in range(4):
        chosen = flags[d + 1]
        rank = pre[d + 1 : d + 2] - 1.0
        leave = jnp.where(chosen, d * MOVE + rank.astype(i32), leave)
        count = pre[d + 1 : d + 2, E - 1 : E]
        pos = hole - start
        inside = departed & (pos >= 0.0) & (pos < count)
        arrive = jnp.where(inside, d * MOVE + pos.astype(i32), arrive)
        start = start + count
    return departed, leave, arrive


def swapped(col):
    return jnp.where(col >= 0, col ^ MOVE, -1)


def lane_low(rows):
    return lax.broadcasted_iota(i32, (rows, 128), 1) < MOVE


def pack_block(x, pa, pb):
    half = NODES // 2
    ya = sum2(dot_nt(stack2(x[0:half]), pa))
    yb = sum2(dot_nt(stack2(x[half:]), pb))
    low = lane_low(half)
    out = []
    for g in (0, 128):
        a, b = ya[:, g : g + 128], yb[:, g : g + 128]
        out.append(jnp.where(low, a, b))
        out.append(jnp.where(low, b, a))
    return out


def land_block(x, got, pa, pb, departed, out):
    half = NODES // 2
    low = lane_low(half)
    zl, zh = [], []
    for g in (0, 2):
        zl.append(jnp.where(low, got[g + 1], got[g]))
        zh.append(jnp.where(low, got[g], got[g + 1]))
    keep = jnp.logical_not(departed)
    for at, z, p in ((slice(0, 4), zl, pb), (slice(4, 8), zh, pa)):
        y = sum2(dot_nn(stack2(jnp.concatenate(z, axis=1)), p))
        v = jnp.where(keep, x[at].reshape(half, E), y)
        out[at] = v.reshape(4, N, N, E)


def halves(table):
    t = table.astype(np.float64)
    return (t[:4, :4] + t[:4, :3:-1]) / 2, (t[:4, :4] - t[:4, :3:-1]) / 2


def combine(xs, table, odd):
    even_w, odd_w = halves(table)
    e = [xs[p] + xs[7 - p] for p in range(4)]
    o = [xs[p] - xs[7 - p] for p in range(4)]
    out = [None] * N
    for a in range(4):
        u = sum(float(even_w[a, p]) * e[p] for p in range(4))
        v = sum(float(odd_w[a, p]) * o[p] for p in range(4))
        out[a] = v + u
        out[7 - a] = v - u if odd else u - v
    return out


def contract_i(src, table, odd, put):
    for j in range(N):
        for a, v in enumerate(combine([src(i, j) for i in range(N)], table, odd)):
            put(a, j, v)


def contract_j(src, table, odd, put):
    for i in range(N):
        for b, v in enumerate(combine([src(i, j) for j in range(N)], table, odd)):
            put(i, b, v)


def key_rows(ids, block, devs, dom_base, both_base, sub_base, tri):
    rel, inside = [], []
    for d in (0, 2, 4, 5):
        r = ids - devs[d] * block
        rel.append(r)
        inside.append((r >= 0) & (r < block))
    key = jnp.where(inside[0], rel[0], -1)
    key = jnp.where(inside[1], dom_base + ranks(inside[1], tri), key)
    key = jnp.where(inside[2], sub_base + ranks(inside[2], tri), key)
    if both_base is not None:
        key = jnp.where(inside[3], both_base + ranks(inside[3], tri), key)
    row = jnp.where(inside[0], rel[0], jnp.where(inside[1], rel[1], jnp.where(inside[2], rel[2], rel[3])))
    return key, row.astype(f32)


def tile(ref, r):
    return ref[pl.ds(r * N, N), :]


def make_keys(ids, devs, key_out, rix, tri):
    k, r = key_rows(ids[0:6], F_BLOCK, devs, 1536, None, 1664, tri)
    key_out[0:6, :] = k
    rix[0:6, :] = r
    k, r = key_rows(ids[6:18], E_BLOCK, devs, 1536, 2016, 2048, tri)
    key_out[6:18, :] = k
    rix[6:18, :] = r
    k, r = key_rows(ids[18:26], C_BLOCK, devs, 512, 960, 1024, tri)
    key_out[18:26, :] = k
    rix[18:26, :] = r


def apply_chunk(c, sol_all, met_all, kmat, im_all, dg_all, rix, vf, ve, vc, ga, gb, gc):
    lanes = pl.ds(pl.multiple_of(c * 128, 128), 128)
    sol = sol_all.at[:, :, :, lanes]
    met = [m.at[:, :, :, lanes] for m in met_all]
    im, dg = im_all.at[c], dg_all.at[c]
    fwd, bwd = kmat.at[0], kmat.at[1]
    slab = N * N

    def kdot(m, x):
        return lax.dot_general(
            m, x, (((1,), (0,)), ((), ())),
            precision=lax.Precision.HIGHEST, preferred_element_type=f32,
        )

    def put_a(i, j, v):
        ga[pl.ds((i * N + j) * N, N), :] = v

    def put_b(i, j, v):
        gb[pl.ds((i * N + j) * N, N), :] = v

    contract_i(lambda i, j: sol[i, j], TABLE, True, put_a)
    contract_j(lambda i, j: sol[i, j], TABLE, True, put_b)
    for h in range(N):
        gc[h * slab : (h + 1) * slab, :] = kdot(fwd[...], sol[h].reshape(slab, 128))

    for i in range(N):
        for j in range(N):
            r = i * N + j
            a, b, t = tile(ga, r), tile(gb, r), tile(gc, r)
            m3, m4, m5 = met[3][i, j], met[4][i, j], met[5][i, j]
            ga[pl.ds(r * N, N), :] = met[0][i, j] * a + m3 * b + m4 * t
            gb[pl.ds(r * N, N), :] = m3 * a + met[1][i, j] * b + m5 * t
            gc[pl.ds(r * N, N), :] = m4 * a + m5 * b + met[2][i, j] * t

    for h in range(N):
        im[h * slab : (h + 1) * slab, :] = kdot(bwd[...], gc[h * slab : (h + 1) * slab, :])

    def add_im(i, j, v):
        im[pl.ds((i * N + j) * N, N), :] += v

    contract_i(lambda i, j: tile(ga, i * N + j), TABLE.T, True, add_im)

    def add_im_last(i, j, v):
        im[pl.ds((i * N + j) * N, N), :] += v + met[6][i, j] * sol[i, j]

    contract_j(lambda i, j: tile(gb, i * N + j), TABLE.T, True, add_im_last)

    sq = kmat.at[2]
    for h in range(N):
        dg[h * slab : (h + 1) * slab, :] = kdot(sq[...], met[2][h].reshape(slab, 128))

    def add_dg(i, j, v):
        dg[pl.ds((i * N + j) * N, N), :] += v

    contract_i(lambda i, j: met[0][i, j], SQUARED.T, False, add_dg)
    kk = lax.broadcasted_iota(i32, (N, 128), 0)
    dk = jnp.where(kk == 0, ALONG[0], jnp.where(kk == N - 1, ALONG[N - 1], 0.0))

    def add_dg_last(i, j, v):
        v = v + met[6][i, j]
        if ALONG[i] * ALONG[j] != 0.0:
            v = v + (2.0 * ALONG[i] * ALONG[j]) * met[3][i, j]
        if ALONG[i] != 0.0:
            v = v + (2.0 * ALONG[i]) * dk * met[4][i, j]
        if ALONG[j] != 0.0:
            v = v + (2.0 * ALONG[j]) * dk * met[5][i, j]
        dg[pl.ds((i * N + j) * N, N), :] += v

    contract_j(lambda i, j: met[1][i, j], SQUARED.T, False, add_dg_last)

    def face(ref, f):
        if f < 2:
            base = 8 if f == 0 else 456
            return ref[base : base + PLANE, :]
        if f < 4:
            j = 0 if f == 2 else 7
            return jnp.concatenate([ref[pl.ds((i * N + j) * N, N), :] for i in range(1, 7)], axis=0)
        return ref[pl.ds(64 if f == 4 else 71, PLANE, stride=N), :]

    top = lax.broadcasted_iota(i32, (N, 128), 0) == 0
    for f in range(6):
        at = pl.ds(pl.multiple_of(f * E + c * 128, 128), 128)
        a, b = face(im, f), face(dg, f)
        mark = jnp.broadcast_to(rix[f : f + 1, lanes], (N, 128))
        a = jnp.concatenate([jnp.where(top, mark, a[0:N]), a[N:]], axis=0)
        for s, (p, q) in enumerate(zip(split2(a), split2(b))):
            vf[s * F_ROWS : s * F_ROWS + PLANE, at] = p
            vf[s * F_ROWS + PLANE : (s + 1) * F_ROWS, at] = q
    for e in range(12):
        at = pl.ds(pl.multiple_of(e * E + c * 128, 128), 128)
        start, stride = EDGE_ROWS[e]
        rows = pl.ds(start, N) if stride == 1 else pl.ds(start, N, stride=stride)
        a, b = im[rows, :], dg[rows, :]
        mark = jnp.broadcast_to(rix[6 + e : 7 + e, lanes], (N, 128))
        x = jnp.concatenate([jnp.where(top, mark, a), b], axis=0)
        for s, p in enumerate(split2(x)):
            ve[s * 16 : s * 16 + 16, at] = p
    for q in range(8):
        at = pl.ds(pl.multiple_of(q * E + c * 128, 128), 128)
        r = CORNER_ROWS[q]
        vc[0:1, at] = im[r : r + 1, :]
        vc[1:2, at] = dg[r : r + 1, :]
        vc[2:3, at] = rix[18 + q : 19 + q, lanes]
        vc[3:8, at] = jnp.zeros((5, 128), f32)


def scatter_faces(key_out, tf, fd, fs, vf, of):
    def face_block(n, carry):
        for f in range(6):
            of[:, f * E : (f + 1) * E] = onehot(small_row(key_out[f : f + 1, :] - n * 256, 256), 256)
        acc = dot_nt(vf[...], of[...])
        tf[:, pl.ds(pl.multiple_of(n * 256, 256), 256)] = sum2(acc)
        return carry

    lax.fori_loop(0, F_KEYS // 256, face_block, 0)
    fd[...] = tf[:, 1536:1664]
    fs[...] = tf[:, 1664:1792]


def scatter_lines(key_out, te, tc, md, ms, ve, vc, le, ol, acc_e):
    for e in range(12):
        at = slice(e * E, (e + 1) * E)
        key = key_out[6 + e : 7 + e, :]
        hi = small_row(key >> 8, E_HI)
        ol[:, at] = onehot(small_row(key & 255, 256), 256)
        for g in range(4):
            ag = slice(e * E + g * 128, e * E + (g + 1) * 128)
            hb = jnp.broadcast_to(hi[:, g * 128 : (g + 1) * 128], (16, 128))
            zero = jnp.zeros((16, 128), bf16)
            parts = [ve[s * 16 : s * 16 + 16, ag] for s in range(2)]
            for h in range(E_HI):
                m = hb == jnp.full((16, 128), float(h), bf16)
                for s in range(2):
                    le[(s * E_HI + h) * 16 : (s * E_HI + h + 1) * 16, ag] = jnp.where(m, parts[s], zero)
    acc_e[...] = dot_nt(le[...], ol[...])
    for h in range(E_HI):
        te[h] = sum(acc_e[(s * E_HI + h) * 16 : (s * E_HI + h + 1) * 16, :] for s in range(2))

    full = E * 8
    for q in range(8):
        at = slice(q * E, (q + 1) * E)
        ol[:, at] = onehot(small_row(key_out[18 + q : 19 + q, :] & 255, 256), 256)
    hi = jnp.concatenate([key_out[18 + q : 19 + q, :] >> 8 for q in range(8)], axis=1)
    x = vc[...]
    big = jnp.concatenate(
        [jnp.where(jnp.broadcast_to(hi, (8, full)) == h, x, 0.0) for h in range(C_HI)], axis=0
    )
    acc = sum2(dot_nt(stack2(big), ol[:, 0:full]))
    for h in range(C_HI):
        tc[h] = acc[h * 8 : (h + 1) * 8]

    for g in range(4):
        er, cr = msg_rows(g)
        half_lanes = slice((g % 2) * 128, (g % 2) * 128 + 128)
        md[er : er + 16, :] = te[6 + g // 2, :, half_lanes]
        ms[er : er + 16, :] = te[8 + g // 2, :, half_lanes]
        md[cr : cr + 8, :] = tc[2 + g // 2, :, half_lanes]
        ms[cr : cr + 8, :] = tc[4 + g // 2, :, half_lanes]


def msg_rows(g):
    if g < 3:
        return 16 * g, 48 + 8 * g
    return 72, 88


def owner_faces(tf, gd, gs, tf2, rd, rs):
    vals = jnp.concatenate([gd[...], gs[...]], axis=1)
    key = vals[0:1, :].astype(i32)
    vs = stack2(vals)
    ret = jnp.zeros((2 * F_ROWS, 256), f32)
    for n in range(F_BLOCK // 256):
        o = onehot(small_row(key - n * 256, 256), 256)
        total = tf[:, n * 256 : (n + 1) * 256] + sum2(dot_nt(vs, o))
        tf2[:, n * 256 : (n + 1) * 256] = total
        ret = ret + dot_nn(stack2(total), o)
    ret = sum2(ret)
    rd[...] = ret[:, 0:128]
    rs[...] = ret[:, 128:256]


def owner_lines(te, tc, gd, gs, gboth, te2, tc2, rd, rs, rb):
    lane = lax.broadcasted_iota(i32, (1, 128), 1)

    def lines(rows, id_row, total_ref, total_out, his, cut, at):
        vals, keys = [], []
        for src in (gd, gs):
            for g in range(4):
                r = msg_rows(g)[at]
                v = src[r : r + rows, :]
                k = v[id_row : id_row + 1].astype(i32)
                if src is gd and g == 3:
                    k = jnp.where(lane >= cut, -1, k)
                vals.append(v)
                keys.append(k)
        r = msg_rows(3)[at] - (LINES - BOTH)
        v = gboth[r : r + rows, :]
        keys.append(jnp.where(lane < cut, -1, v[id_row : id_row + 1].astype(i32)))
        vals.append(v)
        x = jnp.concatenate(vals, axis=1)
        key = jnp.concatenate(keys, axis=1)
        hi = key >> 8
        o = onehot(small_row(key & 255, 256), 256)
        big = jnp.concatenate([jnp.where(jnp.broadcast_to(hi, x.shape) == h, x, 0.0) for h in range(his)], axis=0)
        acc = sum2(dot_nt(stack2(big), o))
        totals = jnp.concatenate([total_ref[h] for h in range(his)], axis=0) + acc
        for h in range(his):
            total_out[h] = totals[h * rows : (h + 1) * rows]
        y = sum2(dot_nn(stack2(totals), o))
        back = jnp.zeros_like(x)
        for h in range(his):
            back = jnp.where(jnp.broadcast_to(hi, x.shape) == h, y[h * rows : (h + 1) * rows], back)
        for n, dst in enumerate((rd, rs)):
            for g in range(4):
                p = msg_rows(g)[at]
                dst[p : p + rows, :] = back[:, (n * 4 + g) * 128 : (n * 4 + g + 1) * 128]
        rb[r : r + rows, :] = back[:, 1024:1152]

    lines(16, 0, te, te2, E_BLOCK // 256, 96, 0)
    lines(8, 2, tc, tc2, C_BLOCK // 256, 64, 1)


def gather_faces(keys, tf, rd, rs, tfs, of, gf):
    for ref, at in ((tf, slice(0, 1536)), (rd, slice(1536, 1664)), (rs, slice(1664, 1792))):
        for s, p in enumerate(split2(ref[...])):
            tfs[s * F_ROWS : (s + 1) * F_ROWS, at] = p

    def face_gather(f, carry):
        key = keys[pl.ds(f, 1), :]
        for n in range(F_KEYS // 256):
            of[n * 256 : (n + 1) * 256, :] = onehot(small_row(key - n * 256, 256), 256)
        gf[f] = sum2(dot_nn(tfs[...], of[...]))
        return carry

    lax.fori_loop(0, 6, face_gather, 0)


def gather_lines(keys, te, tc, rd, rs, rb, ge, gc):
    lane = lax.broadcasted_iota(i32, (1, 128), 1)

    def table(own, his, rows, at, cut):
        blocks = [own[h] for h in range(his)]
        for src in (rd, rs):
            for g in (0, 2):
                pair = []
                for q in (g, g + 1):
                    r = msg_rows(q)[at]
                    v = src[r : r + rows, :]
                    if src is rd and q == 3:
                        b = r - (LINES - BOTH)
                        v = jnp.where(jnp.broadcast_to(lane, (rows, 128)) >= cut, rb[b : b + rows, :], v)
                    pair.append(v)
                blocks.append(jnp.concatenate(pair, axis=1))
        return stack2(jnp.concatenate(blocks, axis=0))

    def line_gather(tab, first, count, his, rows, dst):
        for q in range(count):
            key = keys[first + q : first + q + 1, :]
            hi = key >> 8
            y = sum2(dot_nn(tab, onehot(small_row(key & 255, 256), 256)))
            back = jnp.zeros((rows, E), f32)
            for h in range(his):
                back = jnp.where(jnp.broadcast_to(hi, (rows, E)) == h, y[h * rows : (h + 1) * rows], back)
            dst[q] = back

    line_gather(table(te, 6, 16, 0, 96), 6, 12, E_HI, 16, ge)
    line_gather(table(tc, 2, 8, 1, 64), 18, 8, C_HI, 8, gc)

def place_relax(im, dg, gf, ge, gc, sol, forc, rel):
    for c in range(4):
        at = slice(c * 128, (c + 1) * 128)
        for ref, base in ((im.at[c], 0), (dg.at[c], 1)):
            for f in range(6):
                v = gf[f, base * PLANE : (base + 1) * PLANE, at]
                if f < 2:
                    start = 8 if f == 0 else 456
                    ref[start : start + PLANE, :] = v
                elif f < 4:
                    j = 0 if f == 2 else 7
                    for i in range(1, 7):
                        ref[pl.ds((i * N + j) * N, N), :] = v[(i - 1) * N : i * N]
                else:
                    ref[pl.ds(64 if f == 4 else 71, PLANE, stride=N), :] = v
            for e in range(12):
                start, stride = EDGE_ROWS[e]
                rows = pl.ds(start, N) if stride == 1 else pl.ds(start, N, stride=stride)
                ref[rows, :] = ge[e, base * 8 : base * 8 + 8, at]
            for q in range(8):
                r = CORNER_ROWS[q]
                ref[r : r + 1, :] = gc[q, base : base + 1, at]
        s = sol[:, :, :, at].reshape(NODES, 128)
        v = s + RELAX * (forc[:, :, :, at].reshape(NODES, 128) - im[c]) / dg[c]
        rel[:, :, :, at] = v.reshape(N, N, N, 128)

MESH = pl.DeviceIdType.MESH


def main_kernel(
    owner, ids, kmat_in, sol_in, forc_in, met_in,
    m0, m1, m2, m3, m4, m5, m6, rel, f0, f1, f2, f3,
    sol, forc, kmat, im, dg, keys, rix, tf, te, tc, fd, fs, md, ms,
    gfd, gfs, gd, gs, gb, tf2, te2, tc2, sfd, sfs, sd, ss, sb, rfd, rfs, rd, rs, rb,
    vf, ve, vc, ga, gb2, gc2, of, le, ol, acc_e,
    tfs, og, gf, ge, gc, p0, p1, p2, p3, a0, a1, a2, a3, pa, pb,
    load_sem, msg_send, msg_recv, move_send, move_recv,
):
    na, nb = lax.axis_size("dom"), lax.axis_size("sub")
    d, s = lax.axis_index("dom"), lax.axis_index("sub")
    dn, dp = lax.rem(d + 1, na), lax.rem(d + na - 1, na)
    sn, sp = lax.rem(s + 1, nb), lax.rem(s + nb - 1, nb)
    prev_dom, next_dom, prev_sub, next_sub = (dp, s), (dn, s), (d, sp), (d, sn)
    prev_both, next_both = (dp, sp), (dn, sn)
    met = (m0, m1, m2, m3, m4, m5, m6)
    loads = [pltpu.make_async_copy(met_in.at[m], met[m], load_sem.at[m]) for m in range(7)]
    loads.append(pltpu.make_async_copy(sol_in, sol, load_sem.at[7]))
    loads.append(pltpu.make_async_copy(forc_in, forc, load_sem.at[8]))
    loads.append(pltpu.make_async_copy(kmat_in, kmat, load_sem.at[9]))
    for copy in loads:
        copy.start()

    barrier = pltpu.get_barrier_semaphore()
    for peer in (prev_dom, next_dom, prev_sub, next_sub, prev_both, next_both):
        pl.semaphore_signal(barrier, inc=1, device_id=peer, device_id_type=MESH)

    devs = [x * nb + y for x, y in ((d, s), prev_dom, next_dom, prev_sub, next_sub, next_both)]
    tri = prefix_matrix()
    make_keys(ids, devs, keys, rix, tri)
    _, leave, _ = move_rows(owner[...], devs, tri)
    pa[...] = onehot(small_row(leave, 256), 256)
    pb[...] = onehot(small_row(swapped(leave), 256), 256)
    pl.semaphore_wait(barrier, 6)

    def remote(src, dst, send_sem, recv_sem, peer):
        copy = pltpu.make_async_remote_copy(
            src_ref=src, dst_ref=dst, send_sem=send_sem, recv_sem=recv_sem,
            device_id=peer, device_id_type=MESH,
        )
        copy.start()
        return copy

    half = NODES // 2
    moves = []

    def move(m, x):
        for ref, val in zip((p0, p1, p2, p3), pack_block(x, pa[...], pb[...])):
            ref[m] = val
        for n, (src, dst, last, peer) in enumerate((
            (p2, a3, f3, prev_sub), (p3, a2, f2, next_sub), (p0, a1, f1, prev_dom), (p1, a0, f0, next_dom),
        )):
            to = last if m == 7 else dst.at[m]
            moves.append(remote(src.at[m], to, move_send.at[m, n], move_recv.at[m, n], peer))

    for m in range(7):
        loads[m].wait()
        move(m, met[m][...].reshape(NODES, E))

    loads[7].wait()
    loads[9].wait()

    def chunk(c, carry):
        apply_chunk(c, sol, met, kmat, im, dg, rix, vf, ve, vc, ga, gb2, gc2)
        return carry

    lax.fori_loop(0, 4, chunk, 0)

    def send(n, src, dst, peer):
        return remote(src, dst, msg_send.at[n], msg_recv.at[n], peer)

    scatter_faces(keys, tf, fd, fs, vf, of)
    face_out = [send(0, fs, gfs, next_sub), send(1, fd, gfd, next_dom)]
    scatter_lines(keys, te, tc, md, ms, ve, vc, le, ol, acc_e)
    line_out = [
        send(2, ms, gs, next_sub),
        send(3, md, gd, next_dom),
        send(4, md.at[pl.ds(LINES - BOTH, BOTH)], gb, next_both),
    ]
    for copy in face_out:
        copy.wait()
    owner_faces(tf, gfd, gfs, tf2, sfd, sfs)
    face_back = [send(5, sfs, rfs, prev_sub), send(6, sfd, rfd, prev_dom)]
    for copy in line_out:
        copy.wait()
    owner_lines(te, tc, gd, gs, gb, te2, tc2, sd, ss, sb)
    line_back = [send(7, ss, rs, prev_sub), send(8, sd, rd, prev_dom), send(9, sb, rb, prev_both)]
    for copy in face_back:
        copy.wait()
    gather_faces(keys, tf2, rfd, rfs, tfs, og, gf)
    for copy in line_back:
        copy.wait()
    gather_lines(keys, te2, tc2, rd, rs, rb, ge, gc)
    loads[8].wait()
    place_relax(im, dg, gf, ge, gc, sol, forc, rel)
    move(7, rel[...].reshape(NODES, E))
    departed, _, arrive = move_rows(owner[...], devs, tri)
    pa[...] = onehot(small_row(arrive, 256), 256)
    pb[...] = onehot(small_row(swapped(arrive), 256), 256)
    for m in range(7):
        for copy in moves[4 * m : 4 * m + 4]:
            copy.wait()
        land_block(met[m], [a[m] for a in (a0, a1, a2, a3)], pa[...], pb[...], departed, met[m])
    for copy in moves[28:]:
        copy.wait()


def main_call(owner, ids, solution, forcing, metric):
    half = NODES // 2
    eye = np.eye(N, dtype=np.float32)
    kmat = np.stack([np.kron(eye, TABLE), np.kron(eye, TABLE.T), np.kron(eye, SQUARED.T)])
    vm = pl.BlockSpec(memory_space=pltpu.VMEM)
    hbm = pl.BlockSpec(memory_space=pl.ANY)
    box = pltpu.VMEM((N, N, N, E), f32)
    planes = pltpu.VMEM((4, NODES, 128), f32)
    face, line, both = (pltpu.VMEM((r, 128), f32) for r in (F_ROWS, LINES, BOTH))
    work = pltpu.VMEM((NODES, 128), f32)
    moved = pltpu.VMEM((8, half, 128), f32)
    came = pltpu.VMEM((7, half, 128), f32)
    return pl.pallas_call(
        main_kernel,
        in_specs=[vm] * 2 + [hbm] * 4,
        out_specs=[vm] * 12,
        out_shape=[jax.ShapeDtypeStruct((N, N, N, E), f32)] * 8
        + [jax.ShapeDtypeStruct((half, 128), f32)] * 4,
        scratch_shapes=[
            box, box,
            pltpu.VMEM((3, 64, 64), f32), planes, planes,
            pltpu.VMEM((26, E), i32),
            pltpu.VMEM((26, E), f32),
            pltpu.VMEM((F_ROWS, F_KEYS), f32),
            pltpu.VMEM((E_HI, 16, 256), f32),
            pltpu.VMEM((C_HI, 8, 256), f32),
            face, face, line, line,
            face, face, line, line, both,
            pltpu.VMEM((F_ROWS, F_BLOCK), f32),
            pltpu.VMEM((E_BLOCK // 256, 16, 256), f32),
            pltpu.VMEM((C_BLOCK // 256, 8, 256), f32),
            face, face, line, line, both,
            face, face, line, line, both,
            pltpu.VMEM((2 * F_ROWS, 6 * E), bf16),
            pltpu.VMEM((32, 12 * E), bf16),
            pltpu.VMEM((8, 8 * E), f32),
            work, work, work,
            pltpu.VMEM((256, 6 * E), bf16),
            pltpu.VMEM((2 * E_HI * 16, 12 * E), bf16),
            pltpu.VMEM((256, 12 * E), bf16),
            pltpu.VMEM((2 * E_HI * 16, 256), f32),
            pltpu.VMEM((2 * F_ROWS, F_KEYS), bf16),
            pltpu.VMEM((F_KEYS, E), bf16),
            pltpu.VMEM((6, F_ROWS, E), f32),
            pltpu.VMEM((12, 16, E), f32),
            pltpu.VMEM((8, 8, E), f32),
            moved, moved, moved, moved,
            came, came, came, came,
            pltpu.VMEM((256, E), bf16),
            pltpu.VMEM((256, E), bf16),
            pltpu.SemaphoreType.DMA((10,)),
            pltpu.SemaphoreType.DMA((10,)),
            pltpu.SemaphoreType.DMA((10,)),
            pltpu.SemaphoreType.DMA((8, 4)),
            pltpu.SemaphoreType.DMA((8, 4)),
        ],
        compiler_params=pltpu.CompilerParams(
            vmem_limit_bytes=45 << 20, collective_id=0, has_side_effects=True
        ),
        interpret=pltpu.InterpretParams() if INTERPRET else False,
        name="main",
    )(owner, ids, kmat, solution, forcing, metric)


def land_kernel(
    devs, owner_ref, m0, m1, m2, m3, m4, m5, m6, rel_in, f0, f1, f2, f3, met_out, rel_out, y, out_sem
):
    met = (m0, m1, m2, m3, m4, m5, m6)
    stores = [pltpu.make_async_copy(met[m], met_out.at[m], out_sem.at[m]) for m in range(7)]
    for copy in stores:
        copy.start()
    departed, _, arrive = move_rows(owner_ref[...], [devs[d] for d in range(5)], prefix_matrix())
    pa = onehot(small_row(arrive, 256), 256)
    pb = onehot(small_row(swapped(arrive), 256), 256)
    land_block(rel_in, [f[...] for f in (f0, f1, f2, f3)], pa, pb, departed, y)
    stores.append(pltpu.make_async_copy(y, rel_out, out_sem.at[7]))
    stores[7].start()
    for copy in stores:
        copy.wait()


def land(devs, owner, shape, blocks):
    vm = pl.BlockSpec(memory_space=pltpu.VMEM)
    hbm = pl.BlockSpec(memory_space=pltpu.HBM)
    return pl.pallas_call(
        land_kernel,
        in_specs=[pl.BlockSpec(memory_space=pltpu.SMEM)] + [vm] * 13,
        out_specs=[hbm] * 2,
        out_shape=[jax.ShapeDtypeStruct(shape, f32), jax.ShapeDtypeStruct(shape[1:], f32)],
        scratch_shapes=[
            pltpu.VMEM((N, N, N, E), f32),
            pltpu.SemaphoreType.DMA((8,)),
        ],
        compiler_params=pltpu.CompilerParams(vmem_limit_bytes=8 << 20),
        interpret=INTERPRET,
        name="land",
    )(devs, owner, *blocks)


def on_device(solution, forcing, metric, entity_ids, new_owner):
    a, b = lax.axis_size("dom"), lax.axis_size("sub")
    d, s = lax.axis_index("dom"), lax.axis_index("sub")
    da, db = (d + 1) % a, (d + a - 1) % a
    sa, sb = (s + 1) % b, (s + b - 1) % b
    devs = jnp.stack([d * b + s, db * b + s, da * b + s, d * b + sb, d * b + sa, da * b + sa]).astype(i32)
    owner = new_owner.reshape(1, E)

    blocks = main_call(owner, entity_ids, solution, forcing, metric)
    moved_metric, smoothed = land(devs, owner, metric.shape, blocks)
    return smoothed, moved_metric


def solution(mesh):
    cols = ("dom", "sub")
    placed = (
        P(None, None, None, cols),
        P(None, None, None, cols),
        P(None, None, None, None, cols),
        P(None, cols),
        P(cols),
    )
    return jax.shard_map(
        on_device,
        mesh=mesh,
        in_specs=placed,
        out_specs=(P(None, None, None, cols), P(None, None, None, None, cols)),
        check_vma=False,
    )
```

```python
import functools

import jax
import jax.numpy as jnp
import numpy as np
from jax import lax
from jax.experimental import pallas as pl
from jax.experimental.pallas import tpu as pltpu
from jax.sharding import PartitionSpec as P

N = 8
E = 512
NODES = N * N * N
EX = 4
EY = 4
EZ = 32
MOVE = 64
RELAX = 0.6
F_BLOCK, E_BLOCK, C_BLOCK = 3 * E, 3 * E, E
F_KEYS, E_KEYS, C_KEYS = 1792, 2560, 1536
F_HI, E_HI, C_HI = F_KEYS // 256, E_KEYS // 256, C_KEYS // 256
PLANE = 48
F_ROWS = 2 * PLANE
LINES = 96
BOTH = 24
INTERPRET = False

f32, bf16, i32 = jnp.float32, jnp.bfloat16, jnp.int32


def derivative_table(order):
    count = order + 1
    points = -np.cos(np.pi * np.arange(count) / order)
    legendre = np.zeros((count, count))
    for sweep in range(80):
        legendre[:, 0] = 1.0
        legendre[:, 1] = points
        for degree in range(2, count):
            legendre[:, degree] = (
                (2 * degree - 1) * points * legendre[:, degree - 1]
                - (degree - 1) * legendre[:, degree - 2]
            ) / degree
        points = points - (points * legendre[:, order] - legendre[:, order - 1]) / (
            count * legendre[:, order]
        )
    legendre[:, 0] = 1.0
    legendre[:, 1] = points
    for degree in range(2, count):
        legendre[:, degree] = (
            (2 * degree - 1) * points * legendre[:, degree - 1]
            - (degree - 1) * legendre[:, degree - 2]
        ) / degree
    values = legendre[:, order]
    identity = np.eye(count)
    spread = points[:, None] - points[None, :] + identity
    table = values[:, None] / values[None, :] / spread
    table = table * (1.0 - identity)
    table[0, 0] = -order * count / 4.0
    table[order, order] = order * count / 4.0
    return table.astype(np.float32)


TABLE = derivative_table(N - 1)
SQUARED = TABLE * TABLE
ALONG = [float(v) for v in np.diagonal(TABLE)]


def row_of(i, j, k):
    return (i * N + j) * N + k


EDGE_ROWS = (
    [(row_of(0, a, b), N * N) for a in (0, 7) for b in (0, 7)]
    + [(row_of(a, 0, b), N) for a in (0, 7) for b in (0, 7)]
    + [(row_of(a, b, 0), 1) for a in (0, 7) for b in (0, 7)]
)
CORNER_ROWS = [row_of(a, b, c) for a in (0, 7) for b in (0, 7) for c in (0, 7)]


def split2(x):
    hi = x.astype(bf16)
    return hi, (x - hi.astype(f32)).astype(bf16)


def stack2(x):
    return jnp.concatenate(split2(x), axis=0)


def sum2(x):
    m = x.shape[0] // 2
    return x[0:m] + x[m:]


def dot_nn(a, b):
    return lax.dot_general(a, b, (((1,), (0,)), ((), ())), preferred_element_type=f32)


def dot_nt(a, b):
    return lax.dot_general(a, b, (((1,), (1,)), ((), ())), preferred_element_type=f32)


def small_row(key, count):
    ok = (key >= 0) & (key < count)
    return jnp.where(ok, key, -1).astype(f32).astype(bf16)


def iota_rows(count, lanes):
    return lax.broadcasted_iota(i32, (count, lanes), 0).astype(f32).astype(bf16)


def onehot(row, count):
    lanes = row.shape[1]
    io = iota_rows(count, 128)
    one, zero = jnp.ones((count, 128), bf16), jnp.zeros((count, 128), bf16)
    cols = [
        jnp.where(io == jnp.broadcast_to(row[:, g : g + 128], (count, 128)), one, zero)
        for g in range(0, lanes, 128)
    ]
    return cols[0] if len(cols) == 1 else jnp.concatenate(cols, axis=1)


def prefix_matrix():
    a = lax.broadcasted_iota(i32, (E, E), 0)
    b = lax.broadcasted_iota(i32, (E, E), 1)
    return jnp.where(a <= b, 1.0, 0.0).astype(bf16)


def ranks(mask, tri):
    m = mask.shape[0]
    flags = jnp.where(mask, 1.0, 0.0)
    within = dot_nn(flags.astype(bf16), tri) - 1.0
    if m > 1:
        before = jnp.zeros((1, 1), f32)
        offs = [before]
        for r in range(m - 1):
            before = before + jnp.sum(flags[r : r + 1], axis=1, keepdims=True)
            offs.append(before)
        within = within + jnp.concatenate(offs, axis=0)
    return within.astype(i32)


def move_rows(owner, devs, tri):
    own = devs[0]
    departed = owner != own
    leave = jnp.full((1, E), -1, i32)
    arrive = jnp.full((1, E), -1, i32)
    flags = [departed] + [departed & (owner == devs[d]) for d in range(1, 5)]
    stacked = jnp.concatenate([jnp.where(f, 1.0, 0.0) for f in flags] + [jnp.zeros((3, E), f32)], axis=0)
    pre = dot_nn(stacked.astype(bf16), tri)
    hole = pre[0:1] - 1.0
    start = jnp.zeros((1, 1), f32)
    for d in range(4):
        chosen = flags[d + 1]
        rank = pre[d + 1 : d + 2] - 1.0
        leave = jnp.where(chosen, d * MOVE + rank.astype(i32), leave)
        count = pre[d + 1 : d + 2, E - 1 : E]
        pos = hole - start
        inside = departed & (pos >= 0.0) & (pos < count)
        arrive = jnp.where(inside, d * MOVE + pos.astype(i32), arrive)
        start = start + count
    return departed, leave, arrive


def swapped(col):
    return jnp.where(col >= 0, col ^ MOVE, -1)


def lane_low(rows):
    return lax.broadcasted_iota(i32, (rows, 128), 1) < MOVE


def pack_block(x, pa, pb):
    half = NODES // 2
    ya = sum2(dot_nt(stack2(x[0:half]), pa))
    yb = sum2(dot_nt(stack2(x[half:]), pb))
    low = lane_low(half)
    out = []
    for g in (0, 128):
        a, b = ya[:, g : g + 128], yb[:, g : g + 128]
        out.append(jnp.where(low, a, b))
        out.append(jnp.where(low, b, a))
    return out


def land_block(x, got, pa, pb, departed, out):
    half = NODES // 2
    low = lane_low(half)
    zl, zh = [], []
    for g in (0, 2):
        zl.append(jnp.where(low, got[g + 1], got[g]))
        zh.append(jnp.where(low, got[g], got[g + 1]))
    keep = jnp.logical_not(departed)
    for at, z, p in ((slice(0, 4), zl, pb), (slice(4, 8), zh, pa)):
        y = sum2(dot_nn(stack2(jnp.concatenate(z, axis=1)), p))
        v = jnp.where(keep, x[at].reshape(half, E), y)
        out[at] = v.reshape(4, N, N, E)


def block_table(table):
    r = lax.broadcasted_iota(i32, (N, 64), 0)
    c = lax.broadcasted_iota(i32, (N, 64), 1)
    tile_of = jnp.zeros((N, 64), f32)
    low = c & 7
    for a in range(N):
        row = jnp.zeros((N, 64), f32)
        for i in range(N):
            row = jnp.where(low == i, float(table[a, i]), row)
        tile_of = jnp.where(r == a, row, tile_of)
    return jnp.concatenate([jnp.where(c >> 3 == b, tile_of, 0.0) for b in range(N)], axis=0)


def halves(table):
    t = table.astype(np.float64)
    return (t[:4, :4] + t[:4, :3:-1]) / 2, (t[:4, :4] - t[:4, :3:-1]) / 2


def combine(xs, table, odd):
    even_w, odd_w = halves(table)
    e = [xs[p] + xs[7 - p] for p in range(4)]
    o = [xs[p] - xs[7 - p] for p in range(4)]
    out = [None] * N
    for a in range(4):
        u = sum(float(even_w[a, p]) * e[p] for p in range(4))
        v = sum(float(odd_w[a, p]) * o[p] for p in range(4))
        out[a] = v + u
        out[7 - a] = v - u if odd else u - v
    return out


def contract_i(src, table, odd, put):
    for j in range(N):
        for a, v in enumerate(combine([src(i, j) for i in range(N)], table, odd)):
            put(a, j, v)


def contract_j(src, table, odd, put):
    for i in range(N):
        for b, v in enumerate(combine([src(i, j) for j in range(N)], table, odd)):
            put(i, b, v)


def key_rows(ids, block, devs, dom_base, both_base, sub_base, tri):
    rel, inside = [], []
    for d in (0, 2, 4, 5):
        r = ids - devs[d] * block
        rel.append(r)
        inside.append((r >= 0) & (r < block))
    key = jnp.where(inside[0], rel[0], -1)
    key = jnp.where(inside[1], dom_base + ranks(inside[1], tri), key)
    key = jnp.where(inside[2], sub_base + ranks(inside[2], tri), key)
    if both_base is not None:
        key = jnp.where(inside[3], both_base + ranks(inside[3], tri), key)
    row = jnp.where(inside[0], rel[0], jnp.where(inside[1], rel[1], jnp.where(inside[2], rel[2], rel[3])))
    return key, row.astype(f32)


def tile(ref, r):
    return ref[pl.ds(r * N, N), :]


def make_keys(ids, devs, key_out, rix, tri):
    k, r = key_rows(ids[0:6], F_BLOCK, devs, 1536, None, 1664, tri)
    key_out[0:6, :] = k
    rix[0:6, :] = r
    k, r = key_rows(ids[6:18], E_BLOCK, devs, 1536, 2016, 2048, tri)
    key_out[6:18, :] = k
    rix[6:18, :] = r
    k, r = key_rows(ids[18:26], C_BLOCK, devs, 512, 960, 1024, tri)
    key_out[18:26, :] = k
    rix[18:26, :] = r


def apply_chunk(c, sol_all, met_all, kmat, im_all, dg_all, rix, vf, ve, vc, ga, gb, gc):
    lanes = pl.ds(pl.multiple_of(c * 128, 128), 128)
    sol = sol_all.at[:, :, :, lanes]
    met = [m.at[:, :, :, lanes] for m in met_all]
    im, dg = im_all.at[c], dg_all.at[c]
    fwd, bwd = kmat.at[0], kmat.at[1]
    slab = N * N

    def kdot(m, x):
        return lax.dot_general(
            m, x, (((1,), (0,)), ((), ())),
            precision=lax.Precision.HIGHEST, preferred_element_type=f32,
        )

    def put_a(i, j, v):
        ga[pl.ds((i * N + j) * N, N), :] = v

    def put_b(i, j, v):
        gb[pl.ds((i * N + j) * N, N), :] = v

    contract_i(lambda i, j: sol[i, j], TABLE, True, put_a)
    contract_j(lambda i, j: sol[i, j], TABLE, True, put_b)
    for h in range(N):
        gc[h * slab : (h + 1) * slab, :] = kdot(fwd[...], sol[h].reshape(slab, 128))

    for i in range(N):
        for j in range(N):
            r = i * N + j
            a, b, t = tile(ga, r), tile(gb, r), tile(gc, r)
            m3, m4, m5 = met[3][i, j], met[4][i, j], met[5][i, j]
            ga[pl.ds(r * N, N), :] = met[0][i, j] * a + m3 * b + m4 * t
            gb[pl.ds(r * N, N), :] = m3 * a + met[1][i, j] * b + m5 * t
            gc[pl.ds(r * N, N), :] = m4 * a + m5 * b + met[2][i, j] * t

    for h in range(N):
        im[h * slab : (h + 1) * slab, :] = kdot(bwd[...], gc[h * slab : (h + 1) * slab, :])

    def add_im(i, j, v):
        im[pl.ds((i * N + j) * N, N), :] += v

    contract_i(lambda i, j: tile(ga, i * N + j), TABLE.T, True, add_im)

    def add_im_last(i, j, v):
        im[pl.ds((i * N + j) * N, N), :] += v + met[6][i, j] * sol[i, j]

    contract_j(lambda i, j: tile(gb, i * N + j), TABLE.T, True, add_im_last)

    sq = kmat.at[2]
    for h in range(N):
        dg[h * slab : (h + 1) * slab, :] = kdot(sq[...], met[2][h].reshape(slab, 128))

    def add_dg(i, j, v):
        dg[pl.ds((i * N + j) * N, N), :] += v

    contract_i(lambda i, j: met[0][i, j], SQUARED.T, False, add_dg)
    kk = lax.broadcasted_iota(i32, (N, 128), 0)
    dk = jnp.where(kk == 0, ALONG[0], jnp.where(kk == N - 1, ALONG[N - 1], 0.0))

    def add_dg_last(i, j, v):
        v = v + met[6][i, j]
        if ALONG[i] * ALONG[j] != 0.0:
            v = v + (2.0 * ALONG[i] * ALONG[j]) * met[3][i, j]
        if ALONG[i] != 0.0:
            v = v + (2.0 * ALONG[i]) * dk * met[4][i, j]
        if ALONG[j] != 0.0:
            v = v + (2.0 * ALONG[j]) * dk * met[5][i, j]
        dg[pl.ds((i * N + j) * N, N), :] += v

    contract_j(lambda i, j: met[1][i, j], SQUARED.T, False, add_dg_last)

    def face(ref, f):
        if f < 2:
            base = 8 if f == 0 else 456
            return ref[base : base + PLANE, :]
        if f < 4:
            j = 0 if f == 2 else 7
            return jnp.concatenate([ref[pl.ds((i * N + j) * N, N), :] for i in range(1, 7)], axis=0)
        return ref[pl.ds(64 if f == 4 else 71, PLANE, stride=N), :]

    top = lax.broadcasted_iota(i32, (N, 128), 0) == 0
    for f in range(6):
        at = pl.ds(pl.multiple_of(f * E + c * 128, 128), 128)
        a, b = face(im, f), face(dg, f)
        mark = jnp.broadcast_to(rix[f : f + 1, lanes], (N, 128))
        a = jnp.concatenate([jnp.where(top, mark, a[0:N]), a[N:]], axis=0)
        for s, (p, q) in enumerate(zip(split2(a), split2(b))):
            vf[s * F_ROWS : s * F_ROWS + PLANE, at] = p
            vf[s * F_ROWS + PLANE : (s + 1) * F_ROWS, at] = q
    for e in range(12):
        at = pl.ds(pl.multiple_of(e * E + c * 128, 128), 128)
        start, stride = EDGE_ROWS[e]
        rows = pl.ds(start, N) if stride == 1 else pl.ds(start, N, stride=stride)
        a, b = im[rows, :], dg[rows, :]
        mark = jnp.broadcast_to(rix[6 + e : 7 + e, lanes], (N, 128))
        x = jnp.concatenate([jnp.where(top, mark, a), b], axis=0)
        for s, p in enumerate(split2(x)):
            ve[s * 16 : s * 16 + 16, at] = p
    for q in range(8):
        at = pl.ds(pl.multiple_of(q * E + c * 128, 128), 128)
        r = CORNER_ROWS[q]
        vc[0:1, at] = im[r : r + 1, :]
        vc[1:2, at] = dg[r : r + 1, :]
        vc[2:3, at] = rix[18 + q : 19 + q, lanes]
        vc[3:8, at] = jnp.zeros((5, 128), f32)


def scatter_faces(key_out, tf, fd, fs, vf, lf, of, acc_f):
    rows = 2 * F_ROWS
    zero = jnp.zeros((rows, 128), bf16)
    for f in range(6):
        key = key_out[f : f + 1, :]
        hi = small_row(key >> 8, F_HI)
        of[:, f * E : (f + 1) * E] = onehot(small_row(key & 255, 256), 256)
        for g in range(4):
            at = slice(f * E + g * 128, f * E + (g + 1) * 128)
            hb = jnp.broadcast_to(hi[:, g * 128 : (g + 1) * 128], (rows, 128))
            part = vf[:, at]
            for h in range(F_HI):
                lf[h * rows : (h + 1) * rows, at] = jnp.where(hb == jnp.full((rows, 128), float(h), bf16), part, zero)
    acc_f[...] = dot_nt(lf[...], of[...])
    for h in range(F_HI):
        tf[:, h * 256 : (h + 1) * 256] = sum2(acc_f[h * rows : (h + 1) * rows, :])
    fd[...] = tf[:, 1536:1664]
    fs[...] = tf[:, 1664:1792]


def scatter_lines(key_out, te, tc, md, ms, ve, vc, le, ol, acc_e):
    for e in range(12):
        at = slice(e * E, (e + 1) * E)
        key = key_out[6 + e : 7 + e, :]
        hi = small_row(key >> 8, E_HI)
        ol[:, at] = onehot(small_row(key & 255, 256), 256)
        for g in range(4):
            ag = slice(e * E + g * 128, e * E + (g + 1) * 128)
            hb = jnp.broadcast_to(hi[:, g * 128 : (g + 1) * 128], (16, 128))
            zero = jnp.zeros((16, 128), bf16)
            parts = [ve[s * 16 : s * 16 + 16, ag] for s in range(2)]
            for h in range(E_HI):
                m = hb == jnp.full((16, 128), float(h), bf16)
                for s in range(2):
                    le[(s * E_HI + h) * 16 : (s * E_HI + h + 1) * 16, ag] = jnp.where(m, parts[s], zero)
    acc_e[...] = dot_nt(le[...], ol[...])
    for h in range(E_HI):
        te[h] = sum(acc_e[(s * E_HI + h) * 16 : (s * E_HI + h + 1) * 16, :] for s in range(2))

    full = E * 8
    for q in range(8):
        at = slice(q * E, (q + 1) * E)
        ol[:, at] = onehot(small_row(key_out[18 + q : 19 + q, :] & 255, 256), 256)
    hi = jnp.concatenate([key_out[18 + q : 19 + q, :] >> 8 for q in range(8)], axis=1)
    x = vc[...]
    big = jnp.concatenate(
        [jnp.where(jnp.broadcast_to(hi, (8, full)) == h, x, 0.0) for h in range(C_HI)], axis=0
    )
    acc = sum2(dot_nt(stack2(big), ol[:, 0:full]))
    for h in range(C_HI):
        tc[h] = acc[h * 8 : (h + 1) * 8]

    for g in range(4):
        er, cr = msg_rows(g)
        half_lanes = slice((g % 2) * 128, (g % 2) * 128 + 128)
        md[er : er + 16, :] = te[6 + g // 2, :, half_lanes]
        ms[er : er + 16, :] = te[8 + g // 2, :, half_lanes]
        md[cr : cr + 8, :] = tc[2 + g // 2, :, half_lanes]
        ms[cr : cr + 8, :] = tc[4 + g // 2, :, half_lanes]


def msg_rows(g):
    if g < 3:
        return 16 * g, 48 + 8 * g
    return 72, 88


def owner_faces(tf, gd, gs, tf2, rd, rs):
    vals = jnp.concatenate([gd[...], gs[...]], axis=1)
    key = vals[0:1, :].astype(i32)
    vs = stack2(vals)
    ret = jnp.zeros((2 * F_ROWS, 256), f32)
    for n in range(F_BLOCK // 256):
        o = onehot(small_row(key - n * 256, 256), 256)
        total = tf[:, n * 256 : (n + 1) * 256] + sum2(dot_nt(vs, o))
        tf2[:, n * 256 : (n + 1) * 256] = total
        ret = ret + dot_nn(stack2(total), o)
    ret = sum2(ret)
    rd[...] = ret[:, 0:128]
    rs[...] = ret[:, 128:256]


def owner_lines(te, tc, gd, gs, gboth, te2, tc2, rd, rs, rb):
    lane = lax.broadcasted_iota(i32, (1, 128), 1)

    def lines(rows, id_row, total_ref, total_out, his, cut, at):
        vals, keys = [], []
        for src in (gd, gs):
            for g in range(4):
                r = msg_rows(g)[at]
                v = src[r : r + rows, :]
                k = v[id_row : id_row + 1].astype(i32)
                if src is gd and g == 3:
                    k = jnp.where(lane >= cut, -1, k)
                vals.append(v)
                keys.append(k)
        r = msg_rows(3)[at] - (LINES - BOTH)
        v = gboth[r : r + rows, :]
        keys.append(jnp.where(lane < cut, -1, v[id_row : id_row + 1].astype(i32)))
        vals.append(v)
        x = jnp.concatenate(vals, axis=1)
        key = jnp.concatenate(keys, axis=1)
        hi = key >> 8
        o = onehot(small_row(key & 255, 256), 256)
        big = jnp.concatenate([jnp.where(jnp.broadcast_to(hi, x.shape) == h, x, 0.0) for h in range(his)], axis=0)
        acc = sum2(dot_nt(stack2(big), o))
        totals = jnp.concatenate([total_ref[h] for h in range(his)], axis=0) + acc
        for h in range(his):
            total_out[h] = totals[h * rows : (h + 1) * rows]
        y = sum2(dot_nn(stack2(totals), o))
        back = jnp.zeros_like(x)
        for h in range(his):
            back = jnp.where(jnp.broadcast_to(hi, x.shape) == h, y[h * rows : (h + 1) * rows], back)
        for n, dst in enumerate((rd, rs)):
            for g in range(4):
                p = msg_rows(g)[at]
                dst[p : p + rows, :] = back[:, (n * 4 + g) * 128 : (n * 4 + g + 1) * 128]
        rb[r : r + rows, :] = back[:, 1024:1152]

    lines(16, 0, te, te2, E_BLOCK // 256, 96, 0)
    lines(8, 2, tc, tc2, C_BLOCK // 256, 64, 1)


def gather_faces(keys, tf, rd, rs, tfs, of, gf):
    for ref, at in ((tf, slice(0, 1536)), (rd, slice(1536, 1664)), (rs, slice(1664, 1792))):
        for s, p in enumerate(split2(ref[...])):
            tfs[s * F_ROWS : (s + 1) * F_ROWS, at] = p

    def face_gather(f, carry):
        key = keys[pl.ds(f, 1), :]
        for n in range(F_KEYS // 256):
            of[n * 256 : (n + 1) * 256, :] = onehot(small_row(key - n * 256, 256), 256)
        gf[f] = sum2(dot_nn(tfs[...], of[...]))
        return carry

    lax.fori_loop(0, 6, face_gather, 0)


def gather_lines(keys, te, tc, rd, rs, rb, ge, gc):
    lane = lax.broadcasted_iota(i32, (1, 128), 1)

    def table(own, his, rows, at, cut):
        blocks = [own[h] for h in range(his)]
        for src in (rd, rs):
            for g in (0, 2):
                pair = []
                for q in (g, g + 1):
                    r = msg_rows(q)[at]
                    v = src[r : r + rows, :]
                    if src is rd and q == 3:
                        b = r - (LINES - BOTH)
                        v = jnp.where(jnp.broadcast_to(lane, (rows, 128)) >= cut, rb[b : b + rows, :], v)
                    pair.append(v)
                blocks.append(jnp.concatenate(pair, axis=1))
        return stack2(jnp.concatenate(blocks, axis=0))

    def line_gather(tab, first, count, his, rows, dst):
        for q in range(count):
            key = keys[first + q : first + q + 1, :]
            hi = key >> 8
            y = sum2(dot_nn(tab, onehot(small_row(key & 255, 256), 256)))
            back = jnp.zeros((rows, E), f32)
            for h in range(his):
                back = jnp.where(jnp.broadcast_to(hi, (rows, E)) == h, y[h * rows : (h + 1) * rows], back)
            dst[q] = back

    line_gather(table(te, 6, 16, 0, 96), 6, 12, E_HI, 16, ge)
    line_gather(table(tc, 2, 8, 1, 64), 18, 8, C_HI, 8, gc)

def place_relax(im, dg, gf, ge, gc, sol, forc, rel):
    for c in range(4):
        at = slice(c * 128, (c + 1) * 128)
        for ref, base in ((im.at[c], 0), (dg.at[c], 1)):
            for f in range(6):
                v = gf[f, base * PLANE : (base + 1) * PLANE, at]
                if f < 2:
                    start = 8 if f == 0 else 456
                    ref[start : start + PLANE, :] = v
                elif f < 4:
                    j = 0 if f == 2 else 7
                    for i in range(1, 7):
                        ref[pl.ds((i * N + j) * N, N), :] = v[(i - 1) * N : i * N]
                else:
                    ref[pl.ds(64 if f == 4 else 71, PLANE, stride=N), :] = v
            for e in range(12):
                start, stride = EDGE_ROWS[e]
                rows = pl.ds(start, N) if stride == 1 else pl.ds(start, N, stride=stride)
                ref[rows, :] = ge[e, base * 8 : base * 8 + 8, at]
            for q in range(8):
                r = CORNER_ROWS[q]
                ref[r : r + 1, :] = gc[q, base : base + 1, at]
        s = sol[:, :, :, at].reshape(NODES, 128)
        v = s + RELAX * (forc[:, :, :, at].reshape(NODES, 128) - im[c]) / dg[c]
        rel[:, :, :, at] = v.reshape(N, N, N, 128)

MESH = pl.DeviceIdType.MESH


def main_kernel(
    owner_in, ids_in, sol_in, forc_in, met_in,
    m0, m1, m2, m3, m4, m5, m6, rel, f0, f1, f2, f3,
    owner, ids, sol, forc, kmat, im, dg, keys, rix, tf, te, tc, fd, fs, md, ms,
    gfd, gfs, gd, gs, gb, tf2, te2, tc2, sfd, sfs, sd, ss, sb, rfd, rfs, rd, rs, rb,
    vf, ve, vc, ga, gb2, gc2, lf, of, acc_f, le, ol, acc_e,
    tfs, og, gf, ge, gc, p0, p1, p2, p3, a0, a1, a2, a3, pa, pb, pc, pd,
    load_sem, msg_send, msg_recv, move_send, move_recv,
):
    na, nb = lax.axis_size("dom"), lax.axis_size("sub")
    d, s = lax.axis_index("dom"), lax.axis_index("sub")
    dn, dp = lax.rem(d + 1, na), lax.rem(d + na - 1, na)
    sn, sp = lax.rem(s + 1, nb), lax.rem(s + nb - 1, nb)
    prev_dom, next_dom, prev_sub, next_sub = (dp, s), (dn, s), (d, sp), (d, sn)
    prev_both, next_both = (dp, sp), (dn, sn)
    met = (m0, m1, m2, m3, m4, m5, m6)
    loads = [pltpu.make_async_copy(met_in.at[m], met[m], load_sem.at[m]) for m in range(7)]
    loads.append(pltpu.make_async_copy(sol_in, sol, load_sem.at[7]))
    loads.append(pltpu.make_async_copy(forc_in, forc, load_sem.at[8]))
    early = [pltpu.make_async_copy(owner_in, owner, load_sem.at[9]), pltpu.make_async_copy(ids_in, ids, load_sem.at[10])]
    for copy in early + loads:
        copy.start()

    barrier = pltpu.get_barrier_semaphore()
    for peer in (prev_dom, next_dom, prev_sub, next_sub, prev_both, next_both):
        pl.semaphore_signal(barrier, inc=1, device_id=peer, device_id_type=MESH)

    devs = [x * nb + y for x, y in ((d, s), prev_dom, next_dom, prev_sub, next_sub, next_both)]
    tri = prefix_matrix()
    for n, table in enumerate((TABLE, TABLE.T, SQUARED.T)):
        kmat[n] = block_table(table)
    for copy in early:
        copy.wait()
    departed, leave, arrive = move_rows(owner[...], devs, tri)
    pa[...] = onehot(small_row(leave, 256), 256)
    pb[...] = onehot(small_row(swapped(leave), 256), 256)
    make_keys(ids, devs, keys, rix, tri)
    pl.semaphore_wait(barrier, 6)

    def remote(src, dst, send_sem, recv_sem, peer):
        copy = pltpu.make_async_remote_copy(
            src_ref=src, dst_ref=dst, send_sem=send_sem, recv_sem=recv_sem,
            device_id=peer, device_id_type=MESH,
        )
        copy.start()
        return copy

    half = NODES // 2
    moves = []

    def fill(m, x):
        for ref, val in zip((p0, p1, p2, p3), pack_block(x, pa[...], pb[...])):
            ref[m] = val

    def push(m):
        for n, (src, dst, last, peer) in enumerate((
            (p2, a3, f3, prev_sub), (p3, a2, f2, next_sub), (p0, a1, f1, prev_dom), (p1, a0, f0, next_dom),
        )):
            to = last if m == 7 else dst.at[m]
            moves.append(remote(src.at[m], to, move_send.at[m, n], move_recv.at[m, n], peer))

    for m in range(7):
        loads[m].wait()
        fill(m, met[m][...].reshape(NODES, E))
        if m < 5:
            push(m)

    loads[7].wait()

    def chunk(c, carry):
        apply_chunk(c, sol, met, kmat, im, dg, rix, vf, ve, vc, ga, gb2, gc2)
        return carry

    lax.fori_loop(0, 4, chunk, 0)

    def send(n, src, dst, peer):
        return remote(src, dst, msg_send.at[n], msg_recv.at[n], peer)

    scatter_faces(keys, tf, fd, fs, vf, lf, of, acc_f)
    face_out = [send(0, fs, gfs, next_sub), send(1, fd, gfd, next_dom)]
    scatter_lines(keys, te, tc, md, ms, ve, vc, le, ol, acc_e)
    line_out = [
        send(2, ms, gs, next_sub),
        send(3, md, gd, next_dom),
        send(4, md.at[pl.ds(LINES - BOTH, BOTH)], gb, next_both),
    ]
    pc[...] = onehot(small_row(arrive, 256), 256)
    pd[...] = onehot(small_row(swapped(arrive), 256), 256)
    for copy in face_out:
        copy.wait()
    owner_faces(tf, gfd, gfs, tf2, sfd, sfs)
    face_back = [send(5, sfs, rfs, prev_sub), send(6, sfd, rfd, prev_dom)]
    for copy in line_out:
        copy.wait()
    owner_lines(te, tc, gd, gs, gb, te2, tc2, sd, ss, sb)
    line_back = [send(7, ss, rs, prev_sub), send(8, sd, rd, prev_dom), send(9, sb, rb, prev_both)]
    for m in range(5, 7):
        push(m)
    for copy in face_back:
        copy.wait()
    gather_faces(keys, tf2, rfd, rfs, tfs, og, gf)
    for copy in line_back:
        copy.wait()
    gather_lines(keys, te2, tc2, rd, rs, rb, ge, gc)
    loads[8].wait()
    place_relax(im, dg, gf, ge, gc, sol, forc, rel)
    fill(7, rel[...].reshape(NODES, E))
    push(7)
    for m in range(7):
        for copy in moves[4 * m : 4 * m + 4]:
            copy.wait()
        land_block(met[m], [a[m] for a in (a0, a1, a2, a3)], pc[...], pd[...], departed, met[m])
    for copy in moves[28:]:
        copy.wait()


def main_call(owner, ids, solution, forcing, metric):
    half = NODES // 2
    vm = pl.BlockSpec(memory_space=pltpu.VMEM)
    hbm = pl.BlockSpec(memory_space=pl.ANY)
    box = pltpu.VMEM((N, N, N, E), f32)
    planes = pltpu.VMEM((4, NODES, 128), f32)
    face, line, both = (pltpu.VMEM((r, 128), f32) for r in (F_ROWS, LINES, BOTH))
    work = pltpu.VMEM((NODES, 128), f32)
    moved = pltpu.VMEM((8, half, 128), f32)
    came = pltpu.VMEM((7, half, 128), f32)
    return pl.pallas_call(
        main_kernel,
        in_specs=[hbm] * 5,
        out_specs=[vm] * 12,
        out_shape=[jax.ShapeDtypeStruct((N, N, N, E), f32)] * 8
        + [jax.ShapeDtypeStruct((half, 128), f32)] * 4,
        scratch_shapes=[
            pltpu.VMEM((1, E), i32),
            pltpu.VMEM((26, E), i32),
            box, box,
            pltpu.VMEM((3, 64, 64), f32), planes, planes,
            pltpu.VMEM((26, E), i32),
            pltpu.VMEM((26, E), f32),
            pltpu.VMEM((F_ROWS, F_KEYS), f32),
            pltpu.VMEM((E_HI, 16, 256), f32),
            pltpu.VMEM((C_HI, 8, 256), f32),
            face, face, line, line,
            face, face, line, line, both,
            pltpu.VMEM((F_ROWS, F_BLOCK), f32),
            pltpu.VMEM((E_BLOCK // 256, 16, 256), f32),
            pltpu.VMEM((C_BLOCK // 256, 8, 256), f32),
            face, face, line, line, both,
            face, face, line, line, both,
            pltpu.VMEM((2 * F_ROWS, 6 * E), bf16),
            pltpu.VMEM((32, 12 * E), bf16),
            pltpu.VMEM((8, 8 * E), f32),
            work, work, work,
            pltpu.VMEM((2 * F_ROWS * F_HI, 6 * E), bf16),
            pltpu.VMEM((256, 6 * E), bf16),
            pltpu.VMEM((2 * F_ROWS * F_HI, 256), f32),
            pltpu.VMEM((2 * E_HI * 16, 12 * E), bf16),
            pltpu.VMEM((256, 12 * E), bf16),
            pltpu.VMEM((2 * E_HI * 16, 256), f32),
            pltpu.VMEM((2 * F_ROWS, F_KEYS), bf16),
            pltpu.VMEM((F_KEYS, E), bf16),
            pltpu.VMEM((6, F_ROWS, E), f32),
            pltpu.VMEM((12, 16, E), f32),
            pltpu.VMEM((8, 8, E), f32),
            moved, moved, moved, moved,
            came, came, came, came,
            pltpu.VMEM((256, E), bf16),
            pltpu.VMEM((256, E), bf16),
            pltpu.VMEM((256, E), bf16),
            pltpu.VMEM((256, E), bf16),
            pltpu.SemaphoreType.DMA((11,)),
            pltpu.SemaphoreType.DMA((10,)),
            pltpu.SemaphoreType.DMA((10,)),
            pltpu.SemaphoreType.DMA((8, 4)),
            pltpu.SemaphoreType.DMA((8, 4)),
        ],
        compiler_params=pltpu.CompilerParams(
            vmem_limit_bytes=47448064, collective_id=0, has_side_effects=True
        ),
        interpret=pltpu.InterpretParams() if INTERPRET else False,
        name="main",
    )(owner, ids, solution, forcing, metric)


def land_kernel(
    devs, owner_ref, m0, m1, m2, m3, m4, m5, m6, rel_in, f0, f1, f2, f3, met_out, rel_out, y, out_sem
):
    met = (m0, m1, m2, m3, m4, m5, m6)
    stores = [pltpu.make_async_copy(met[m], met_out.at[m], out_sem.at[m]) for m in range(7)]
    for copy in stores:
        copy.start()
    departed, _, arrive = move_rows(owner_ref[...], [devs[d] for d in range(5)], prefix_matrix())
    pa = onehot(small_row(arrive, 256), 256)
    pb = onehot(small_row(swapped(arrive), 256), 256)
    land_block(rel_in, [f[...] for f in (f0, f1, f2, f3)], pa, pb, departed, y)
    stores.append(pltpu.make_async_copy(y, rel_out, out_sem.at[7]))
    stores[7].start()
    for copy in stores:
        copy.wait()


def land(devs, owner, shape, blocks):
    vm = pl.BlockSpec(memory_space=pltpu.VMEM)
    hbm = pl.BlockSpec(memory_space=pltpu.HBM)
    return pl.pallas_call(
        land_kernel,
        in_specs=[pl.BlockSpec(memory_space=pltpu.SMEM)] + [vm] * 13,
        out_specs=[hbm] * 2,
        out_shape=[jax.ShapeDtypeStruct(shape, f32), jax.ShapeDtypeStruct(shape[1:], f32)],
        scratch_shapes=[
            pltpu.VMEM((N, N, N, E), f32),
            pltpu.SemaphoreType.DMA((8,)),
        ],
        compiler_params=pltpu.CompilerParams(vmem_limit_bytes=8 << 20),
        interpret=INTERPRET,
        name="land",
    )(devs, owner, *blocks)


def on_device(solution, forcing, metric, entity_ids, new_owner):
    a, b = lax.axis_size("dom"), lax.axis_size("sub")
    d, s = lax.axis_index("dom"), lax.axis_index("sub")
    da, db = (d + 1) % a, (d + a - 1) % a
    sa, sb = (s + 1) % b, (s + b - 1) % b
    devs = jnp.stack([d * b + s, db * b + s, da * b + s, d * b + sb, d * b + sa, da * b + sa]).astype(i32)
    owner = new_owner.reshape(1, E)

    blocks = main_call(owner, entity_ids, solution, forcing, metric)
    moved_metric, smoothed = land(devs, owner, metric.shape, blocks)
    return smoothed, moved_metric


def solution(mesh):
    cols = ("dom", "sub")
    placed = (
        P(None, None, None, cols),
        P(None, None, None, cols),
        P(None, None, None, None, cols),
        P(None, cols),
        P(cols),
    )
    return jax.shard_map(
        on_device,
        mesh=mesh,
        in_specs=placed,
        out_specs=(P(None, None, None, cols), P(None, None, None, None, cols)),
        check_vma=False,
    )
```

```python
import functools

import jax
import jax.numpy as jnp
import numpy as np
from jax import lax
from jax.experimental import pallas as pl
from jax.experimental.pallas import tpu as pltpu
from jax.sharding import PartitionSpec as P

N = 8
E = 512
NODES = N * N * N
EX = 4
EY = 4
EZ = 32
MOVE = 64
RELAX = 0.6
F_BLOCK, E_BLOCK, C_BLOCK = 3 * E, 3 * E, E
F_KEYS, E_KEYS, C_KEYS = 1792, 2560, 1536
F_HI, E_HI, C_HI = F_KEYS // 256, E_KEYS // 256, C_KEYS // 256
PLANE = 48
F_ROWS = 2 * PLANE
LINES = 96
BOTH = 24
INTERPRET = False

f32, bf16, i32 = jnp.float32, jnp.bfloat16, jnp.int32


def derivative_table(order):
    count = order + 1
    points = -np.cos(np.pi * np.arange(count) / order)
    legendre = np.zeros((count, count))
    for sweep in range(80):
        legendre[:, 0] = 1.0
        legendre[:, 1] = points
        for degree in range(2, count):
            legendre[:, degree] = (
                (2 * degree - 1) * points * legendre[:, degree - 1]
                - (degree - 1) * legendre[:, degree - 2]
            ) / degree
        points = points - (points * legendre[:, order] - legendre[:, order - 1]) / (
            count * legendre[:, order]
        )
    legendre[:, 0] = 1.0
    legendre[:, 1] = points
    for degree in range(2, count):
        legendre[:, degree] = (
            (2 * degree - 1) * points * legendre[:, degree - 1]
            - (degree - 1) * legendre[:, degree - 2]
        ) / degree
    values = legendre[:, order]
    identity = np.eye(count)
    spread = points[:, None] - points[None, :] + identity
    table = values[:, None] / values[None, :] / spread
    table = table * (1.0 - identity)
    table[0, 0] = -order * count / 4.0
    table[order, order] = order * count / 4.0
    return table.astype(np.float32)


TABLE = derivative_table(N - 1)
SQUARED = TABLE * TABLE
ALONG = [float(v) for v in np.diagonal(TABLE)]


def row_of(i, j, k):
    return (i * N + j) * N + k


EDGE_ROWS = (
    [(row_of(0, a, b), N * N) for a in (0, 7) for b in (0, 7)]
    + [(row_of(a, 0, b), N) for a in (0, 7) for b in (0, 7)]
    + [(row_of(a, b, 0), 1) for a in (0, 7) for b in (0, 7)]
)
CORNER_ROWS = [row_of(a, b, c) for a in (0, 7) for b in (0, 7) for c in (0, 7)]


def split2(x):
    hi = x.astype(bf16)
    return hi, (x - hi.astype(f32)).astype(bf16)


def stack2(x):
    return jnp.concatenate(split2(x), axis=0)


def sum2(x):
    m = x.shape[0] // 2
    return x[0:m] + x[m:]


def dot_nn(a, b):
    return lax.dot_general(a, b, (((1,), (0,)), ((), ())), preferred_element_type=f32)


def dot_nt(a, b):
    return lax.dot_general(a, b, (((1,), (1,)), ((), ())), preferred_element_type=f32)


def small_row(key, count):
    ok = (key >= 0) & (key < count)
    return jnp.where(ok, key, -1).astype(f32).astype(bf16)


def iota_rows(count, lanes):
    return lax.broadcasted_iota(i32, (count, lanes), 0).astype(f32).astype(bf16)


def onehot(row, count):
    lanes = row.shape[1]
    io = iota_rows(count, 128)
    one, zero = jnp.ones((count, 128), bf16), jnp.zeros((count, 128), bf16)
    cols = [
        jnp.where(io == jnp.broadcast_to(row[:, g : g + 128], (count, 128)), one, zero)
        for g in range(0, lanes, 128)
    ]
    return cols[0] if len(cols) == 1 else jnp.concatenate(cols, axis=1)


def prefix_matrix():
    a = lax.broadcasted_iota(i32, (E, E), 0)
    b = lax.broadcasted_iota(i32, (E, E), 1)
    return jnp.where(a <= b, 1.0, 0.0).astype(bf16)


def ranks(mask, tri):
    m = mask.shape[0]
    flags = jnp.where(mask, 1.0, 0.0)
    within = dot_nn(flags.astype(bf16), tri) - 1.0
    if m > 1:
        before = jnp.zeros((1, 1), f32)
        offs = [before]
        for r in range(m - 1):
            before = before + jnp.sum(flags[r : r + 1], axis=1, keepdims=True)
            offs.append(before)
        within = within + jnp.concatenate(offs, axis=0)
    return within.astype(i32)


def move_rows(owner, devs, tri):
    own = devs[0]
    departed = owner != own
    leave = jnp.full((1, E), -1, i32)
    arrive = jnp.full((1, E), -1, i32)
    flags = [departed] + [departed & (owner == devs[d]) for d in range(1, 5)]
    stacked = jnp.concatenate([jnp.where(f, 1.0, 0.0) for f in flags] + [jnp.zeros((3, E), f32)], axis=0)
    pre = dot_nn(stacked.astype(bf16), tri)
    hole = pre[0:1] - 1.0
    start = jnp.zeros((1, 1), f32)
    for d in range(4):
        chosen = flags[d + 1]
        rank = pre[d + 1 : d + 2] - 1.0
        leave = jnp.where(chosen, d * MOVE + rank.astype(i32), leave)
        count = pre[d + 1 : d + 2, E - 1 : E]
        pos = hole - start
        inside = departed & (pos >= 0.0) & (pos < count)
        arrive = jnp.where(inside, d * MOVE + pos.astype(i32), arrive)
        start = start + count
    return departed, leave, arrive


def swapped(col):
    return jnp.where(col >= 0, col ^ MOVE, -1)


def lane_low(rows):
    return lax.broadcasted_iota(i32, (rows, 128), 1) < MOVE


def pack_block(x, pa, pb):
    half = NODES // 2
    ya = sum2(dot_nt(stack2(x[0:half]), pa))
    yb = sum2(dot_nt(stack2(x[half:]), pb))
    low = lane_low(half)
    out = []
    for g in (0, 128):
        a, b = ya[:, g : g + 128], yb[:, g : g + 128]
        out.append(jnp.where(low, a, b))
        out.append(jnp.where(low, b, a))
    return out


def land_block(x, got, pa, pb, departed, out):
    half = NODES // 2
    low = lane_low(half)
    zl, zh = [], []
    for g in (0, 2):
        zl.append(jnp.where(low, got[g + 1], got[g]))
        zh.append(jnp.where(low, got[g], got[g + 1]))
    keep = jnp.logical_not(departed)
    for at, z, p in ((slice(0, 4), zl, pb), (slice(4, 8), zh, pa)):
        y = sum2(dot_nn(stack2(jnp.concatenate(z, axis=1)), p))
        v = jnp.where(keep, x[at].reshape(half, E), y)
        out[at] = v.reshape(4, N, N, E)


def block_table(table):
    r = lax.broadcasted_iota(i32, (N, 64), 0)
    c = lax.broadcasted_iota(i32, (N, 64), 1)
    tile_of = jnp.zeros((N, 64), f32)
    low = c & 7
    for a in range(N):
        row = jnp.zeros((N, 64), f32)
        for i in range(N):
            row = jnp.where(low == i, float(table[a, i]), row)
        tile_of = jnp.where(r == a, row, tile_of)
    return jnp.concatenate([jnp.where(c >> 3 == b, tile_of, 0.0) for b in range(N)], axis=0)


def halves(table):
    t = table.astype(np.float64)
    return (t[:4, :4] + t[:4, :3:-1]) / 2, (t[:4, :4] - t[:4, :3:-1]) / 2


def combine(xs, table, odd):
    even_w, odd_w = halves(table)
    e = [xs[p] + xs[7 - p] for p in range(4)]
    o = [xs[p] - xs[7 - p] for p in range(4)]
    out = [None] * N
    for a in range(4):
        u = sum(float(even_w[a, p]) * e[p] for p in range(4))
        v = sum(float(odd_w[a, p]) * o[p] for p in range(4))
        out[a] = v + u
        out[7 - a] = v - u if odd else u - v
    return out


def contract_i(src, table, odd, put):
    for j in range(N):
        for a, v in enumerate(combine([src(i, j) for i in range(N)], table, odd)):
            put(a, j, v)


def contract_j(src, table, odd, put):
    for i in range(N):
        for b, v in enumerate(combine([src(i, j) for j in range(N)], table, odd)):
            put(i, b, v)


def key_rows(ids, block, devs, dom_base, both_base, sub_base, tri):
    rel, inside = [], []
    for d in (0, 2, 4, 5):
        r = ids - devs[d] * block
        rel.append(r)
        inside.append((r >= 0) & (r < block))
    key = jnp.where(inside[0], rel[0], -1)
    key = jnp.where(inside[1], dom_base + ranks(inside[1], tri), key)
    key = jnp.where(inside[2], sub_base + ranks(inside[2], tri), key)
    if both_base is not None:
        key = jnp.where(inside[3], both_base + ranks(inside[3], tri), key)
    row = jnp.where(inside[0], rel[0], jnp.where(inside[1], rel[1], jnp.where(inside[2], rel[2], rel[3])))
    return key, row.astype(f32)


def tile(ref, r):
    return ref[pl.ds(r * N, N), :]


def make_keys(ids, devs, key_out, rix, tri):
    k, r = key_rows(ids[0:6], F_BLOCK, devs, 1536, None, 1664, tri)
    key_out[0:6, :] = k
    rix[0:6, :] = r
    k, r = key_rows(ids[6:18], E_BLOCK, devs, 1536, 2016, 2048, tri)
    key_out[6:18, :] = k
    rix[6:18, :] = r
    k, r = key_rows(ids[18:26], C_BLOCK, devs, 512, 960, 1024, tri)
    key_out[18:26, :] = k
    rix[18:26, :] = r


def kdot(m, x):
    return lax.dot_general(
        m, x, (((1,), (0,)), ((), ())),
        precision=lax.Precision.HIGHEST, preferred_element_type=f32,
    )


def gradient_chunk(c, sol_all, kmat, ga_all, gb_all, gc_all):
    lanes = pl.ds(pl.multiple_of(c * 128, 128), 128)
    sol = sol_all.at[:, :, :, lanes]
    ga, gb, gc = ga_all.at[c], gb_all.at[c], gc_all.at[c]
    slab = N * N

    def put_a(i, j, v):
        ga[pl.ds((i * N + j) * N, N), :] = v

    def put_b(i, j, v):
        gb[pl.ds((i * N + j) * N, N), :] = v

    contract_i(lambda i, j: sol[i, j], TABLE, True, put_a)
    contract_j(lambda i, j: sol[i, j], TABLE, True, put_b)
    for h in range(N):
        gc[h * slab : (h + 1) * slab, :] = kdot(kmat[0], sol[h].reshape(slab, 128))


def apply_chunk(c, sol_all, met_all, kmat, im_all, dg_all, rix, vf, ve, vc, ga_all, gb_all, gc_all):
    lanes = pl.ds(pl.multiple_of(c * 128, 128), 128)
    sol = sol_all.at[:, :, :, lanes]
    met = [m.at[:, :, :, lanes] for m in met_all]
    im, dg = im_all.at[c], dg_all.at[c]
    ga, gb, gc = ga_all.at[c], gb_all.at[c], gc_all.at[c]
    bwd = kmat.at[1]
    slab = N * N

    for i in range(N):
        for j in range(N):
            r = i * N + j
            a, b, t = tile(ga, r), tile(gb, r), tile(gc, r)
            m3, m4, m5 = met[3][i, j], met[4][i, j], met[5][i, j]
            ga[pl.ds(r * N, N), :] = met[0][i, j] * a + m3 * b + m4 * t
            gb[pl.ds(r * N, N), :] = m3 * a + met[1][i, j] * b + m5 * t
            gc[pl.ds(r * N, N), :] = m4 * a + m5 * b + met[2][i, j] * t

    for h in range(N):
        im[h * slab : (h + 1) * slab, :] = kdot(bwd[...], gc[h * slab : (h + 1) * slab, :])

    def add_im(i, j, v):
        im[pl.ds((i * N + j) * N, N), :] += v

    contract_i(lambda i, j: tile(ga, i * N + j), TABLE.T, True, add_im)

    def add_im_last(i, j, v):
        im[pl.ds((i * N + j) * N, N), :] += v + met[6][i, j] * sol[i, j]

    contract_j(lambda i, j: tile(gb, i * N + j), TABLE.T, True, add_im_last)

    sq = kmat.at[2]
    for h in range(N):
        dg[h * slab : (h + 1) * slab, :] = kdot(sq[...], met[2][h].reshape(slab, 128))

    def add_dg(i, j, v):
        dg[pl.ds((i * N + j) * N, N), :] += v

    contract_i(lambda i, j: met[0][i, j], SQUARED.T, False, add_dg)
    kk = lax.broadcasted_iota(i32, (N, 128), 0)
    dk = jnp.where(kk == 0, ALONG[0], jnp.where(kk == N - 1, ALONG[N - 1], 0.0))

    def add_dg_last(i, j, v):
        v = v + met[6][i, j]
        if ALONG[i] * ALONG[j] != 0.0:
            v = v + (2.0 * ALONG[i] * ALONG[j]) * met[3][i, j]
        if ALONG[i] != 0.0:
            v = v + (2.0 * ALONG[i]) * dk * met[4][i, j]
        if ALONG[j] != 0.0:
            v = v + (2.0 * ALONG[j]) * dk * met[5][i, j]
        dg[pl.ds((i * N + j) * N, N), :] += v

    contract_j(lambda i, j: met[1][i, j], SQUARED.T, False, add_dg_last)

    def face(ref, f):
        if f < 2:
            base = 8 if f == 0 else 456
            return ref[base : base + PLANE, :]
        if f < 4:
            j = 0 if f == 2 else 7
            return jnp.concatenate([ref[pl.ds((i * N + j) * N, N), :] for i in range(1, 7)], axis=0)
        return ref[pl.ds(64 if f == 4 else 71, PLANE, stride=N), :]

    top = lax.broadcasted_iota(i32, (N, 128), 0) == 0
    for f in range(6):
        at = pl.ds(pl.multiple_of(f * E + c * 128, 128), 128)
        a, b = face(im, f), face(dg, f)
        mark = jnp.broadcast_to(rix[f : f + 1, lanes], (N, 128))
        a = jnp.concatenate([jnp.where(top, mark, a[0:N]), a[N:]], axis=0)
        for s, (p, q) in enumerate(zip(split2(a), split2(b))):
            vf[s * F_ROWS : s * F_ROWS + PLANE, at] = p
            vf[s * F_ROWS + PLANE : (s + 1) * F_ROWS, at] = q
    for e in range(12):
        at = pl.ds(pl.multiple_of(e * E + c * 128, 128), 128)
        start, stride = EDGE_ROWS[e]
        rows = pl.ds(start, N) if stride == 1 else pl.ds(start, N, stride=stride)
        a, b = im[rows, :], dg[rows, :]
        mark = jnp.broadcast_to(rix[6 + e : 7 + e, lanes], (N, 128))
        x = jnp.concatenate([jnp.where(top, mark, a), b], axis=0)
        for s, p in enumerate(split2(x)):
            ve[s * 16 : s * 16 + 16, at] = p
    for q in range(8):
        at = pl.ds(pl.multiple_of(q * E + c * 128, 128), 128)
        r = CORNER_ROWS[q]
        vc[0:1, at] = im[r : r + 1, :]
        vc[1:2, at] = dg[r : r + 1, :]
        vc[2:3, at] = rix[18 + q : 19 + q, lanes]
        vc[3:8, at] = jnp.zeros((5, 128), f32)


def scatter_faces(key_out, tf, fd, fs, vf, lf, of, acc_f):
    rows = 2 * F_ROWS
    zero = jnp.zeros((rows, 128), bf16)
    for f in range(6):
        key = key_out[f : f + 1, :]
        hi = small_row(key >> 8, F_HI)
        of[:, f * E : (f + 1) * E] = onehot(small_row(key & 255, 256), 256)
        for g in range(4):
            at = slice(f * E + g * 128, f * E + (g + 1) * 128)
            hb = jnp.broadcast_to(hi[:, g * 128 : (g + 1) * 128], (rows, 128))
            part = vf[:, at]
            for h in range(F_HI):
                lf[h * rows : (h + 1) * rows, at] = jnp.where(hb == jnp.full((rows, 128), float(h), bf16), part, zero)
    acc_f[...] = dot_nt(lf[...], of[...])
    for h in range(F_HI):
        tf[:, h * 256 : (h + 1) * 256] = sum2(acc_f[h * rows : (h + 1) * rows, :])
    fd[...] = tf[:, 1536:1664]
    fs[...] = tf[:, 1664:1792]


def scatter_lines(key_out, te, tc, md, ms, ve, vc, le, ol, acc_e):
    for e in range(12):
        at = slice(e * E, (e + 1) * E)
        key = key_out[6 + e : 7 + e, :]
        hi = small_row(key >> 8, E_HI)
        ol[:, at] = onehot(small_row(key & 255, 256), 256)
        for g in range(4):
            ag = slice(e * E + g * 128, e * E + (g + 1) * 128)
            hb = jnp.broadcast_to(hi[:, g * 128 : (g + 1) * 128], (16, 128))
            zero = jnp.zeros((16, 128), bf16)
            parts = [ve[s * 16 : s * 16 + 16, ag] for s in range(2)]
            for h in range(E_HI):
                m = hb == jnp.full((16, 128), float(h), bf16)
                for s in range(2):
                    le[(s * E_HI + h) * 16 : (s * E_HI + h + 1) * 16, ag] = jnp.where(m, parts[s], zero)
    acc_e[...] = dot_nt(le[...], ol[...])
    for h in range(E_HI):
        te[h] = sum(acc_e[(s * E_HI + h) * 16 : (s * E_HI + h + 1) * 16, :] for s in range(2))

    full = E * 8
    for q in range(8):
        at = slice(q * E, (q + 1) * E)
        ol[:, at] = onehot(small_row(key_out[18 + q : 19 + q, :] & 255, 256), 256)
    hi = jnp.concatenate([key_out[18 + q : 19 + q, :] >> 8 for q in range(8)], axis=1)
    x = vc[...]
    big = jnp.concatenate(
        [jnp.where(jnp.broadcast_to(hi, (8, full)) == h, x, 0.0) for h in range(C_HI)], axis=0
    )
    acc = sum2(dot_nt(stack2(big), ol[:, 0:full]))
    for h in range(C_HI):
        tc[h] = acc[h * 8 : (h + 1) * 8]

    for g in range(4):
        er, cr = msg_rows(g)
        half_lanes = slice((g % 2) * 128, (g % 2) * 128 + 128)
        md[er : er + 16, :] = te[6 + g // 2, :, half_lanes]
        ms[er : er + 16, :] = te[8 + g // 2, :, half_lanes]
        md[cr : cr + 8, :] = tc[2 + g // 2, :, half_lanes]
        ms[cr : cr + 8, :] = tc[4 + g // 2, :, half_lanes]


def msg_rows(g):
    if g < 3:
        return 16 * g, 48 + 8 * g
    return 72, 88


def owner_faces(tf, gd, gs, tf2, rd, rs):
    rows, his = 2 * F_ROWS, F_BLOCK // 256
    vals = jnp.concatenate([gd[...], gs[...]], axis=1)
    key = vals[0:1, :].astype(i32)
    hi = key >> 8
    o = onehot(small_row(key & 255, 256), 256)
    vs = stack2(vals)
    hb = jnp.broadcast_to(small_row(hi, his), (rows, 256))
    zero = jnp.zeros((rows, 256), bf16)
    big = [jnp.where(hb == jnp.full((rows, 256), float(h), bf16), vs, zero) for h in range(his)]
    acc = dot_nt(jnp.concatenate(big, axis=0), o)
    parts = []
    for h in range(his):
        total = tf[:, h * 256 : (h + 1) * 256] + sum2(acc[h * rows : (h + 1) * rows])
        tf2[:, h * 256 : (h + 1) * 256] = total
        parts.append(stack2(total))
    y = dot_nn(jnp.concatenate(parts, axis=0), o)
    back = jnp.zeros((F_ROWS, 256), f32)
    for h in range(his):
        mine = jnp.broadcast_to(hi, (F_ROWS, 256)) == h
        back = jnp.where(mine, sum2(y[h * rows : (h + 1) * rows]), back)
    rd[...] = back[:, 0:128]
    rs[...] = back[:, 128:256]


def owner_lines(te, tc, gd, gs, gboth, te2, tc2, rd, rs, rb):
    lane = lax.broadcasted_iota(i32, (1, 128), 1)

    def lines(rows, id_row, total_ref, total_out, his, cut, at):
        vals, keys = [], []
        for src in (gd, gs):
            for g in range(4):
                r = msg_rows(g)[at]
                v = src[r : r + rows, :]
                k = v[id_row : id_row + 1].astype(i32)
                if src is gd and g == 3:
                    k = jnp.where(lane >= cut, -1, k)
                vals.append(v)
                keys.append(k)
        r = msg_rows(3)[at] - (LINES - BOTH)
        v = gboth[r : r + rows, :]
        keys.append(jnp.where(lane < cut, -1, v[id_row : id_row + 1].astype(i32)))
        vals.append(v)
        x = jnp.concatenate(vals, axis=1)
        key = jnp.concatenate(keys, axis=1)
        hi = key >> 8
        o = onehot(small_row(key & 255, 256), 256)
        big = jnp.concatenate([jnp.where(jnp.broadcast_to(hi, x.shape) == h, x, 0.0) for h in range(his)], axis=0)
        acc = sum2(dot_nt(stack2(big), o))
        totals = jnp.concatenate([total_ref[h] for h in range(his)], axis=0) + acc
        for h in range(his):
            total_out[h] = totals[h * rows : (h + 1) * rows]
        y = sum2(dot_nn(stack2(totals), o))
        back = jnp.zeros_like(x)
        for h in range(his):
            back = jnp.where(jnp.broadcast_to(hi, x.shape) == h, y[h * rows : (h + 1) * rows], back)
        for n, dst in enumerate((rd, rs)):
            for g in range(4):
                p = msg_rows(g)[at]
                dst[p : p + rows, :] = back[:, (n * 4 + g) * 128 : (n * 4 + g + 1) * 128]
        rb[r : r + rows, :] = back[:, 1024:1152]

    lines(16, 0, te, te2, E_BLOCK // 256, 96, 0)
    lines(8, 2, tc, tc2, C_BLOCK // 256, 64, 1)


def gather_faces(keys, tf, rd, rs, tfs, of, gf):
    for ref, at in ((tf, slice(0, 1536)), (rd, slice(1536, 1664)), (rs, slice(1664, 1792))):
        for s, p in enumerate(split2(ref[...])):
            tfs[s * F_ROWS : (s + 1) * F_ROWS, at] = p

    def face_gather(f, carry):
        key = keys[pl.ds(f, 1), :]
        for n in range(F_KEYS // 256):
            of[n * 256 : (n + 1) * 256, :] = onehot(small_row(key - n * 256, 256), 256)
        gf[f] = sum2(dot_nn(tfs[...], of[...]))
        return carry

    lax.fori_loop(0, 6, face_gather, 0)


def gather_lines(keys, te, tc, rd, rs, rb, ge, gc):
    lane = lax.broadcasted_iota(i32, (1, 128), 1)

    def table(own, his, rows, at, cut):
        blocks = [own[h] for h in range(his)]
        for src in (rd, rs):
            for g in (0, 2):
                pair = []
                for q in (g, g + 1):
                    r = msg_rows(q)[at]
                    v = src[r : r + rows, :]
                    if src is rd and q == 3:
                        b = r - (LINES - BOTH)
                        v = jnp.where(jnp.broadcast_to(lane, (rows, 128)) >= cut, rb[b : b + rows, :], v)
                    pair.append(v)
                blocks.append(jnp.concatenate(pair, axis=1))
        return stack2(jnp.concatenate(blocks, axis=0))

    def line_gather(tab, first, count, his, rows, dst):
        for q in range(count):
            key = keys[first + q : first + q + 1, :]
            hi = key >> 8
            y = sum2(dot_nn(tab, onehot(small_row(key & 255, 256), 256)))
            back = jnp.zeros((rows, E), f32)
            for h in range(his):
                back = jnp.where(jnp.broadcast_to(hi, (rows, E)) == h, y[h * rows : (h + 1) * rows], back)
            dst[q] = back

    line_gather(table(te, 6, 16, 0, 96), 6, 12, E_HI, 16, ge)
    line_gather(table(tc, 2, 8, 1, 64), 18, 8, C_HI, 8, gc)

def place_relax(im, dg, gf, ge, gc, sol, forc, rel):
    for c in range(4):
        at = slice(c * 128, (c + 1) * 128)
        for ref, base in ((im.at[c], 0), (dg.at[c], 1)):
            for f in range(6):
                v = gf[f, base * PLANE : (base + 1) * PLANE, at]
                if f < 2:
                    start = 8 if f == 0 else 456
                    ref[start : start + PLANE, :] = v
                elif f < 4:
                    j = 0 if f == 2 else 7
                    for i in range(1, 7):
                        ref[pl.ds((i * N + j) * N, N), :] = v[(i - 1) * N : i * N]
                else:
                    ref[pl.ds(64 if f == 4 else 71, PLANE, stride=N), :] = v
            for e in range(12):
                start, stride = EDGE_ROWS[e]
                rows = pl.ds(start, N) if stride == 1 else pl.ds(start, N, stride=stride)
                ref[rows, :] = ge[e, base * 8 : base * 8 + 8, at]
            for q in range(8):
                r = CORNER_ROWS[q]
                ref[r : r + 1, :] = gc[q, base : base + 1, at]
        s = sol[:, :, :, at].reshape(NODES, 128)
        v = s + RELAX * (forc[:, :, :, at].reshape(NODES, 128) - im[c]) / dg[c]
        rel[:, :, :, at] = v.reshape(N, N, N, 128)

MESH = pl.DeviceIdType.MESH


def main_kernel(
    owner_in, ids_in, sol_in, forc_in, met_in,
    m0, m1, m2, m3, m4, m5, m6, rel, f0, f1, f2, f3,
    owner, ids, sol, forc, kmat, im, dg, keys, rix, tf, te, tc, fd, fs, md, ms,
    gfd, gfs, gd, gs, gb, tf2, te2, tc2, sfd, sfs, sd, ss, sb, rfd, rfs, rd, rs, rb,
    vf, ve, vc, ga, gb2, gc2, lf, of, acc_f, le, ol, acc_e,
    tfs, og, gf, ge, gc, p0, p1, p2, p3, a0, a1, a2, a3, pa, pb, pc, pd,
    load_sem, msg_send, msg_recv, move_send, move_recv,
):
    na, nb = lax.axis_size("dom"), lax.axis_size("sub")
    d, s = lax.axis_index("dom"), lax.axis_index("sub")
    dn, dp = lax.rem(d + 1, na), lax.rem(d + na - 1, na)
    sn, sp = lax.rem(s + 1, nb), lax.rem(s + nb - 1, nb)
    prev_dom, next_dom, prev_sub, next_sub = (dp, s), (dn, s), (d, sp), (d, sn)
    prev_both, next_both = (dp, sp), (dn, sn)
    met = (m0, m1, m2, m3, m4, m5, m6)
    loads = [pltpu.make_async_copy(met_in.at[m], met[m], load_sem.at[m]) for m in range(7)]
    loads.append(pltpu.make_async_copy(sol_in, sol, load_sem.at[7]))
    loads.append(pltpu.make_async_copy(forc_in, forc, load_sem.at[8]))
    early = [pltpu.make_async_copy(owner_in, owner, load_sem.at[9]), pltpu.make_async_copy(ids_in, ids, load_sem.at[10])]
    for copy in early + loads[7:8] + loads[:7] + loads[8:]:
        copy.start()

    barrier = pltpu.get_barrier_semaphore()
    for peer in (prev_dom, next_dom, prev_sub, next_sub, prev_both, next_both):
        pl.semaphore_signal(barrier, inc=1, device_id=peer, device_id_type=MESH)

    devs = [x * nb + y for x, y in ((d, s), prev_dom, next_dom, prev_sub, next_sub, next_both)]
    tri = prefix_matrix()
    for n, table in enumerate((TABLE, TABLE.T, SQUARED.T)):
        kmat[n] = block_table(table)
    for copy in early:
        copy.wait()
    departed, leave, arrive = move_rows(owner[...], devs, tri)
    pa[...] = onehot(small_row(leave, 256), 256)
    pb[...] = onehot(small_row(swapped(leave), 256), 256)
    make_keys(ids, devs, keys, rix, tri)
    pl.semaphore_wait(barrier, 6)

    def remote(src, dst, send_sem, recv_sem, peer):
        copy = pltpu.make_async_remote_copy(
            src_ref=src, dst_ref=dst, send_sem=send_sem, recv_sem=recv_sem,
            device_id=peer, device_id_type=MESH,
        )
        copy.start()
        return copy

    half = NODES // 2
    moves = [[] for _ in range(8)]

    def fill(m, x):
        for ref, val in zip((p0, p1, p2, p3), pack_block(x, pa[...], pb[...])):
            ref[m] = val

    def push_sub(m):
        for n, (src, dst, last, peer) in enumerate(((p2, a3, f3, prev_sub), (p3, a2, f2, next_sub))):
            to = last if m == 7 else dst.at[m]
            moves[m].append(remote(src.at[m], to, move_send.at[m, n], move_recv.at[m, n], peer))

    def push_dom(m):
        for n, (src, dst, last, peer) in enumerate(((p0, a1, f1, prev_dom), (p1, a0, f0, next_dom))):
            to = last if m == 7 else dst.at[m]
            moves[m].append(remote(src.at[m], to, move_send.at[m, n + 2], move_recv.at[m, n + 2], peer))

    loads[7].wait()

    def gradients(c, carry):
        gradient_chunk(c, sol, kmat, ga, gb2, gc2)
        return carry

    lax.fori_loop(0, 4, gradients, 0)
    for m in range(7):
        loads[m].wait()
        fill(m, met[m][...].reshape(NODES, E))
        if m < 4:
            push_sub(m)
        push_dom(m)

    def chunk(c, carry):
        apply_chunk(c, sol, met, kmat, im, dg, rix, vf, ve, vc, ga, gb2, gc2)
        return carry

    lax.fori_loop(0, 4, chunk, 0)

    def send(n, src, dst, peer):
        return remote(src, dst, msg_send.at[n], msg_recv.at[n], peer)

    scatter_faces(keys, tf, fd, fs, vf, lf, of, acc_f)
    face_out = [send(0, fs, gfs, next_sub), send(1, fd, gfd, next_dom)]
    scatter_lines(keys, te, tc, md, ms, ve, vc, le, ol, acc_e)
    line_out = [
        send(2, ms, gs, next_sub),
        send(3, md, gd, next_dom),
        send(4, md.at[pl.ds(LINES - BOTH, BOTH)], gb, next_both),
    ]
    for m in range(4, 5):
        push_sub(m)
    pc[...] = onehot(small_row(arrive, 256), 256)
    pd[...] = onehot(small_row(swapped(arrive), 256), 256)
    for copy in face_out:
        copy.wait()
    owner_faces(tf, gfd, gfs, tf2, sfd, sfs)
    face_back = [send(5, sfs, rfs, prev_sub), send(6, sfd, rfd, prev_dom)]
    for copy in line_out:
        copy.wait()
    owner_lines(te, tc, gd, gs, gb, te2, tc2, sd, ss, sb)
    line_back = [send(7, ss, rs, prev_sub), send(8, sd, rd, prev_dom), send(9, sb, rb, prev_both)]
    for m in range(5, 7):
        push_sub(m)
    for copy in face_back:
        copy.wait()
    gather_faces(keys, tf2, rfd, rfs, tfs, og, gf)
    for copy in line_back:
        copy.wait()
    gather_lines(keys, te2, tc2, rd, rs, rb, ge, gc)
    loads[8].wait()
    place_relax(im, dg, gf, ge, gc, sol, forc, rel)
    fill(7, rel[...].reshape(NODES, E))
    push_sub(7)
    push_dom(7)
    for m in range(7):
        for copy in moves[m]:
            copy.wait()
        land_block(met[m], [a[m] for a in (a0, a1, a2, a3)], pc[...], pd[...], departed, met[m])
    for copy in moves[7]:
        copy.wait()


def main_call(owner, ids, solution, forcing, metric):
    half = NODES // 2
    vm = pl.BlockSpec(memory_space=pltpu.VMEM)
    hbm = pl.BlockSpec(memory_space=pl.ANY)
    box = pltpu.VMEM((N, N, N, E), f32)
    planes = pltpu.VMEM((4, NODES, 128), f32)
    face, line, both = (pltpu.VMEM((r, 128), f32) for r in (F_ROWS, LINES, BOTH))
    moved = pltpu.VMEM((8, half, 128), f32)
    came = pltpu.VMEM((7, half, 128), f32)
    return pl.pallas_call(
        main_kernel,
        in_specs=[hbm] * 5,
        out_specs=[vm] * 12,
        out_shape=[jax.ShapeDtypeStruct((N, N, N, E), f32)] * 8
        + [jax.ShapeDtypeStruct((half, 128), f32)] * 4,
        scratch_shapes=[
            pltpu.VMEM((1, E), i32),
            pltpu.VMEM((26, E), i32),
            box, box,
            pltpu.VMEM((3, 64, 64), f32), planes, planes,
            pltpu.VMEM((26, E), i32),
            pltpu.VMEM((26, E), f32),
            pltpu.VMEM((F_ROWS, F_KEYS), f32),
            pltpu.VMEM((E_HI, 16, 256), f32),
            pltpu.VMEM((C_HI, 8, 256), f32),
            face, face, line, line,
            face, face, line, line, both,
            pltpu.VMEM((F_ROWS, F_BLOCK), f32),
            pltpu.VMEM((E_BLOCK // 256, 16, 256), f32),
            pltpu.VMEM((C_BLOCK // 256, 8, 256), f32),
            face, face, line, line, both,
            face, face, line, line, both,
            pltpu.VMEM((2 * F_ROWS, 6 * E), bf16),
            pltpu.VMEM((32, 12 * E), bf16),
            pltpu.VMEM((8, 8 * E), f32),
            planes, planes, planes,
            pltpu.VMEM((2 * F_ROWS * F_HI, 6 * E), bf16),
            pltpu.VMEM((256, 6 * E), bf16),
            pltpu.VMEM((2 * F_ROWS * F_HI, 256), f32),
            pltpu.VMEM((2 * E_HI * 16, 12 * E), bf16),
            pltpu.VMEM((256, 12 * E), bf16),
            pltpu.VMEM((2 * E_HI * 16, 256), f32),
            pltpu.VMEM((2 * F_ROWS, F_KEYS), bf16),
            pltpu.VMEM((F_KEYS, E), bf16),
            pltpu.VMEM((6, F_ROWS, E), f32),
            pltpu.VMEM((12, 16, E), f32),
            pltpu.VMEM((8, 8, E), f32),
            moved, moved, moved, moved,
            came, came, came, came,
            pltpu.VMEM((256, E), bf16),
            pltpu.VMEM((256, E), bf16),
            pltpu.VMEM((256, E), bf16),
            pltpu.VMEM((256, E), bf16),
            pltpu.SemaphoreType.DMA((11,)),
            pltpu.SemaphoreType.DMA((10,)),
            pltpu.SemaphoreType.DMA((10,)),
            pltpu.SemaphoreType.DMA((8, 4)),
            pltpu.SemaphoreType.DMA((8, 4)),
        ],
        compiler_params=pltpu.CompilerParams(
            vmem_limit_bytes=47448064, collective_id=0, has_side_effects=True
        ),
        interpret=pltpu.InterpretParams() if INTERPRET else False,
        name="main",
    )(owner, ids, solution, forcing, metric)


def land_kernel(
    devs, owner_ref, m0, m1, m2, m3, m4, m5, m6, rel_in, f0, f1, f2, f3, met_out, rel_out, y, out_sem
):
    met = (m0, m1, m2, m3, m4, m5, m6)
    stores = [pltpu.make_async_copy(met[m], met_out.at[m], out_sem.at[m]) for m in range(7)]
    for copy in stores:
        copy.start()
    departed, _, arrive = move_rows(owner_ref[...], [devs[d] for d in range(5)], prefix_matrix())
    pa = onehot(small_row(arrive, 256), 256)
    pb = onehot(small_row(swapped(arrive), 256), 256)
    land_block(rel_in, [f[...] for f in (f0, f1, f2, f3)], pa, pb, departed, y)
    stores.append(pltpu.make_async_copy(y, rel_out, out_sem.at[7]))
    stores[7].start()
    for copy in stores:
        copy.wait()


def land(devs, owner, shape, blocks):
    vm = pl.BlockSpec(memory_space=pltpu.VMEM)
    hbm = pl.BlockSpec(memory_space=pltpu.HBM)
    return pl.pallas_call(
        land_kernel,
        in_specs=[pl.BlockSpec(memory_space=pltpu.SMEM)] + [vm] * 13,
        out_specs=[hbm] * 2,
        out_shape=[jax.ShapeDtypeStruct(shape, f32), jax.ShapeDtypeStruct(shape[1:], f32)],
        scratch_shapes=[
            pltpu.VMEM((N, N, N, E), f32),
            pltpu.SemaphoreType.DMA((8,)),
        ],
        compiler_params=pltpu.CompilerParams(vmem_limit_bytes=8 << 20),
        interpret=INTERPRET,
        name="land",
    )(devs, owner, *blocks)


def on_device(solution, forcing, metric, entity_ids, new_owner):
    a, b = lax.axis_size("dom"), lax.axis_size("sub")
    d, s = lax.axis_index("dom"), lax.axis_index("sub")
    da, db = (d + 1) % a, (d + a - 1) % a
    sa, sb = (s + 1) % b, (s + b - 1) % b
    devs = jnp.stack([d * b + s, db * b + s, da * b + s, d * b + sb, d * b + sa, da * b + sa]).astype(i32)
    owner = new_owner.reshape(1, E)

    blocks = main_call(owner, entity_ids, solution, forcing, metric)
    moved_metric, smoothed = land(devs, owner, metric.shape, blocks)
    return smoothed, moved_metric


def solution(mesh):
    cols = ("dom", "sub")
    placed = (
        P(None, None, None, cols),
        P(None, None, None, cols),
        P(None, None, None, None, cols),
        P(None, cols),
        P(cols),
    )
    return jax.shard_map(
        on_device,
        mesh=mesh,
        in_specs=placed,
        out_specs=(P(None, None, None, cols), P(None, None, None, None, cols)),
        check_vma=False,
    )
```
